32 devices in a mesh: section: 2 (over y), dp: 4 (over z), tensor: 4 (over x, core).
Axes of the slice: x: 2, y: 2, z: 4, core: 2. Of those that a mesh axis runs over, the one named last changes fastest.
Arguments:
- frames: bfloat16 [2, 2, 4, 1024, 768], P('section', None, 'dp', 'tensor'), may hold values from -6 to 6
- lengths: int32 [2, 2, 4], P(None, None, 'dp'), may hold values from 128 to 1024, as said below
- bucket_of: int32 [2, 2047], P('section'), may hold values from 0 to 319
- rel_table: float32 [2, 320, 12], P('section', None, 'tensor'), may hold values from -4 to 4
- norms: float32 [2, 3, 2, 768], P('section')
- attn_in: bfloat16 [2, 3, 768, 768], P('section', None, None, 'tensor'), may hold values from -0.21875 to 0.21875
- attn_out: bfloat16 [2, 768, 768], P('section', 'tensor'), may hold values from -3.5 to 3.5
- cross_pair: bfloat16 [2, 2, 768, 768], P('section', None, None, 'tensor')
- ffn_in: bfloat16 [2, 768, 3072], P('section', None, 'tensor'), may hold values from -0.21875 to 0.21875
- ffn_out: bfloat16 [2, 3072, 768], P('section', 'tensor'), may hold values from -0.109375 to 0.109375
- cotangent: bfloat16 [2, 2, 4, 1024, 768], P('section', None, 'dp', 'tensor'), may hold values from -6 to 6
Outputs:
- section_out: bfloat16 [2, 2, 4, 1024, 768], P('section', None, 'dp', 'tensor')
- frames_grad: float32 [2, 2, 4, 1024, 768], P('section', None, 'dp', 'tensor')
- rel_table_grad: float32 [2, 320, 12], P('section', None, 'tensor')
- norms_grad: float32 [2, 3, 2, 768], P('section')
- attn_in_grad: float32 [2, 3, 768, 768], P('section', None, None, 'tensor')
- attn_out_grad: float32 [2, 768, 768], P('section', 'tensor')
- cross_pair_grad: float32 [2, 2, 768, 768], P('section', None, None, 'tensor')
- ffn_in_grad: float32 [2, 768, 3072], P('section', None, 'tensor')
- ffn_out_grad: float32 [2, 3072, 768], P('section', 'tensor')
- stats: float32 [2], P('section')
The draws below stay inside these ranges and needn't reach their ends.
Inputs may be any that keep to these rules, and one draw needn't show every extreme that they name: `lengths`: in each section and micro-batch, one sequence has all 1024 frames valid.
All inputs are finite; a program needn't handle non-finite values.
Results may differ from the reference program's by a relative error of at most 0.015.
Values may be sent and summed in bfloat16 or wider, within the bound.
No kernel may reach another device: no remote copies, remote signals or barrier semaphores. Data moves between devices by JAX's collectives and lax.ppermute only.
A program may use at most 896 MiB of HBM per device.

```python
import jax
import jax.numpy as jnp
from jax import lax

D = 768
HEADS = 12
HEAD_DIM = 64
FF = 3072
BUCKETS = 320
L = 1024
MB = 2
SEQS = 4


def draw_lengths(key, part):
    minimal_length = max(1, L // 8)
    values = jax.random.randint(jax.random.fold_in(key, 11), (2, MB, SEQS), minimal_length, L + 1)
    chosen = jax.random.randint(jax.random.fold_in(key, 12), (2, MB, 1), 0, SEQS)
    places = lax.broadcasted_iota(jnp.int32, (2, MB, SEQS), 2)
    return jnp.where(places == chosen, L, values).astype(jnp.int32)


def draw_norms(key, part):
    gain_values = 1.0 + 0.4 * jax.random.uniform(jax.random.fold_in(key, 21), (2, 3, 1, D), jnp.float32, -1.0, 1.0)
    shifts = 0.3 * jax.random.normal(jax.random.fold_in(key, 22), (2, 3, 1, D), jnp.float32)
    return jnp.concatenate([gain_values, shifts], axis=2)


def draw_cross_pair(key, part):
    normal_draw = jnp.clip(jax.random.normal(jax.random.fold_in(key, 31), (2, 2, D, D), jnp.float32), -6.0, 6.0)
    inner_scale = D ** (-0.5)
    query_scale = 2.0 * D ** (-0.5)
    outer_scale = max(1, D // 128) ** (-0.5)
    factor = jnp.array([[inner_scale, inner_scale], [query_scale, outer_scale]], jnp.float32).reshape(2, 2, 1, 1)
    return (normal_draw * factor).astype(jnp.bfloat16)


def touch_ends(drawn, rng, smallest, top_value):
    spot = [jax.random.randint(jax.random.fold_in(rng, axis), (), 0, length) for axis, length in enumerate(drawn.shape)]
    main_axis = drawn.shape.index(max(drawn.shape))
    beside = spot[:main_axis] + [(spot[main_axis] + 1) % drawn.shape[main_axis]] + spot[main_axis + 1:]
    return drawn.at[tuple(spot)].set(smallest).at[tuple(beside)].set(top_value)


def block_levels(rng, dims, shards, low, largest):
    gain, own = 1.0, jax.random.fold_in(rng, 6)
    for position, parts in shards:
        heights = jnp.exp(jax.random.uniform(jax.random.fold_in(own, position), (parts,), jnp.float32, low / len(shards), largest / len(shards)))
        gain = gain * jnp.repeat(heights, dims[position] // parts).reshape([-1 if axis == position else 1 for axis in range(len(dims))])
    return gain


def noise(own_key, dims, width, bound, shards=(), dtype=jnp.bfloat16):
    values = width * jax.random.normal(own_key, dims, jnp.float32)
    if shards:
        values = values * block_levels(own_key, dims, shards, -0.22, 0.18)
    return jnp.clip(values, -bound, bound).astype(dtype)


def setup_inputs(seed: int = 0) -> dict:
    streams_of = jax.random.split(jax.random.key(seed), 12)
    frames = noise(streams_of[0], (2, MB, SEQS, L, D), 1.0, 6.0, ((0, 2), (2, 4), (3, 4)))
    lengths = draw_lengths(jax.random.fold_in(streams_of[11], 71), 0)
    bucket_of = touch_ends(jax.random.randint(streams_of[2], (2, 2 * L - 1), 0, BUCKETS), jax.random.fold_in(streams_of[2], 1), 0, BUCKETS - 1).astype(jnp.int32)
    rel_table = noise(streams_of[3], (2, BUCKETS, HEADS), 1.0, 4.0, ((0, 2), (2, 4)), jnp.float32)
    norms = draw_norms(jax.random.fold_in(streams_of[11], 71), 0)
    attn_in = noise(streams_of[5], (2, 3, D, D), D ** -0.5, 0.21875, ((0, 2), (3, 4)))
    attn_out = noise(streams_of[6], (2, D, D), (max(1, D // 256)) ** -0.5, 3.5, ((0, 2), (1, 4)))
    cross_pair = draw_cross_pair(jax.random.fold_in(streams_of[11], 71), 0)
    ffn_in = noise(streams_of[8], (2, D, FF), D ** -0.5, 0.21875, ((0, 2), (2, 4)))
    ffn_out = noise(streams_of[9], (2, FF, D), FF ** -0.5, 0.109375, ((0, 2), (1, 4)))
    cotangent = noise(streams_of[10], (2, MB, SEQS, L, D), 1.0, 6.0, ((0, 2), (2, 4), (3, 4)))
    return {"frames": frames, "lengths": lengths, "bucket_of": bucket_of, "rel_table": rel_table, "norms": norms, "attn_in": attn_in, "attn_out": attn_out, "cross_pair": cross_pair, "ffn_in": ffn_in, "ffn_out": ffn_out, "cotangent": cotangent}


@jax.custom_vjp
def low(v):
    return lax.optimization_barrier(v.astype(jnp.bfloat16)).astype(jnp.float32)

@jax.custom_vjp
def low_back(v):
    return v

def low_keep(v):
    return (low(v), None)

def low_pass(kept, grad):
    return (grad,)

def back_keep(v):
    return (v, None)

def back_low(kept, grad):
    return (low(grad),)
low.defvjp(low_keep, low_pass)
low_back.defvjp(back_keep, back_low)
highest = lax.Precision.HIGHEST
epsilon = 1e-05
masked_score = -1000000000.0

def product(left, right):
    return jnp.dot(left, right, precision=highest, preferred_element_type=jnp.float32)

def layer_norm(stream, norm_pair):
    centred = stream - lax.optimization_barrier(jnp.mean(stream, -1, keepdims=True))
    return centred * lax.rsqrt(lax.optimization_barrier(jnp.mean(centred * centred, -1, keepdims=True)) + epsilon) * norm_pair[0] + norm_pair[1]

def split_heads(block):
    return block.reshape(block.shape[0], -1, HEAD_DIM).transpose(1, 0, 2)

def join_heads(block):
    return block.transpose(1, 0, 2).reshape(block.shape[1], -1)

def attend(queries, keys, values, bias, allowed):
    raw = low_back(jnp.einsum('hid,hjd->hij', queries, keys, precision=highest) * HEAD_DIM ** (-0.5))
    weights = low(jax.nn.softmax(jnp.where(allowed, raw + bias, masked_score), axis=-1))
    result = jnp.einsum('hij,hjd->hid', weights, values, precision=highest)
    return join_heads(low(low_back(result)))

def project(normed, weight):
    return split_heads(low(low_back(product(normed, weight))))

def self_block(stream, norm_pair, input_weight, result_matrix, bias, allowed):
    normed = low(layer_norm(stream, norm_pair))
    mixed = attend(project(normed, input_weight[0]), project(normed, input_weight[1]), project(normed, input_weight[2]), bias, allowed)
    return stream + low_back(product(mixed, result_matrix))

def feed_block(stream, norm_pair, up_weight, down_weight):
    normed = low(layer_norm(stream, norm_pair))
    hidden_rows = low_back(product(normed, up_weight))
    activated_rows = low(jax.nn.gelu(hidden_rows, approximate=False))
    return stream + low_back(product(activated_rows, down_weight))

def pair_pass(params, biases, stream_enc, stream_dec, len_enc, len_dec):
    norms, attn_in, attn_out, cross_pair, ffn_in, ffn_out = params[1:]
    row_index = lax.broadcasted_iota(jnp.int32, (L, L), 0)
    col_index = lax.broadcasted_iota(jnp.int32, (L, L), 1)
    enc_keys = col_index < len_enc
    dec_allowed = (col_index < len_dec) & (col_index <= row_index)
    enc_rows = (row_index[:, :1] < len_enc).astype(jnp.float32)
    dec_rows = (row_index[:, :1] < len_dec).astype(jnp.float32)
    hidden_enc = self_block(stream_enc, norms[0, 0], attn_in[0], attn_out[0], biases[0], enc_keys)
    hidden_enc = feed_block(hidden_enc, norms[0, 1], ffn_in[0], ffn_out[0])
    enc_out = layer_norm(hidden_enc, norms[0, 2]) * enc_rows
    sent = low(enc_out)
    keys = project(sent, cross_pair[0, 0])
    values = project(sent, cross_pair[0, 1])
    hidden_dec = self_block(stream_dec, norms[1, 0], attn_in[1], attn_out[1], biases[1], dec_allowed)
    normed = low(layer_norm(hidden_dec, norms[1, 1]))
    mixed = attend(project(normed, cross_pair[1, 0]), keys, values, 0.0, enc_keys)
    hidden_dec = hidden_dec + low_back(product(mixed, cross_pair[1, 1].T))
    hidden_dec = feed_block(hidden_dec, norms[1, 2], ffn_in[1], ffn_out[1])
    return (enc_out, hidden_dec * dec_rows)

def reference(frames, lengths, bucket_of, rel_table, norms, attn_in, attn_out, cross_pair, ffn_in, ffn_out, cotangent):
    pairs_total = MB * SEQS
    row_index = lax.broadcasted_iota(jnp.int32, (L, L), 0)
    col_index = lax.broadcasted_iota(jnp.int32, (L, L), 1)
    offsets = (col_index - row_index + L - 1).astype(jnp.int32)
    params = (rel_table, norms, attn_in.astype(jnp.float32), attn_out.astype(jnp.float32), cross_pair.astype(jnp.float32), ffn_in.astype(jnp.float32), ffn_out.astype(jnp.float32))
    inputs = frames.astype(jnp.float32).reshape(2, pairs_total, L, D)
    seq_lengths = lengths.reshape(2, pairs_total)
    checked = jax.checkpoint(pair_pass)

    def forward(params, inputs):
        biases = [jnp.transpose(params[0][section_number][bucket_of[section_number][offsets]], (2, 0, 1)) for section_number in range(2)]

        def visit(carry, member):
            return (carry, checked(params, biases, member[0], member[1], member[2], member[3]))
        carry_out, outputs = lax.scan(visit, jnp.zeros((), jnp.float32), (inputs[0], inputs[1], seq_lengths[0], seq_lengths[1]))
        return outputs
    outputs, pullback = jax.vjp(forward, params, inputs)
    cotangents = cotangent.astype(jnp.float32).reshape(2, pairs_total, L, D)
    gradients, d_inputs = pullback((cotangents[0], cotangents[1]))
    stacked = jnp.stack(outputs)
    squares = lax.optimization_barrier(jnp.sum(stacked * stacked, axis=(1, 2, 3)))
    counted = lax.optimization_barrier(jnp.sum(lengths.astype(jnp.float32), axis=(1, 2)))
    stats = jnp.sqrt(squares / (counted * D))
    full_shape = (2, MB, SEQS, L, D)
    return (stacked.reshape(full_shape).astype(jnp.bfloat16), d_inputs.reshape(full_shape), gradients[0], gradients[1], gradients[2], gradients[3], gradients[4], gradients[5], gradients[6], stats)
```

```python
import jax
import jax.numpy as jnp
from jax import lax
from jax.experimental import pallas as pl
from jax.experimental.pallas import tpu as pltpu
from jax.sharding import PartitionSpec as P

HEAD_DIM = 64


epsilon = 1e-05
masked_score = -1000000000.0
highest = lax.Precision.HIGHEST


def passed_along(value, axis, steps):
    count = lax.axis_size(axis)
    initial, last = (max(0, -steps), min(count, count - steps))
    return lax.ppermute(value, axis, [(source, source + steps) for source in range(initial, last)])


def norm_forward(values, gain_row, shift_row):
    centred = values - jnp.mean(values, -1, keepdims=True)
    reciprocal_factor = lax.rsqrt(jnp.mean(centred * centred, -1, keepdims=True) + epsilon)
    unit_rows = centred * reciprocal_factor
    return (unit_rows * gain_row + shift_row, unit_rows, reciprocal_factor)


def norm_backward(upstream, unit_rows, reciprocal_factor, gain_row):
    scaled = upstream * gain_row
    inner_term = (
        scaled
        - jnp.mean(scaled, -1, keepdims=True)
        - unit_rows * jnp.mean(scaled * unit_rows, -1, keepdims=True)
    )
    return (
        reciprocal_factor * inner_term,
        jnp.sum(upstream * unit_rows, (0, 1)),
        jnp.sum(upstream, (0, 1)),
    )


def gelu_slope(hidden_rows):
    return (
        0.5 * (1.0 + lax.erf(hidden_rows * 0.7071067811865476))
        + hidden_rows * jnp.exp(-0.5 * hidden_rows * hidden_rows) * 0.3989422804014327
    )


def split_heads(block):
    shaped = block.reshape(block.shape[:-1] + (block.shape[-1] // HEAD_DIM, HEAD_DIM))
    return jnp.moveaxis(shaped, -2, -3)


def join_heads(block):
    moved = jnp.moveaxis(block, -3, -2)
    return moved.reshape(moved.shape[:-2] + (moved.shape[-2] * moved.shape[-1],))


def skew_kernel(distance_ref, table_ref):
    width = table_ref.shape[2]
    for head in range(distance_ref.shape[0]):
        row = jnp.broadcast_to(distance_ref[head : head + 1, :], (128, width))
        table_ref[head] = pltpu.roll(row, width - 127, 1, stride=1, stride_axis=0)


def unskew_kernel(band_ref, total_ref):
    width = band_ref.shape[2]
    amount = 127 - lax.broadcasted_iota(jnp.int32, (128, width), 0)
    for head in range(band_ref.shape[0]):
        rows = band_ref[head]
        for bit in range(7):
            rows = jnp.where(((amount >> bit) & 1) == 1, pltpu.roll(rows, 1 << bit, 1), rows)
        total_ref[head : head + 1, :] = jnp.sum(rows, 0, keepdims=True)


def whole():
    return pl.BlockSpec(memory_space=pltpu.VMEM)


def bias_of(distance_bias, length):
    padded = jnp.pad(distance_bias.T, ((0, 0), (0, 1)))
    heads = padded.shape[0]
    table = pl.pallas_call(
        skew_kernel,
        out_shape=jax.ShapeDtypeStruct((heads, 128, 2 * length), jnp.float32),
        in_specs=[whole()],
        out_specs=whole(),
    )(padded)
    starts = [length - 128 - 128 * block for block in range(length // 128)]
    blocks = [table[:, :, start : start + length] for start in starts]
    return jnp.concatenate(blocks, 1)


def unskew_sum(score_total):
    heads, length = (score_total.shape[0], score_total.shape[1])
    band = jnp.zeros((heads, 128, 2 * length), jnp.float32)
    for block in range(length // 128):
        start = length - 128 - 128 * block
        rows = score_total[:, 128 * block : 128 * block + 128]
        band = band + jnp.pad(rows, ((0, 0), (0, 0), (start, length - start)))
    total = pl.pallas_call(
        unskew_kernel,
        out_shape=jax.ShapeDtypeStruct((heads, 2 * length), jnp.float32),
        in_specs=[whole()],
        out_specs=whole(),
    )(band)
    return total[:, : 2 * length - 1]


def score_block(queries, keys, bias, allowed):
    raw = jnp.einsum(
        "hid,hjd->hij", queries, keys, preferred_element_type=jnp.float32
    ) * HEAD_DIM ** (-0.5)
    return jnp.where(allowed, raw + bias, masked_score)


def attend_forward(queries, keys, values, bias, allowed):
    scores = score_block(queries, keys, bias, allowed)
    peak = jnp.max(scores, -1, keepdims=True)
    lifted = jnp.exp(scores - peak)
    total = jnp.sum(lifted, -1, keepdims=True)
    log_total = peak + jnp.log(total)
    weights = (lifted / total).astype(jnp.bfloat16)
    result = jnp.einsum("hij,hjd->hid", weights, values, preferred_element_type=jnp.float32)
    return (result.astype(jnp.bfloat16), log_total[..., 0])


def attend_backward(queries, keys, values, bias, allowed, log_total, upstream):
    scores = score_block(queries, keys, bias, allowed)
    probs = jnp.exp(scores - log_total[..., None])
    d_values = jnp.einsum(
        "hij,hid->hjd", probs.astype(jnp.bfloat16), upstream, preferred_element_type=jnp.float32
    )
    d_probs = jnp.einsum("hid,hjd->hij", upstream, values, preferred_element_type=jnp.float32)
    d_scores = probs * (d_probs - jnp.sum(d_probs * probs, -1, keepdims=True))
    rounded_values = d_scores.astype(jnp.bfloat16)
    d_queries = jnp.einsum(
        "hij,hjd->hid", rounded_values, keys, preferred_element_type=jnp.float32
    ) * HEAD_DIM ** (-0.5)
    d_keys = jnp.einsum(
        "hij,hid->hjd", rounded_values, queries, preferred_element_type=jnp.float32
    ) * HEAD_DIM ** (-0.5)
    return (
        d_queries.astype(jnp.bfloat16),
        d_keys.astype(jnp.bfloat16),
        d_values.astype(jnp.bfloat16),
        d_scores,
    )


def pick_entries(block):
    return lax.all_gather(block, "tensor", axis=1, tiled=True)


def sum_rows(block):
    return lax.psum_scatter(block, "tensor", scatter_dimension=1, tiled=True)


def gather_grads(block):
    return lax.all_gather(block, "tensor", axis=1, tiled=True)


def sum_grads(block):
    return lax.psum_scatter(block, "tensor", scatter_dimension=1, tiled=True)


def feed_forward(collected_rows, up_weight, down_weight):
    hidden_rows = jnp.einsum(
        "jua,ai->jui", collected_rows, up_weight, preferred_element_type=jnp.float32
    )
    activated_rows = jax.nn.gelu(hidden_rows, approximate=False).astype(jnp.bfloat16)
    return (
        jnp.einsum("jry,yx->jrx", activated_rows, down_weight, preferred_element_type=jnp.float32),
        hidden_rows,
        activated_rows,
    )


def feed_backward(
    rounded_values, collected_rows, hidden_rows, activated_rows, up_weight, down_weight
):
    down_weight_gradient = jnp.einsum(
        "nxv,nxt->vt", activated_rows, rounded_values, preferred_element_type=jnp.float32
    )
    activated_gradient = jnp.einsum(
        "hot,pt->hop", rounded_values, down_weight, preferred_element_type=jnp.float32
    )
    hidden_gradient = (activated_gradient * gelu_slope(hidden_rows)).astype(jnp.bfloat16)
    up_weight_gradient = jnp.einsum(
        "qwk,qwz->kz", collected_rows, hidden_gradient, preferred_element_type=jnp.float32
    )
    branch_portion = jnp.einsum(
        "knu,zu->knz", hidden_gradient, up_weight, preferred_element_type=jnp.float32
    )
    return (branch_portion, up_weight_gradient, down_weight_gradient)


def layer_forward(inputs16, keys_values, weights, context):
    norm_gains, input_weight, result_matrix, cross_weight, up_weight, down_weight = weights
    decoder, self_bias, self_allowed, cross_allowed, row_mask = context
    heads_here = input_weight.shape[2] // HEAD_DIM
    inputs = inputs16.astype(jnp.float32)
    normed, unit_one, inverse_one = norm_forward(inputs, norm_gains[0, 0], norm_gains[0, 1])
    gathered_single = pick_entries(normed.astype(jnp.bfloat16))
    seq_count, length = (gathered_single.shape[0], gathered_single.shape[1])
    projected = split_heads(
        jnp.einsum(
            "fgh,whn->wfgn", gathered_single, input_weight, preferred_element_type=jnp.float32
        ).astype(jnp.bfloat16)
    )

    def self_one(member):
        return attend_forward(member[0], member[1], member[2], self_bias, member[3])

    result_heads, lse_one = lax.map(
        self_one, (projected[0], projected[1], projected[2], self_allowed)
    )
    outcome_first = join_heads(result_heads)
    after_one = inputs + sum_rows(
        jnp.einsum("fpr,rg->fpg", outcome_first, result_matrix, preferred_element_type=jnp.float32)
    )
    normed, unit_two, inverse_two = norm_forward(after_one, norm_gains[1, 0], norm_gains[1, 1])
    collected_two = pick_entries(normed.astype(jnp.bfloat16))
    hidden_zeros = jnp.zeros((seq_count, length, up_weight.shape[1]), jnp.float32)

    def cross_one(member):
        return attend_forward(member[0], member[1], member[2], 0.0, member[3])

    def cross_branch(collected_rows):
        queries = split_heads(
            jnp.einsum(
                "uzm,my->uzy", collected_rows, cross_weight[0], preferred_element_type=jnp.float32
            ).astype(jnp.bfloat16)
        )
        sources = split_heads(keys_values)
        result_cross, lse_cross = lax.map(
            cross_one, (queries, sources[0], sources[1], cross_allowed)
        )
        merged_heads = join_heads(result_cross)
        branch_portion = jnp.einsum(
            "upj,tj->upt", merged_heads, cross_weight[1], preferred_element_type=jnp.float32
        )
        return (
            branch_portion,
            queries,
            merged_heads,
            lse_cross,
            hidden_zeros,
            hidden_zeros.astype(jnp.bfloat16),
        )

    def feed_branch(collected_rows):
        branch_portion, hidden_rows, activated_rows = feed_forward(
            collected_rows, up_weight, down_weight
        )
        query_zeros = jnp.zeros((seq_count, heads_here, length, HEAD_DIM), jnp.bfloat16)
        joined_zeros = jnp.zeros((seq_count, length, input_weight.shape[2]), jnp.bfloat16)
        lse_zeros = jnp.zeros((seq_count, heads_here, length), jnp.float32)
        return (branch_portion, query_zeros, joined_zeros, lse_zeros, hidden_rows, activated_rows)

    part_two, queries, merged_heads_two, lse_two, hidden_two, active_two = lax.cond(
        decoder, cross_branch, feed_branch, collected_two
    )
    after_two = after_one + sum_rows(part_two)
    normed, unit_three, inverse_three = norm_forward(after_two, norm_gains[2, 0], norm_gains[2, 1])
    normed = jnp.where(decoder, normed, normed * row_mask)
    collected_three = pick_entries(normed.astype(jnp.bfloat16))
    kv_zeros = jnp.zeros((2, seq_count, length, input_weight.shape[2]), jnp.bfloat16)

    def feed_third(collected_rows):
        branch_portion, hidden_rows, activated_rows = feed_forward(
            collected_rows, up_weight, down_weight
        )
        return (branch_portion, hidden_rows, activated_rows, kv_zeros)

    def project_third(collected_rows):
        kv_new = jnp.einsum(
            "fgh,whn->wfgn", collected_rows, cross_weight, preferred_element_type=jnp.float32
        ).astype(jnp.bfloat16)
        return (jnp.zeros(collected_rows.shape, jnp.float32), hidden_two, active_two, kv_new)

    part_three, hidden_used, active_used, kv_new = lax.cond(
        decoder, feed_third, project_third, collected_three
    )
    after_three = after_two + sum_rows(part_three)
    result = jnp.where(decoder, after_three * row_mask, normed)
    saved = (
        unit_one,
        inverse_one,
        gathered_single,
        projected,
        outcome_first,
        lse_one,
        unit_two,
        inverse_two,
        collected_two,
        queries,
        merged_heads_two,
        lse_two,
        unit_three,
        inverse_three,
        collected_three,
        hidden_used,
        active_used,
    )
    return (result, saved, kv_new)


def layer_backward(saved, upstream, returned_key_value, keys_values, weights, context):
    norm_gains, input_weight, result_matrix, cross_weight, up_weight, down_weight = weights
    decoder, self_bias, self_allowed, cross_allowed, row_mask = context
    (
        unit_one,
        inverse_one,
        gathered_single,
        projected,
        outcome_first,
        lse_one,
        unit_two,
        inverse_two,
        collected_two,
        queries,
        merged_heads_two,
        lse_two,
        unit_three,
        inverse_three,
        collected_three,
        hidden_used,
        active_used,
    ) = saved
    cross_zeros = jnp.zeros(cross_weight.shape, jnp.float32)
    up_zeros = jnp.zeros(up_weight.shape, jnp.float32)
    down_zeros = jnp.zeros(down_weight.shape, jnp.float32)
    cot_masked = upstream * row_mask
    incoming = gather_grads(jnp.where(decoder, cot_masked, 0.0).astype(jnp.bfloat16))

    def decoder_first(collected_rows):
        branch_portion, up_weight_gradient, down_weight_gradient = feed_backward(
            collected_rows, collected_three, hidden_used, active_used, up_weight, down_weight
        )
        return (branch_portion, cross_zeros, up_weight_gradient, down_weight_gradient)

    def encoder_first(collected_rows):
        branch_portion = jnp.einsum(
            "mgky,mty->gkt", returned_key_value, cross_weight, preferred_element_type=jnp.float32
        )
        d_cross = jnp.einsum(
            "wxn,rwxo->rno", collected_three, returned_key_value, preferred_element_type=jnp.float32
        )
        return (branch_portion, d_cross, up_zeros, down_zeros)

    part_first, cross_first, expand_leading, down_first = lax.cond(
        decoder, decoder_first, encoder_first, incoming
    )
    summed_first = sum_grads(part_first)
    upstream_first = jnp.where(decoder, summed_first, (upstream + summed_first) * row_mask)
    norm_first, gain_first, shift_first = norm_backward(
        upstream_first, unit_three, inverse_three, norm_gains[2, 0]
    )
    grad_two = jnp.where(decoder, cot_masked, 0.0) + norm_first
    gathered_grad_two = gather_grads(grad_two.astype(jnp.bfloat16))

    def cross_back(member):
        d_query, d_key, d_value, d_scores = attend_backward(
            member[0], member[1], member[2], 0.0, member[3], member[4], member[5]
        )
        return (d_query, d_key, d_value)

    def decoder_second(collected_rows):
        d_out_w = jnp.einsum(
            "vhg,vhr->gr", collected_rows, merged_heads_two, preferred_element_type=jnp.float32
        )
        d_joined = split_heads(
            jnp.einsum(
                "uzm,my->uzy", collected_rows, cross_weight[1], preferred_element_type=jnp.float32
            ).astype(jnp.bfloat16)
        )
        sources = split_heads(keys_values)
        d_query, d_key, d_value = lax.map(
            cross_back, (queries, sources[0], sources[1], cross_allowed, lse_two, d_joined)
        )
        flattened_query = join_heads(d_query)
        d_query_w = jnp.einsum(
            "vhg,vhr->gr", collected_two, flattened_query, preferred_element_type=jnp.float32
        )
        branch_portion = jnp.einsum(
            "upj,tj->upt", flattened_query, cross_weight[0], preferred_element_type=jnp.float32
        )
        kv_grad = jnp.stack([join_heads(d_key), join_heads(d_value)])
        return (branch_portion, jnp.stack([d_query_w, d_out_w]), up_zeros, down_zeros, kv_grad)

    def encoder_second(collected_rows):
        branch_portion, up_weight_gradient, down_weight_gradient = feed_backward(
            collected_rows, collected_two, hidden_used, active_used, up_weight, down_weight
        )
        return (
            branch_portion,
            cross_zeros,
            up_weight_gradient,
            down_weight_gradient,
            jnp.zeros(keys_values.shape, jnp.bfloat16),
        )

    part_second, cross_second, up_second, down_second, kv_grad = lax.cond(
        decoder, decoder_second, encoder_second, gathered_grad_two
    )
    summed_second = sum_grads(part_second)
    norm_second, gain_second, shift_second = norm_backward(
        summed_second, unit_two, inverse_two, norm_gains[1, 0]
    )
    grad_one = grad_two + norm_second
    gathered_derivative_single = gather_grads(grad_one.astype(jnp.bfloat16))

    def self_back(member):
        return attend_backward(
            member[0], member[1], member[2], self_bias, member[3], member[4], member[5]
        )

    d_attn_out = jnp.einsum(
        "rnb,rnx->bx", outcome_first, gathered_derivative_single, preferred_element_type=jnp.float32
    )
    d_joined = split_heads(
        jnp.einsum(
            "lus,ts->lut",
            gathered_derivative_single,
            result_matrix,
            preferred_element_type=jnp.float32,
        ).astype(jnp.bfloat16)
    )
    d_query, d_key, d_value, d_scores = lax.map(
        self_back, (projected[0], projected[1], projected[2], self_allowed, lse_one, d_joined)
    )
    projection_gradient = jnp.stack([join_heads(d_query), join_heads(d_key), join_heads(d_value)])
    d_attn_in = jnp.einsum(
        "wxn,rwxo->rno", gathered_single, projection_gradient, preferred_element_type=jnp.float32
    )
    summed_third = sum_grads(
        jnp.einsum(
            "mgky,mty->gkt", projection_gradient, input_weight, preferred_element_type=jnp.float32
        )
    )
    norm_third, gain_third, shift_third = norm_backward(
        summed_third, unit_one, inverse_one, norm_gains[0, 0]
    )
    grad_input = grad_one + norm_third
    gain_grads = jnp.stack(
        [
            jnp.stack([gain_third, shift_third]),
            jnp.stack([gain_second, shift_second]),
            jnp.stack([gain_first, shift_first]),
        ]
    )
    tick_grads = (
        jnp.sum(d_scores, 0),
        gain_grads,
        d_attn_in,
        d_attn_out,
        cross_first + cross_second,
        expand_leading + up_second,
        down_first + down_second,
    )
    return (grad_input, kv_grad, tick_grads)


def put_block(store, block_index, value):
    return lax.dynamic_update_index_in_dim(store, value, block_index, 0)


def body(
    frames,
    lengths,
    bucket_of,
    rel_table,
    norms,
    attn_in,
    attn_out,
    cross_pair,
    ffn_in,
    ffn_out,
    cotangent,
):
    section_index = lax.axis_index("section")
    decoder = section_index == 1
    micro_count = frames.shape[1]
    seq_count = frames.shape[2]
    quarter = frames.shape[3]
    model_width = frames.shape[4]
    length = quarter * lax.axis_size("tensor")
    head_width = attn_in.shape[3]
    bucket_count = rel_table.shape[1]
    weights = (norms[0], attn_in[0], attn_out[0], cross_pair[0], ffn_in[0], ffn_out[0])
    row_index = lax.broadcasted_iota(jnp.int32, (length, length), 0)
    col_index = lax.broadcasted_iota(jnp.int32, (length, length), 1)
    one_hot = (
        bucket_of[0][:, None] == lax.broadcasted_iota(jnp.int32, (1, bucket_count), 1)
    ).astype(jnp.float32)
    distance_bias = jnp.dot(
        one_hot, rel_table[0], precision=highest, preferred_element_type=jnp.float32
    )
    self_bias = bias_of(distance_bias, length)
    own_lengths = lax.dynamic_index_in_dim(lengths, section_index, 0, keepdims=False)
    positions = lax.axis_index("tensor") * quarter + lax.broadcasted_iota(
        jnp.int32, (1, quarter, 1), 1
    )

    def context_of(block_index):
        own_length = lax.dynamic_index_in_dim(own_lengths, block_index, 0, keepdims=False)
        source_length = lax.dynamic_index_in_dim(lengths[0], block_index, 0, keepdims=False)
        keys_ok = col_index[None] < own_length[:, None, None]
        causal = (col_index <= row_index)[None] | jnp.logical_not(decoder)
        self_allowed = (keys_ok & causal)[:, None]
        cross_allowed = (col_index[None] < source_length[:, None, None])[:, None]
        row_mask = (positions < own_length[:, None, None]).astype(jnp.float32)
        return (decoder, self_bias, self_allowed, cross_allowed, row_mask)

    slot_count = micro_count + 1
    empty_kv = jnp.zeros((2, seq_count, length, head_width), jnp.bfloat16)
    received = empty_kv
    kv_store = jnp.zeros((micro_count,) + empty_kv.shape, jnp.bfloat16)
    out_store = jnp.zeros((slot_count, seq_count, quarter, model_width), jnp.float32)
    saved_store = None
    for tick_number in range(micro_count + 1):
        raw_index = tick_number - section_index
        is_valid = (raw_index >= 0) & (raw_index < micro_count)
        block_index = jnp.clip(raw_index, 0, micro_count - 1)
        write_index = jnp.where(is_valid, block_index, micro_count)
        context = context_of(block_index)
        inputs16 = lax.dynamic_index_in_dim(frames[0], block_index, 0, keepdims=False)
        result, saved, kv_new = layer_forward(inputs16, received, weights, context)
        kv_store = put_block(kv_store, block_index, received)
        out_store = put_block(out_store, write_index, result)
        if saved_store is None:
            saved_store = jax.tree.map(
                lambda array_leaf: jnp.zeros((slot_count,) + array_leaf.shape, array_leaf.dtype),
                saved,
            )
        saved_store = jax.tree.map(
            lambda saved_tree_node, array_leaf: put_block(saved_tree_node, write_index, array_leaf),
            saved_store,
            saved,
        )
        if tick_number < micro_count:
            received = passed_along(kv_new, "section", 1)
    returned = empty_kv
    grads_store = jnp.zeros((slot_count, seq_count, quarter, model_width), jnp.float32)
    totals = None
    for tick_number in range(micro_count + 1):
        raw_index = tick_number - 1 + section_index
        is_valid = (raw_index >= 0) & (raw_index < micro_count)
        block_index = jnp.clip(raw_index, 0, micro_count - 1)
        write_index = jnp.where(is_valid, block_index, micro_count)
        context = context_of(block_index)
        keys_values = lax.dynamic_index_in_dim(kv_store, block_index, 0, keepdims=False)
        saved = jax.tree.map(
            lambda saved_tree_node: lax.dynamic_index_in_dim(
                saved_tree_node, block_index, 0, keepdims=False
            ),
            saved_store,
        )
        upstream = lax.dynamic_index_in_dim(cotangent[0], block_index, 0, keepdims=False).astype(
            jnp.float32
        )
        grad_input, kv_grad, tick_grads = layer_backward(
            saved, upstream, returned, keys_values, weights, context
        )
        grads_store = put_block(grads_store, write_index, grad_input)
        tick_grads = jax.tree.map(
            lambda array_leaf: jnp.where(is_valid, array_leaf, 0.0), tick_grads
        )
        totals = tick_grads if totals is None else jax.tree.map(jnp.add, totals, tick_grads)
        if tick_number < micro_count:
            returned = passed_along(kv_grad, "section", -1)
    out_final = out_store[:micro_count]
    grads_final = grads_store[:micro_count]
    spread = unskew_sum(totals[0])
    squares = jnp.sum(out_final * out_final)
    valid_rows = jnp.sum((positions[None] < own_lengths[:, :, None, None]).astype(jnp.float32))
    gain_total, square_total, count_total = lax.psum(
        (totals[1], squares, valid_rows), ("dp", "tensor")
    )
    stats = jnp.sqrt(square_total / (count_total * model_width)).reshape(1)
    local_shape = (1, micro_count, seq_count, quarter, model_width)
    return (
        out_final.reshape(local_shape).astype(jnp.bfloat16),
        grads_final.reshape(local_shape),
        lax.psum(
            jnp.dot(
                one_hot.T, spread.T, precision=highest, preferred_element_type=jnp.float32
            ).astype(jnp.bfloat16),
            "dp",
        ).astype(jnp.float32)[None],
        gain_total[None],
        lax.psum(totals[2].astype(jnp.bfloat16), "dp").astype(jnp.float32)[None],
        lax.psum(totals[3].astype(jnp.bfloat16), "dp").astype(jnp.float32)[None],
        lax.psum(totals[4].astype(jnp.bfloat16), "dp").astype(jnp.float32)[None],
        lax.psum(totals[5].astype(jnp.bfloat16), "dp").astype(jnp.float32)[None],
        lax.psum(totals[6].astype(jnp.bfloat16), "dp").astype(jnp.float32)[None],
        stats,
    )


def solution(mesh):
    in_specs = (
        P("section", None, "dp", "tensor", None),
        P(None, None, "dp"),
        P("section", None),
        P("section", None, "tensor"),
        P("section", None, None, None),
        P("section", None, None, "tensor"),
        P("section", "tensor", None),
        P("section", None, None, "tensor"),
        P("section", None, "tensor"),
        P("section", "tensor", None),
        P("section", None, "dp", "tensor", None),
    )
    out_specs = (
        P("section", None, "dp", "tensor", None),
        P("section", None, "dp", "tensor", None),
        P("section", None, "tensor"),
        P("section", None, None, None),
        P("section", None, None, "tensor"),
        P("section", "tensor", None),
        P("section", None, None, "tensor"),
        P("section", None, "tensor"),
        P("section", "tensor", None),
        P("section"),
    )
    return jax.shard_map(body, mesh=mesh, in_specs=in_specs, out_specs=out_specs, check_vma=False)
```

```python
import functools
import math

import jax
import jax.numpy as jnp
from jax import lax
from jax.experimental import pallas as pl
from jax.experimental.pallas import tpu as pltpu
from jax.sharding import PartitionSpec as P

HEAD_DIM = 64
SCALE = HEAD_DIM ** (-0.5)
EPSILON = 1e-05
MASKED = -1000000000.0
HIGHEST = lax.Precision.HIGHEST
BF = jnp.bfloat16
F32 = jnp.float32
NN = (((1,), (0,)), ((), ()))
NT = (((1,), (1,)), ((), ()))
TN = (((0,), (0,)), ((), ()))
TILE = 256
BAND = 128
ENCODER, DECODER = 0, 1
ROLE, OWN_LEN, SOURCE_LEN, CORE, START = 0, 1, 2, 3, 4
VMEM_BYTES = 58 * 1024 * 1024


def mm(left, right, dims):
    return lax.dot_general(left, right, dims, preferred_element_type=F32)


def whole():
    return pl.BlockSpec(memory_space=pltpu.VMEM)


def scalars():
    return pl.BlockSpec(memory_space=pltpu.SMEM)


def shape(dims, dtype):
    return jax.ShapeDtypeStruct(dims, dtype)


def cost(flops, nbytes, exps=0):
    return pl.CostEstimate(flops=int(flops), bytes_accessed=int(nbytes), transcendentals=int(exps))


def params(**extra):
    return pltpu.CompilerParams(vmem_limit_bytes=VMEM_BYTES, **extra)


def norm_of(values, norm_ref):
    centred = values - jnp.mean(values, -1, keepdims=True)
    factor = lax.rsqrt(jnp.mean(centred * centred, -1, keepdims=True) + EPSILON)
    return centred * factor * norm_ref[0:1, :] + norm_ref[1:2, :]


def enter_kernel(info, mine, core_mine, far, core_far, norm_ref, rows_ref, normed_ref):
    quarter = mine.shape[0]
    for step, piece in enumerate((mine, core_mine, far, core_far)):
        start = pl.multiple_of(info[START + step], quarter)
        values = piece[...]
        rows_ref[pl.ds(start, quarter), :] = values
        normed_ref[pl.ds(start, quarter), :] = norm_of(values.astype(F32), norm_ref).astype(BF)


def enter(info, pieces, norm):
    quarter, width = pieces[0].shape
    out = shape((4 * quarter, width), BF)
    return pl.pallas_call(
        enter_kernel,
        out_shape=(out, out),
        in_specs=[scalars()] + [whole()] * 5,
        out_specs=(whole(), whole()),
        compiler_params=params(),
        cost_estimate=cost(16 * quarter * width * 4, quarter * width * 24),
    )(info, *pieces, norm)


def masked_kernel(info, mine, core_mine, far, core_far, rows_ref):
    quarter = mine.shape[0]
    for step, piece in enumerate((mine, core_mine, far, core_far)):
        start = pl.multiple_of(info[START + step], quarter)
        row = start + lax.broadcasted_iota(jnp.int32, (quarter, 1), 0)
        values = jnp.where(row < info[OWN_LEN], piece[...].astype(F32), 0.0)
        rows_ref[pl.ds(start, quarter), :] = values.astype(BF)


def masked_rows(info, pieces):
    quarter, width = pieces[0].shape
    return pl.pallas_call(
        masked_kernel,
        out_shape=shape((4 * quarter, width), BF),
        in_specs=[scalars()] + [whole()] * 4,
        out_specs=whole(),
        compiler_params=params(),
        cost_estimate=cost(quarter * width * 8, quarter * width * 16),
    )(info, *pieces)


def skew_kernel(distance_ref, table_ref):
    width = table_ref.shape[2]
    for head in range(distance_ref.shape[0]):
        row = jnp.broadcast_to(distance_ref[head : head + 1, :], (BAND, width))
        table_ref[head] = pltpu.roll(row, width - (BAND - 1), 1, stride=1, stride_axis=0)


def skew(distances):
    heads, width = distances.shape
    return pl.pallas_call(
        skew_kernel,
        out_shape=shape((heads, BAND, width), F32),
        in_specs=[whole()],
        out_specs=whole(),
        compiler_params=params(),
        cost_estimate=cost(heads * BAND * width, heads * BAND * width * 4),
    )(distances)


def unskewed(band):
    width = band.shape[1]
    amount = (BAND - 1) - lax.broadcasted_iota(jnp.int32, (BAND, width), 0)
    for bit in range(7):
        band = jnp.where(((amount >> bit) & 1) == 1, pltpu.roll(band, 1 << bit, 1), band)
    return jnp.sum(band, 0, keepdims=True)


def lane_limit(info, row_start, rows, causal, length_at):
    last = info[length_at] - 1
    if not causal:
        return last
    row = row_start + lax.broadcasted_iota(jnp.int32, (rows, 1), 0)
    free = jnp.where(info[ROLE] == DECODER, 0, 1 << 20)
    return jnp.minimum(row + free, last)


def bias_block(table_ref, head, row_start, length):
    blocks = []
    for part in range(TILE // BAND):
        offset = pl.multiple_of(length - BAND - row_start - part * BAND, BAND)
        blocks.append(table_ref[head, :, pl.ds(offset, length)])
    return jnp.concatenate(blocks, 0)


def attend_loop(info, qkv_ref, table_ref, out_ref, lse_ref, length_at):
    length, width = out_ref.shape
    causal = table_ref is not None

    def block(index, carry):
        start = pl.multiple_of(index * TILE, TILE)
        rows = pl.ds(start, TILE)
        limit = lane_limit(info, start, TILE, causal, length_at)
        allowed = lax.broadcasted_iota(jnp.int32, (TILE, length), 1) <= limit
        for head in range(width // HEAD_DIM):
            span = slice(head * HEAD_DIM, (head + 1) * HEAD_DIM)
            queries = qkv_ref[0, rows, span] * jnp.asarray(SCALE, BF)
            scores = mm(queries, qkv_ref[1, :, span], NT)
            if causal:
                scores = scores + bias_block(table_ref, head, start, length)
            scores = jnp.where(allowed, scores, MASKED)
            peak = jnp.max(scores, -1, keepdims=True)
            lifted = jnp.exp(scores - peak)
            total = jnp.sum(lifted, -1, keepdims=True)
            mixed = mm(lifted.astype(BF), qkv_ref[2, :, span], NN)
            out_ref[rows, span] = (mixed / total).astype(BF)
            lse_ref[rows, head : head + 1] = peak + jnp.log(total)
        return carry

    lax.fori_loop(0, length // TILE, block, 0)


def by_rows(count, body):
    def step(index, carry):
        body(pl.ds(pl.multiple_of(index * TILE, TILE), TILE))
        return carry

    lax.fori_loop(0, count // TILE, step, 0)


def self_forward_kernel(has_sum, info, normed, weights, project, table, *refs):
    previous = refs[0] if has_sum else None
    sum_ref, qkv_ref, out_ref, lse_ref = refs[1 if has_sum else 0 :]
    length = out_ref.shape[0]

    def inputs(rows):
        block = normed[rows, :]
        for place in range(3):
            qkv_ref[place, rows, :] = mm(block, weights[place], NN).astype(BF)

    by_rows(length, inputs)
    attend_loop(info, qkv_ref, table, out_ref, lse_ref, OWN_LEN)

    def outputs(rows):
        value = mm(out_ref[rows, :], project[...], NN)
        if has_sum:
            value = value + previous[rows, :]
        sum_ref[rows, :] = value.astype(sum_ref.dtype)

    by_rows(length, outputs)


def attention_cost(length, width, model, matmuls, projections):
    heads = width // HEAD_DIM
    return cost(
        heads * length * length * HEAD_DIM * 2 * matmuls * 4 + projections * 2 * length * model * width,
        length * model * 8,
        heads * length * length,
    )


def self_forward(info, normed, weights, project, table, previous):
    length, model = normed.shape
    width = project.shape[0]
    has_sum = previous is not None
    operands = [info, normed, weights, project, table] + ([previous] if has_sum else [])
    return pl.pallas_call(
        functools.partial(self_forward_kernel, has_sum),
        out_shape=(
            shape((length, model), BF if has_sum else F32),
            shape((3, length, width), BF),
            shape((length, width), BF),
            shape((length, 128), F32),
        ),
        in_specs=[scalars()] + [whole()] * (len(operands) - 1),
        out_specs=(whole(),) * 4,
        compiler_params=params(),
        cost_estimate=attention_cost(length, width, model, 2, 4),
    )(*operands)


def cross_forward_kernel(has_sum, info, normed, near, far, query_pair, source_pair, *refs):
    previous = refs[0] if has_sum else None
    sum_ref, qkv_ref, out_ref, lse_ref = refs[1 if has_sum else 0 :]
    length = out_ref.shape[0]
    half = near.shape[0]

    @pl.when(info[ROLE] == DECODER)
    def _():
        def queries(rows):
            qkv_ref[0, rows, :] = mm(normed[rows, :], query_pair[0], NN).astype(BF)

        by_rows(length, queries)
        for piece, side in ((near, info[CORE]), (far, 1 - info[CORE])):
            base = side * half

            def sources(index, carry, piece=piece, base=base):
                local = pl.multiple_of(index * TILE, TILE)
                block = piece[pl.ds(local, TILE), :]
                rows = pl.ds(pl.multiple_of(base + local, TILE), TILE)
                for place in range(2):
                    qkv_ref[1 + place, rows, :] = mm(block, source_pair[place], NN).astype(BF)
                return carry

            lax.fori_loop(0, half // TILE, sources, 0)
        attend_loop(info, qkv_ref, None, out_ref, lse_ref, SOURCE_LEN)

        def outputs(rows):
            value = mm(out_ref[rows, :], query_pair[1], NT)
            if has_sum:
                value = value + previous[rows, :]
            sum_ref[rows, :] = value.astype(sum_ref.dtype)

        by_rows(length, outputs)


def cross_forward(info, normed, near, far, query_pair, source_pair, previous):
    length, model = normed.shape
    width = query_pair.shape[2]
    has_sum = previous is not None
    operands = [info, normed, near, far, query_pair, source_pair]
    operands += [previous] if has_sum else []
    return pl.pallas_call(
        functools.partial(cross_forward_kernel, has_sum),
        out_shape=(
            shape((length, model), BF if has_sum else F32),
            shape((3, length, width), BF),
            shape((length, width), BF),
            shape((length, 128), F32),
        ),
        in_specs=[scalars()] + [whole()] * (len(operands) - 1),
        out_specs=(whole(),) * 4,
        compiler_params=params(),
        cost_estimate=attention_cost(length, width, model, 2, 4),
    )(*operands)


def attend_back_loop(
    info, qkv_ref, table_ref, lse_ref, upstream, grads_ref, key_sum, value_sum, band, length_at
):
    length, width = upstream.shape
    causal = table_ref is not None
    key_sum[...] = jnp.zeros_like(key_sum)
    value_sum[...] = jnp.zeros_like(value_sum)
    if causal:
        band[...] = jnp.zeros_like(band)

    def block(index, carry):
        start = pl.multiple_of(index * TILE, TILE)
        rows = pl.ds(start, TILE)
        limit = lane_limit(info, start, TILE, causal, length_at)
        allowed = lax.broadcasted_iota(jnp.int32, (TILE, length), 1) <= limit
        for head in range(width // HEAD_DIM):
            span = slice(head * HEAD_DIM, (head + 1) * HEAD_DIM)
            queries = qkv_ref[0, rows, span] * jnp.asarray(SCALE, BF)
            keys = qkv_ref[1, :, span]
            scores = mm(queries, keys, NT)
            if causal:
                scores = scores + bias_block(table_ref, head, start, length)
            probs = jnp.where(allowed, jnp.exp(scores - lse_ref[rows, head : head + 1]), 0.0)
            above = upstream[rows, span]
            d_probs = mm(above, qkv_ref[2, :, span], NT)
            inner = jnp.sum(d_probs * probs, -1, keepdims=True)
            d_scores = probs * (d_probs - inner)
            low = d_scores.astype(BF)
            grads_ref[0, rows, span] = (mm(low, keys, NN) * SCALE).astype(BF)
            key_sum[span, :] += mm(queries, low, TN)
            value_sum[span, :] += mm(above, probs.astype(BF), TN)
            if causal:
                for part in range(TILE // BAND):
                    offset = pl.multiple_of(length - BAND - start - part * BAND, BAND)
                    cols = pl.ds(offset, length)
                    band[head, :, cols] += d_scores[part * BAND : (part + 1) * BAND, :]
        return carry

    lax.fori_loop(0, length // TILE, block, 0)
    grads_ref[1] = key_sum[...].T.astype(BF)
    grads_ref[2] = value_sum[...].T.astype(BF)


def self_backward_kernel(has_sum, info, qkv, lse, above, weights, project, table, *refs):
    previous = refs[0] if has_sum else None
    sum_ref, grads_ref, spread_ref, upstream, key_sum, value_sum, band = refs[1 if has_sum else 0 :]
    length = above.shape[0]

    def entering(rows):
        upstream[rows, :] = mm(above[rows, :], project[...], NT).astype(BF)

    by_rows(length, entering)
    attend_back_loop(
        info, qkv, table, lse, upstream, grads_ref, key_sum, value_sum, band, OWN_LEN
    )

    def leaving(rows):
        value = mm(grads_ref[0, rows, :], weights[0], NT)
        for place in (1, 2):
            value = value + mm(grads_ref[place, rows, :], weights[place], NT)
        if has_sum:
            value = value + previous[rows, :]
        sum_ref[rows, :] = value.astype(sum_ref.dtype)

    by_rows(length, leaving)
    for head in range(table.shape[0]):
        spread_ref[head : head + 1, :] = unskewed(band[head])


def self_backward(info, qkv, lse, above, weights, project, table, previous):
    length, model = above.shape
    width = project.shape[0]
    has_sum = previous is not None
    operands = [info, qkv, lse, above, weights, project, table]
    operands += [previous] if has_sum else []
    return pl.pallas_call(
        functools.partial(self_backward_kernel, has_sum),
        out_shape=(
            shape((length, model), BF if has_sum else F32),
            shape((3, length, width), BF),
            shape((table.shape[0], table.shape[2]), F32),
        ),
        in_specs=[scalars()] + [whole()] * (len(operands) - 1),
        out_specs=(whole(),) * 3,
        scratch_shapes=[
            pltpu.VMEM((length, width), BF),
            pltpu.VMEM((width, length), F32),
            pltpu.VMEM((width, length), F32),
            pltpu.VMEM(table.shape, F32),
        ],
        compiler_params=params(),
        cost_estimate=attention_cost(length, width, model, 5, 4),
    )(*operands)


def cross_backward_kernel(has_sum, info, qkv, lse, above, query_pair, source_pair, *refs):
    before = refs[:2] if has_sum else (None, None)
    sum_ref, source_ref, grads_ref, upstream, key_sum, value_sum = refs[2 if has_sum else 0 :]
    length = above.shape[0]

    @pl.when(info[ROLE] == DECODER)
    def _():
        def entering(rows):
            upstream[rows, :] = mm(above[rows, :], query_pair[1], NN).astype(BF)

        by_rows(length, entering)
        attend_back_loop(
            info, qkv, None, lse, upstream, grads_ref, key_sum, value_sum, None, SOURCE_LEN
        )

        def leaving(rows):
            value = mm(grads_ref[0, rows, :], query_pair[0], NT)
            source = mm(grads_ref[1, rows, :], source_pair[0], NT)
            source = source + mm(grads_ref[2, rows, :], source_pair[1], NT)
            if has_sum:
                value = value + before[0][rows, :]
                source = source + before[1][rows, :]
            sum_ref[rows, :] = value.astype(sum_ref.dtype)
            source_ref[rows, :] = source.astype(source_ref.dtype)

        by_rows(length, leaving)


def cross_backward(info, qkv, lse, above, query_pair, source_pair, before):
    length, model = above.shape
    width = query_pair.shape[2]
    has_sum = before is not None
    operands = [info, qkv, lse, above, query_pair, source_pair] + (list(before) if has_sum else [])
    out = shape((length, model), BF if has_sum else F32)
    return pl.pallas_call(
        functools.partial(cross_backward_kernel, has_sum),
        out_shape=(out, out, shape((3, length, width), BF)),
        in_specs=[scalars()] + [whole()] * (len(operands) - 1),
        out_specs=(whole(),) * 3,
        scratch_shapes=[
            pltpu.VMEM((length, width), BF),
            pltpu.VMEM((width, length), F32),
            pltpu.VMEM((width, length), F32),
        ],
        compiler_params=params(),
        cost_estimate=attention_cost(length, width, model, 5, 4),
    )(*operands)


def row_spec(width):
    return pl.BlockSpec((TILE, width), lambda index: (index, 0))


def fixed_spec(dims):
    return pl.BlockSpec(dims, lambda index: (0,) * len(dims))


def add_norm_kernel(stream, near, far, norm_ref, sum_ref, normed_ref):
    value = stream[...].astype(F32) + (near[...].astype(F32) + far[...].astype(F32))
    sum_ref[...] = value
    normed_ref[...] = norm_of(value, norm_ref).astype(BF)


def add_norm(stream, near, far, norm):
    length, model = stream.shape
    return pl.pallas_call(
        add_norm_kernel,
        grid=(length // TILE,),
        out_shape=(shape((length, model), F32), shape((length, model), BF)),
        in_specs=[row_spec(model)] * 3 + [fixed_spec((2, model))],
        out_specs=(row_spec(model),) * 2,
        compiler_params=params(),
        cost_estimate=cost(length * model * 12, length * model * 14),
    )(stream, near, far, norm)


def row_mask(info, index, at):
    row = index * TILE + lax.broadcasted_iota(jnp.int32, (TILE, 1), 0)
    return row < info[at]


def squares_of(value):
    return jnp.sum(jnp.sum(value * value, 0, keepdims=True), 1, keepdims=True)


def source_kernel(info, stream, near, far, norm_ref, sum_ref, sent_ref, square_ref):
    index = pl.program_id(0)
    value = stream[...] + (near[...].astype(F32) + far[...].astype(F32))
    sum_ref[...] = value
    result = jnp.where(row_mask(info, index, OWN_LEN), norm_of(value, norm_ref), 0.0)
    sent_ref[...] = result.astype(BF)

    @pl.when(index == 0)
    def _():
        square_ref[...] = jnp.zeros_like(square_ref)

    square_ref[...] += squares_of(result)


def source_out(info, stream, near, far, norm):
    length, model = stream.shape
    return pl.pallas_call(
        source_kernel,
        grid=(length // TILE,),
        out_shape=(shape((length, model), F32), shape((length, model), BF), shape((8, 128), F32)),
        in_specs=[scalars()] + [row_spec(model)] * 3 + [fixed_spec((2, model))],
        out_specs=(row_spec(model), row_spec(model), fixed_spec((8, 128))),
        compiler_params=params(),
        cost_estimate=cost(length * model * 14, length * model * 14),
    )(info, stream, near, far, norm)


def finish_kernel(info, stream, near, far, sent, square, out_ref, square_ref):
    index = pl.program_id(0)

    @pl.when(info[ROLE] == DECODER)
    def _():
        value = stream[...] + (near[...].astype(F32) + far[...].astype(F32))
        value = jnp.where(row_mask(info, index, OWN_LEN), value, 0.0)
        out_ref[...] = value.astype(BF)

        @pl.when(index == 0)
        def _():
            square_ref[...] = jnp.zeros_like(square_ref)

        square_ref[...] += squares_of(value)

    @pl.when(info[ROLE] == ENCODER)
    def _():
        out_ref[...] = sent[...]
        square_ref[...] = square[...]


def finish(info, stream, near, far, sent, square):
    length, model = stream.shape
    return pl.pallas_call(
        finish_kernel,
        grid=(length // TILE,),
        out_shape=(shape((length, model), BF), shape((8, 128), F32)),
        in_specs=[scalars()] + [row_spec(model)] * 4 + [fixed_spec((8, 128))],
        out_specs=(row_spec(model), fixed_spec((8, 128))),
        compiler_params=params(),
        cost_estimate=cost(length * model * 6, length * model * 12),
    )(info, stream, near, far, sent, square)


def norm_back(upstream, values, norm_ref):
    centred = values - jnp.mean(values, -1, keepdims=True)
    factor = lax.rsqrt(jnp.mean(centred * centred, -1, keepdims=True) + EPSILON)
    unit = centred * factor
    scaled = upstream * norm_ref[0:1, :]
    inner = scaled - jnp.mean(scaled, -1, keepdims=True)
    inner = inner - unit * jnp.mean(scaled * unit, -1, keepdims=True)
    gain = jnp.sum(upstream * unit, 0, keepdims=True)
    shift = jnp.sum(upstream, 0, keepdims=True)
    return factor * inner, gain, shift


def norm_back_kernel(residual, near, far, values, norm_ref, grad_ref, low_ref, norm_grad_ref):
    upstream = near[...].astype(F32) + far[...].astype(F32)
    grad, gain, shift = norm_back(upstream, values[...].astype(F32), norm_ref)
    grad = residual[...].astype(F32) + grad
    grad_ref[...] = grad
    low_ref[...] = grad.astype(BF)

    @pl.when(pl.program_id(0) == 0)
    def _():
        norm_grad_ref[...] = jnp.zeros_like(norm_grad_ref)

    norm_grad_ref[0:1, :] += gain
    norm_grad_ref[1:2, :] += shift


def norm_backward(residual, near, far, values, norm):
    length, model = values.shape
    return pl.pallas_call(
        norm_back_kernel,
        grid=(length // TILE,),
        out_shape=(shape((length, model), F32), shape((length, model), BF), shape((2, model), F32)),
        in_specs=[row_spec(model)] * 4 + [fixed_spec((2, model))],
        out_specs=(row_spec(model), row_spec(model), fixed_spec((2, model))),
        compiler_params=params(),
        cost_estimate=cost(length * model * 20, length * model * 18),
    )(residual, near, far, values, norm)


def source_back_kernel(
    info, cot, returned, values, norm_ref, kept, kept_low, kept_norm, grad_ref, low_ref, norm_grad_ref
):
    index = pl.program_id(0)

    @pl.when(info[ROLE] == ENCODER)
    def _():
        upstream = cot[...].astype(F32) + returned[...].astype(F32)
        upstream = jnp.where(row_mask(info, index, OWN_LEN), upstream, 0.0)
        grad, gain, shift = norm_back(upstream, values[...], norm_ref)
        grad_ref[...] = grad
        low_ref[...] = grad.astype(BF)

        @pl.when(index == 0)
        def _():
            norm_grad_ref[...] = jnp.zeros_like(norm_grad_ref)

        norm_grad_ref[0:1, :] += gain
        norm_grad_ref[1:2, :] += shift

    @pl.when(info[ROLE] == DECODER)
    def _():
        grad_ref[...] = kept[...]
        low_ref[...] = kept_low[...]
        norm_grad_ref[...] = kept_norm[...]


def source_back(info, cot, returned, values, norm, kept):
    length, model = values.shape
    return pl.pallas_call(
        source_back_kernel,
        grid=(length // TILE,),
        out_shape=(shape((length, model), F32), shape((length, model), BF), shape((2, model), F32)),
        in_specs=[scalars()]
        + [row_spec(model)] * 3
        + [fixed_spec((2, model)), row_spec(model), row_spec(model), fixed_spec((2, model))],
        out_specs=(row_spec(model), row_spec(model), fixed_spec((2, model))),
        compiler_params=params(),
        cost_estimate=cost(length * model * 20, length * model * 18),
    )(info, cot, returned, values, norm, *kept)


def gelu_parts(hidden):
    half = 0.5 * (1.0 + lax.erf(hidden * math.sqrt(0.5)))
    slope = half + hidden * jnp.exp(-0.5 * hidden * hidden) * (1.0 / math.sqrt(2.0 * math.pi))
    return hidden * half, slope


def feed_forward_kernel(has_sum, info, normed, up, down, *refs):
    previous = refs[0] if has_sum else None
    sum_ref, active_ref, slope_ref = refs[1 if has_sum else 0 :]

    @pl.when(info[ROLE] == ENCODER)
    def _():
        active, slope = gelu_parts(mm(normed[...], up[...], NN))
        active = active.astype(BF)
        active_ref[...] = active
        slope_ref[...] = slope
        value = mm(active, down[...], NN)
        if has_sum:
            value = value + previous[...]
        sum_ref[...] = value.astype(sum_ref.dtype)


def feed_forward(info, normed, up, down, previous):
    length, model = normed.shape
    hidden = up.shape[1]
    has_sum = previous is not None
    operands = [info, normed, up, down] + ([previous] if has_sum else [])
    return pl.pallas_call(
        functools.partial(feed_forward_kernel, has_sum),
        grid=(length // TILE,),
        out_shape=(
            shape((length, model), BF if has_sum else F32),
            shape((length, hidden), BF),
            shape((length, hidden), F32),
        ),
        in_specs=[scalars(), row_spec(model), fixed_spec(up.shape), fixed_spec(down.shape)]
        + ([row_spec(model)] if has_sum else []),
        out_specs=(row_spec(model), row_spec(hidden), row_spec(hidden)),
        compiler_params=params(),
        cost_estimate=cost(4 * length * model * hidden, length * model * 12, length * hidden),
    )(*operands)


def feed_both_kernel(has_sum, info, normed, cot, up, down, passed, *refs):
    before = refs[:2] if has_sum else (None, None)
    sum_ref, back_ref, active_ref, hidden_grad_ref = refs[2 if has_sum else 0 :]

    @pl.when(info[ROLE] == DECODER)
    def _():
        active, slope = gelu_parts(mm(normed[...], up[...], NN))
        active = active.astype(BF)
        active_ref[...] = active
        value = mm(active, down[...], NN)
        grad = (mm(cot[...], down[...], NT) * slope).astype(BF)
        hidden_grad_ref[...] = grad
        back = mm(grad, up[...], NT)
        if has_sum:
            value = value + before[0][...]
            back = back + before[1][...]
        sum_ref[...] = value.astype(sum_ref.dtype)
        back_ref[...] = back.astype(back_ref.dtype)

    @pl.when(info[ROLE] == ENCODER)
    def _():
        active_ref[...] = passed[...]


def feed_both(info, normed, cot, up, down, passed, before):
    length, model = normed.shape
    hidden = up.shape[1]
    has_sum = before is not None
    operands = [info, normed, cot, up, down, passed] + (list(before) if has_sum else [])
    out = shape((length, model), BF if has_sum else F32)
    return pl.pallas_call(
        functools.partial(feed_both_kernel, has_sum),
        grid=(length // TILE,),
        out_shape=(out, out, shape((length, hidden), BF), shape((length, hidden), BF)),
        in_specs=[
            scalars(),
            row_spec(model),
            row_spec(model),
            fixed_spec(up.shape),
            fixed_spec(down.shape),
            row_spec(hidden),
        ]
        + ([row_spec(model)] * 2 if has_sum else []),
        out_specs=(row_spec(model), row_spec(model), row_spec(hidden), row_spec(hidden)),
        compiler_params=params(),
        cost_estimate=cost(8 * length * model * hidden, length * model * 16, length * hidden),
    )(*operands)


def feed_back_kernel(has_sum, info, above, slope, up, down, passed, *refs):
    before, passed_sum = refs[:2] if has_sum else (None, None)
    back_ref, hidden_grad_ref = refs[2 if has_sum else 0 :]

    @pl.when(info[ROLE] == ENCODER)
    def _():
        grad = (mm(above[...], down[...], NT) * slope[...]).astype(BF)
        hidden_grad_ref[...] = grad
        back = mm(grad, up[...], NT)
        if has_sum:
            back = back + before[...]
        back_ref[...] = back.astype(back_ref.dtype)

    @pl.when(info[ROLE] == DECODER)
    def _():
        hidden_grad_ref[...] = passed[...]
        if has_sum:
            back_ref[...] = passed_sum[...]


def feed_back(info, above, slope, up, down, passed, before):
    length, model = above.shape
    hidden = up.shape[1]
    has_sum = before is not None
    operands = [info, above, slope, up, down, passed] + (list(before) if has_sum else [])
    return pl.pallas_call(
        functools.partial(feed_back_kernel, has_sum),
        grid=(length // TILE,),
        out_shape=(shape((length, model), BF if has_sum else F32), shape((length, hidden), BF)),
        in_specs=[
            scalars(),
            row_spec(model),
            row_spec(hidden),
            fixed_spec(up.shape),
            fixed_spec(down.shape),
            row_spec(hidden),
        ]
        + ([row_spec(model)] * 2 if has_sum else []),
        out_specs=(row_spec(model), row_spec(hidden)),
        compiler_params=params(),
        cost_estimate=cost(4 * length * model * hidden, length * model * 12),
    )(*operands)


def across(value):
    return lax.ppermute(value, "tensor", [(0, 2), (1, 3), (2, 0), (3, 1)])


def across_in(value, role):
    links = [(0, 2), (1, 3), (2, 0), (3, 1)]
    return lax.ppermute(
        value, ("section", "tensor"), [(role * 4 + a, role * 4 + b) for a, b in links]
    )


def beside(value):
    return lax.ppermute(value, "tensor", [(0, 1), (1, 0), (2, 3), (3, 2)])


def to_decoder(value):
    return lax.ppermute(value, "section", [(ENCODER, DECODER)])


def to_encoder(value):
    return lax.ppermute(value, "section", [(DECODER, ENCODER)])


def total_over_sequences(value):
    if lax.axis_size("dp") != 4:
        return lax.psum(value, "dp")
    place = lax.axis_index("dp")
    inner = (place == 1) | (place == 2)
    value = value + lax.ppermute(value, "dp", [(0, 1), (3, 2)])
    value = value + lax.ppermute(value, "dp", [(1, 2), (2, 1)])
    return jnp.where(inner, value, lax.ppermute(value, "dp", [(1, 0), (2, 3)]))


def weight_total(own, other):
    value = (own + across(other.astype(BF)).astype(F32)).astype(BF)
    return total_over_sequences(value).astype(F32)


def after(value, done):
    return lax.optimization_barrier((value, done))[0]


def rows_product(left, right):
    return lax.dot_general(left, right, TN, preferred_element_type=F32)


def body(
    frames,
    lengths,
    bucket_of,
    rel_table,
    norms,
    attn_in,
    attn_out,
    cross_pair,
    ffn_in,
    ffn_out,
    cotangent,
):
    section = lax.axis_index("section")
    tensor = lax.axis_index("tensor")
    pair, core = tensor // 2, tensor % 2
    decoder = section == DECODER
    quarter, model = frames.shape[3], frames.shape[4]
    length = 4 * quarter
    half = length // 2
    width = attn_in.shape[3]
    heads = width // HEAD_DIM
    buckets = rel_table.shape[1]

    own_length = lengths[section, pair, 0]
    source_length = lengths[ENCODER, pair, 0]
    starts = [(tensor ^ step) * quarter for step in range(4)]
    info = jnp.stack([section, own_length, source_length, core] + starts).astype(jnp.int32)

    def pick(array, index):
        return lax.dynamic_index_in_dim(array[0, :, 0], index, 0, keepdims=False)

    def quarters(array):
        mine = pick(array, pair)
        far = across(pick(array, 1 - pair))
        both = beside(jnp.stack([mine, far]))
        return mine, both[0], far, both[1]

    frame_pieces = quarters(frames)
    rel_far = across(rel_table[0])
    in_near, out_near, up_near, down_near = attn_in[0], attn_out[0], ffn_in[0], ffn_out[0]
    in_far = across(in_near)
    out_far = across(out_near)
    pair_near = cross_pair[0]
    up_far_e = across_in(up_near, ENCODER)
    down_far_e = across_in(down_near, ENCODER)
    source_near = to_decoder(pair_near)
    pair_far = across_in(pair_near, DECODER)
    source_far = across_in(source_near, DECODER)
    cot_pieces = quarters(cotangent)
    up_far_d = across_in(up_near, DECODER)
    down_far_d = across_in(down_near, DECODER)

    buckets_here = jnp.pad(bucket_of[0], (0, 1), constant_values=-1)
    one_hot = (lax.broadcasted_iota(jnp.int32, (buckets, 2 * length), 0) == buckets_here[None]).astype(F32)
    distances = lax.dot_general(
        jnp.concatenate([rel_table[0], rel_far], 1),
        one_hot,
        TN,
        precision=HIGHEST,
        preferred_element_type=F32,
    )
    table_near = skew(distances[:heads])
    table_far = skew(distances[heads:])

    rows, normed_one = enter(info, frame_pieces, norms[0, 0])
    part, qkv_near, mixed_near, lse_near = self_forward(
        info, normed_one, in_near, out_near, table_near, None
    )
    part, qkv_far, mixed_far, lse_far = self_forward(
        info, normed_one, in_far, out_far, table_far, part
    )
    stream_one, normed_two = add_norm(rows, part, beside(part), norms[0, 1])
    cot = masked_rows(info, cot_pieces)

    part, active_near, slope_near = feed_forward(info, normed_two, up_near, down_near, None)
    part, active_far, slope_far = feed_forward(info, normed_two, up_far_e, down_far_e, part)
    stream_e, sent, squares = source_out(info, stream_one, part, beside(part), norms[0, 2])
    sent_near = to_decoder(lax.dynamic_slice_in_dim(sent, core * half, half, 0))
    sent_far = beside(sent_near)

    part, cross_near, joined_near, cross_lse_near = cross_forward(
        info, normed_two, sent_near, sent_far, pair_near, source_near, None
    )
    part, cross_far, joined_far, cross_lse_far = cross_forward(
        info, normed_two, sent_near, sent_far, pair_far, source_far, part
    )
    stream_d, normed_three = add_norm(stream_one, part, beside(part), norms[0, 2])
    part, back, active_near, grad_near = feed_both(
        info, normed_three, cot, up_near, down_near, active_near, None
    )
    part_d, back, active_far, grad_far = feed_both(
        info, normed_three, cot, up_far_d, down_far_d, active_far, (part, back)
    )
    kept = norm_backward(cot, back, beside(back), stream_d, norms[0, 2])
    above_two = kept[1]
    back, returned, d_cross_near = cross_backward(
        info, cross_near, cross_lse_near, above_two, pair_near, source_near, None
    )
    back, returned, d_cross_far = cross_backward(
        info, cross_far, cross_lse_far, above_two, pair_far, source_far, (back, returned)
    )
    returned_mine = lax.dynamic_slice_in_dim(returned, core * half, half, 0)
    returned_theirs = lax.dynamic_slice_in_dim(returned, (1 - core) * half, half, 0)
    returned = returned_mine.astype(F32) + beside(returned_theirs).astype(F32)
    returned = to_encoder(returned.astype(BF))
    returned_theirs = beside(returned)
    returned = jnp.where(
        core == 0,
        jnp.concatenate([returned, returned_theirs]),
        jnp.concatenate([returned_theirs, returned]),
    )

    grad_two, above_e, norm_grad_three = source_back(
        info, cot, returned, stream_e, norms[0, 2], kept
    )
    back_e, grad_near = feed_back(info, above_e, slope_near, up_near, down_near, grad_near, None)
    back, grad_far = feed_back(
        info, above_e, slope_far, up_far_e, down_far_e, grad_far, (back_e, back)
    )
    grad_one, above_one, norm_grad_two = norm_backward(
        grad_two, back, beside(back), stream_one, norms[0, 1]
    )

    normed_feed = jnp.where(decoder, normed_three, normed_two)
    above_feed = jnp.where(decoder, cot, above_e)
    d_ffn_out = weight_total(
        rows_product(active_near, above_feed), rows_product(active_far, above_feed)
    )
    d_ffn_in = weight_total(
        rows_product(normed_feed, grad_near), rows_product(normed_feed, grad_far)
    )

    back, d_qkv_near, spread_near = self_backward(
        info, qkv_near, lse_near, above_one, in_near, out_near, table_near, None
    )
    back, d_qkv_far, spread_far = self_backward(
        info, qkv_far, lse_far, above_one, in_far, out_far, table_far, back
    )
    grad_rows, _, norm_grad_one = norm_backward(grad_one, back, beside(back), rows, norms[0, 0])

    def input_grads(normed, grads):
        return jnp.stack([rows_product(normed, grads[place]) for place in range(3)])

    d_attn_out = weight_total(
        rows_product(mixed_near, above_one), rows_product(mixed_far, above_one)
    )
    d_attn_in = weight_total(
        input_grads(normed_one, d_qkv_near), input_grads(normed_one, d_qkv_far)
    )

    sent_all = jnp.where(
        core == 0,
        jnp.concatenate([sent_near, sent_far]),
        jnp.concatenate([sent_far, sent_near]),
    )

    def cross_grads(grads, joined):
        return jnp.stack(
            [
                rows_product(sent_all, grads[1]),
                rows_product(sent_all, grads[2]),
                rows_product(normed_two, grads[0]),
                rows_product(above_two, joined),
            ]
        )

    d_far = across_in(cross_grads(d_cross_far, joined_far).astype(BF), DECODER)
    d_pair = (cross_grads(d_cross_near, joined_near) + d_far.astype(F32)).astype(BF)
    d_source = to_encoder(d_pair[:2])
    d_pair = jnp.where(decoder, d_pair[2:], d_source)
    d_pair = total_over_sequences(d_pair).astype(F32)

    result, squares = finish(info, stream_d, part_d, beside(part_d), sent, squares)

    def placed(value):
        mine = lax.dynamic_slice_in_dim(value, tensor * quarter, quarter, 0)
        theirs = lax.dynamic_slice_in_dim(value, (tensor ^ 2) * quarter, quarter, 0)
        other = across(theirs.astype(BF)).astype(value.dtype)
        stacked = jnp.where(pair == 0, jnp.stack([mine, other]), jnp.stack([other, mine]))
        return stacked[None, :, None]

    spreads = jnp.concatenate([spread_near, spread_far])
    d_table = lax.dot_general(
        one_hot, spreads, NT, precision=HIGHEST, preferred_element_type=F32
    )
    small = jnp.concatenate(
        [
            norm_grad_one,
            norm_grad_two,
            norm_grad_three,
            jnp.broadcast_to(squares[:1, :1], (1, model)),
            jnp.broadcast_to(own_length.astype(F32), (1, model)),
        ]
    )
    small = total_over_sequences(small + across(small))
    d_table = total_over_sequences(d_table[:, :heads] + across(d_table[:, heads:]))
    stats = jnp.sqrt(small[6, :1] / (small[7, :1] * model))
    return (
        placed(result),
        placed(grad_rows),
        d_table[None],
        small[:6].reshape(1, 3, 2, model),
        d_attn_in[None],
        d_attn_out[None],
        d_pair[None],
        d_ffn_in[None],
        d_ffn_out[None],
        stats,
    )


def solution(mesh):
    in_specs = (
        P("section", None, "dp", "tensor", None),
        P(None, None, "dp"),
        P("section", None),
        P("section", None, "tensor"),
        P("section", None, None, None),
        P("section", None, None, "tensor"),
        P("section", "tensor", None),
        P("section", None, None, "tensor"),
        P("section", None, "tensor"),
        P("section", "tensor", None),
        P("section", None, "dp", "tensor", None),
    )
    out_specs = (
        P("section", None, "dp", "tensor", None),
        P("section", None, "dp", "tensor", None),
        P("section", None, "tensor"),
        P("section", None, None, None),
        P("section", None, None, "tensor"),
        P("section", "tensor", None),
        P("section", None, None, "tensor"),
        P("section", None, "tensor"),
        P("section", "tensor", None),
        P("section"),
    )
    return jax.shard_map(body, mesh=mesh, in_specs=in_specs, out_specs=out_specs, check_vma=False)
```

```python
import functools
import math

import jax
import jax.numpy as jnp
from jax import lax
from jax.experimental import pallas as pl
from jax.experimental.pallas import tpu as pltpu
from jax.sharding import PartitionSpec as P

HEAD_DIM = 64
SCALE = HEAD_DIM ** (-0.5)
EPSILON = 1e-05
MASKED = -1000000000.0
HIGHEST = lax.Precision.HIGHEST
BF = jnp.bfloat16
F32 = jnp.float32
NN = (((1,), (0,)), ((), ()))
NT = (((1,), (1,)), ((), ()))
TN = (((0,), (0,)), ((), ()))
TILE = 256
QUERIES = 512
BAND = 128
ENCODER, DECODER = 0, 1
ROLE, OWN_LEN, SOURCE_LEN, CORE, START = 0, 1, 2, 3, 4
HIDES_LITTLE = 0.02
HIDES_MUCH = 2.0


def mm(left, right, dims):
    return lax.dot_general(left, right, dims, preferred_element_type=F32)


def whole():
    return pl.BlockSpec(memory_space=pltpu.VMEM)


def scalars():
    return pl.BlockSpec(memory_space=pltpu.SMEM)


def shape(dims, dtype):
    return jax.ShapeDtypeStruct(dims, dtype)


def cost(flops, nbytes, weight=HIDES_LITTLE):
    return pl.CostEstimate(
        flops=int(flops * weight), bytes_accessed=int(nbytes * weight), transcendentals=0
    )


def params(megabytes=28):
    return pltpu.CompilerParams(vmem_limit_bytes=megabytes * 1024 * 1024)


def norm_of(values, norm_ref):
    centred = values - jnp.mean(values, -1, keepdims=True)
    factor = lax.rsqrt(jnp.mean(centred * centred, -1, keepdims=True) + EPSILON)
    return centred * factor * norm_ref[0:1, :] + norm_ref[1:2, :]


def enter_kernel(info, mine, core_mine, far, core_far, norm_ref, rows_ref, normed_ref):
    quarter = mine.shape[0]
    for step, piece in enumerate((mine, core_mine, far, core_far)):
        start = pl.multiple_of(info[START + step], quarter)
        values = piece[...]
        rows_ref[pl.ds(start, quarter), :] = values
        normed_ref[pl.ds(start, quarter), :] = norm_of(values.astype(F32), norm_ref).astype(BF)


def enter(info, pieces, norm):
    quarter, width = pieces[0].shape
    out = shape((4 * quarter, width), BF)
    return pl.pallas_call(
        enter_kernel,
        out_shape=(out, out),
        in_specs=[scalars()] + [whole()] * 5,
        out_specs=(whole(), whole()),
        compiler_params=params(),
        cost_estimate=cost(16 * quarter * width * 4, quarter * width * 24),
    )(info, *pieces, norm)


def masked_kernel(info, mine, core_mine, far, core_far, rows_ref):
    quarter = mine.shape[0]
    for step, piece in enumerate((mine, core_mine, far, core_far)):
        start = pl.multiple_of(info[START + step], quarter)
        row = start + lax.broadcasted_iota(jnp.int32, (quarter, 1), 0)
        values = jnp.where(row < info[OWN_LEN], piece[...].astype(F32), 0.0)
        rows_ref[pl.ds(start, quarter), :] = values.astype(BF)


def masked_rows(info, pieces):
    quarter, width = pieces[0].shape
    return pl.pallas_call(
        masked_kernel,
        out_shape=shape((4 * quarter, width), BF),
        in_specs=[scalars()] + [whole()] * 4,
        out_specs=whole(),
        compiler_params=params(),
        cost_estimate=cost(quarter * width * 8, quarter * width * 16),
    )(info, *pieces)


def skew_kernel(distance_ref, table_ref):
    width = table_ref.shape[2]
    for head in range(distance_ref.shape[0]):
        row = jnp.broadcast_to(distance_ref[head : head + 1, :], (BAND, width))
        table_ref[head] = pltpu.roll(row, width - (BAND - 1), 1, stride=1, stride_axis=0)


def skew(distances):
    heads, width = distances.shape
    return pl.pallas_call(
        skew_kernel,
        out_shape=shape((heads, BAND, width), F32),
        in_specs=[whole()],
        out_specs=whole(),
        compiler_params=params(),
        cost_estimate=cost(heads * BAND * width, heads * BAND * width * 4),
    )(distances)


def unskewed(band):
    width = band.shape[1]
    amount = (BAND - 1) - lax.broadcasted_iota(jnp.int32, (BAND, width), 0)
    for bit in range(7):
        band = jnp.where(((amount >> bit) & 1) == 1, pltpu.roll(band, 1 << bit, 1), band)
    return jnp.sum(band, 0, keepdims=True)


def by_blocks(count, body):
    def step(index, carry):
        body(pl.ds(pl.multiple_of(index * TILE, TILE), TILE))
        return carry

    lax.fori_loop(0, count // TILE, step, 0)


def head_span(head):
    return slice(head * HEAD_DIM, (head + 1) * HEAD_DIM)


def allowed_keys(info, start, length, causal, length_at):
    key = lax.broadcasted_iota(jnp.int32, (length, QUERIES), 0)
    last = info[length_at] - 1
    if not causal:
        return key <= last
    query = start + lax.broadcasted_iota(jnp.int32, (1, QUERIES), 1)
    free = jnp.where(info[ROLE] == DECODER, 0, 1 << 20)
    return key <= jnp.minimum(query + free, last)


def bias_block(table_ref, head, start, length):
    blocks = []
    for band in range(length // BAND):
        offset = pl.multiple_of(length - BAND - band * BAND + start, BAND)
        blocks.append(table_ref[head, :, pl.ds(offset, QUERIES)])
    return jnp.concatenate(blocks, 0)


def upright(source, place, target):
    def step(cols):
        block = source[place, :, cols].astype(F32).T
        for head in range(target.shape[0]):
            target[head, cols, :] = block[:, head_span(head)].astype(BF)

    by_blocks(source.shape[2], step)


def attend_loop(info, qkv_ref, keys_ref, table_ref, out_ref, lse_ref, length_at):
    width, length = out_ref.shape
    causal = table_ref is not None

    def block(index, carry):
        start = pl.multiple_of(index * QUERIES, QUERIES)
        cols = pl.ds(start, QUERIES)
        allowed = allowed_keys(info, start, length, causal, length_at)
        for head in range(width // HEAD_DIM):
            span = head_span(head)
            queries = qkv_ref[0, span, cols] * jnp.asarray(SCALE, BF)
            scores = mm(keys_ref[head], queries, NN)
            if causal:
                scores = scores + bias_block(table_ref, head, start, length)
            scores = jnp.where(allowed, scores, MASKED)
            peak = jnp.max(scores, 0, keepdims=True)
            lifted = jnp.exp(scores - peak)
            total = jnp.sum(lifted, 0, keepdims=True)
            mixed = mm(qkv_ref[2, span, :], lifted.astype(BF), NN)
            out_ref[span, cols] = mixed / total
            lse_ref[head : head + 1, cols] = peak + jnp.log(total)
        return carry

    lax.fori_loop(0, length // QUERIES, block, 0)


def self_forward_kernel(has_sum, info, normed, weights, table, *refs):
    previous = refs[0] if has_sum else None
    sum_ref, qkv_ref, out_ref, lse_ref, keys = refs[1 if has_sum else 0 :]
    length = out_ref.shape[1]

    def inputs(cols):
        block = normed[cols, :]
        for place in range(3):
            qkv_ref[place, :, cols] = mm(weights[place], block, NT).astype(BF)

    by_blocks(length, inputs)
    upright(qkv_ref, 1, keys)
    attend_loop(info, qkv_ref, keys, table, out_ref, lse_ref, OWN_LEN)

    def outputs(cols):
        value = mm(out_ref[:, cols].astype(BF), weights[3], TN)
        if has_sum:
            value = value + previous[cols, :]
        sum_ref[cols, :] = value.astype(sum_ref.dtype)

    by_blocks(length, outputs)


def attention_cost(length, width, model, matmuls, projections, weight=HIDES_LITTLE):
    heads = width // HEAD_DIM
    return cost(
        heads * length * length * HEAD_DIM * 2 * matmuls * 4 + projections * 2 * length * model * width,
        length * model * 8,
        weight,
    )


def saved_shapes(length, width):
    return (shape((3, width, length), BF), shape((width, length), F32), shape((8, length), F32))


def self_forward(info, normed, weights, table, previous):
    length, model = normed.shape
    width = weights.shape[1]
    has_sum = previous is not None
    operands = [info, normed, weights, table] + ([previous] if has_sum else [])
    return pl.pallas_call(
        functools.partial(self_forward_kernel, has_sum),
        out_shape=(shape((length, model), BF if has_sum else F32),) + saved_shapes(length, width),
        in_specs=[scalars()] + [whole()] * (len(operands) - 1),
        out_specs=(whole(),) * 4,
        scratch_shapes=[pltpu.VMEM((width // HEAD_DIM, length, HEAD_DIM), BF)],
        compiler_params=params(),
        cost_estimate=attention_cost(length, width, model, 2, 4, HIDES_MUCH),
    )(*operands)


def cross_forward_kernel(info, normed, near, far, weights_near, weights_far, *refs):
    sum_ref, keys = refs[0], refs[7]
    length = normed.shape[0]
    half = near.shape[0]
    sides = ((weights_near, refs[1:4]), (weights_far, refs[4:7]))

    @pl.when(info[ROLE] == DECODER)
    def _():
        for weights, (qkv_ref, out_ref, lse_ref) in sides:

            def queries(cols, weights=weights, qkv_ref=qkv_ref):
                qkv_ref[0, :, cols] = mm(weights[0], normed[cols, :], NT).astype(BF)

            by_blocks(length, queries)
            for piece, side in ((near, info[CORE]), (far, 1 - info[CORE])):
                base = side * half

                def sources(index, carry, piece=piece, base=base, weights=weights, qkv_ref=qkv_ref):
                    local = pl.multiple_of(index * TILE, TILE)
                    block = piece[pl.ds(local, TILE), :]
                    cols = pl.ds(pl.multiple_of(base + local, TILE), TILE)
                    for place in (1, 2):
                        qkv_ref[place, :, cols] = mm(weights[1 + place], block, NT).astype(BF)
                    return carry

                lax.fori_loop(0, half // TILE, sources, 0)
            upright(qkv_ref, 1, keys)
            attend_loop(info, qkv_ref, keys, None, out_ref, lse_ref, SOURCE_LEN)

        def outputs(cols):
            value = mm(refs[2][:, cols].astype(BF), weights_near[1], TN)
            value = value + mm(refs[5][:, cols].astype(BF), weights_far[1], TN)
            sum_ref[cols, :] = value.astype(sum_ref.dtype)

        by_blocks(length, outputs)


def cross_forward(info, normed, near, far, weights_near, weights_far):
    length, model = normed.shape
    width = weights_near.shape[1]
    saved = saved_shapes(length, width)
    results = pl.pallas_call(
        cross_forward_kernel,
        out_shape=(shape((length, model), BF),) + saved + saved,
        in_specs=[scalars()] + [whole()] * 5,
        out_specs=(whole(),) * 7,
        scratch_shapes=[pltpu.VMEM((width // HEAD_DIM, length, HEAD_DIM), BF)],
        compiler_params=params(),
        cost_estimate=attention_cost(length, 2 * width, model, 2, 4),
    )(info, normed, near, far, weights_near, weights_far)
    return results[0], results[1:4], results[4:7]


def attend_back_loop(
    info, saved, table_ref, upstream, grads_ref, upright_refs, key_sum, value_sum, band, length_at
):
    qkv_ref, out_ref, lse_ref = saved
    width, length = out_ref.shape
    causal = table_ref is not None
    keys_up, values_up, queries_up, above_up = upright_refs
    upright(qkv_ref, 1, keys_up)
    upright(qkv_ref, 2, values_up)
    upright(qkv_ref, 0, queries_up)
    upright(upstream, 0, above_up)
    key_sum[...] = jnp.zeros_like(key_sum)
    value_sum[...] = jnp.zeros_like(value_sum)
    if causal:
        band[...] = jnp.zeros_like(band)

    def block(index, carry):
        start = pl.multiple_of(index * QUERIES, QUERIES)
        cols = pl.ds(start, QUERIES)
        allowed = allowed_keys(info, start, length, causal, length_at)
        for head in range(width // HEAD_DIM):
            span = head_span(head)
            queries = qkv_ref[0, span, cols] * jnp.asarray(SCALE, BF)
            scores = mm(keys_up[head], queries, NN)
            if causal:
                scores = scores + bias_block(table_ref, head, start, length)
            scores = jnp.where(allowed, scores, MASKED)
            probs = jnp.exp(scores - lse_ref[head : head + 1, cols])
            above = upstream[0, span, cols]
            d_probs = mm(values_up[head], above, NN)
            inner = above.astype(F32) * out_ref[span, cols]
            inner = jnp.sum(inner, 0, keepdims=True)
            d_scores = probs * (d_probs - inner)
            low = d_scores.astype(BF)
            grads_ref[0, span, cols] = (mm(qkv_ref[1, span, :], low, NN) * SCALE).astype(BF)
            key_sum[head] += mm(low, queries_up[head, cols, :], NN)
            value_sum[head] += mm(probs.astype(BF), above_up[head, cols, :], NN)
            if causal:
                for part in range(length // BAND):
                    offset = pl.multiple_of(length - BAND - part * BAND + start, BAND)
                    place = pl.ds(offset, QUERIES)
                    band[head, :, place] += d_scores[part * BAND : (part + 1) * BAND, :]
        return carry

    lax.fori_loop(0, length // QUERIES, block, 0)
    for head in range(width // HEAD_DIM):
        span = head_span(head)
        grads_ref[1, span, :] = (key_sum[head] * SCALE).T.astype(BF)
        grads_ref[2, span, :] = value_sum[head].T.astype(BF)


def back_scratch(length, width):
    heads = width // HEAD_DIM
    return [
        pltpu.VMEM((1, width, length), BF),
        *[pltpu.VMEM((heads, length, HEAD_DIM), BF) for _ in range(4)],
        pltpu.VMEM((heads, length, HEAD_DIM), F32),
        pltpu.VMEM((heads, length, HEAD_DIM), F32),
    ]


def self_backward_kernel(has_sum, info, qkv, out, lse, above, normed, weights, table, *refs):
    previous = refs[0] if has_sum else None
    refs = refs[1 if has_sum else 0 :]
    sum_ref, weight_ref, spread_ref, upstream = refs[:4]
    upright_refs, key_sum, value_sum, band, grads_ref = refs[4:8], refs[8], refs[9], refs[10], refs[11]
    length = above.shape[0]

    def entering(cols):
        upstream[0, :, cols] = mm(weights[3], above[cols, :], NT).astype(BF)

    by_blocks(length, entering)
    attend_back_loop(
        info,
        (qkv, out, lse),
        table,
        upstream,
        grads_ref,
        upright_refs,
        key_sum,
        value_sum,
        band,
        OWN_LEN,
    )

    def leaving(cols):
        value = mm(grads_ref[0, :, cols], weights[0], TN)
        for place in (1, 2):
            value = value + mm(grads_ref[place, :, cols], weights[place], TN)
        if has_sum:
            value = value + previous[cols, :]
        sum_ref[cols, :] = value.astype(sum_ref.dtype)

    by_blocks(length, leaving)
    for place in range(3):
        weight_ref[place] = mm(grads_ref[place], normed[...], NN).astype(weight_ref.dtype)
    weight_ref[3] = mm(out[...].astype(BF), above[...], NN).astype(weight_ref.dtype)
    for head in range(table.shape[0]):
        spread_ref[head : head + 1, :] = unskewed(band[head])


def self_backward(info, saved, above, normed, weights, table, previous, weight_type):
    length, model = above.shape
    width = weights.shape[1]
    has_sum = previous is not None
    operands = [info, *saved, above, normed, weights, table] + ([previous] if has_sum else [])
    return pl.pallas_call(
        functools.partial(self_backward_kernel, has_sum),
        out_shape=(
            shape((length, model), BF if has_sum else F32),
            shape((4, width, model), weight_type),
            shape((table.shape[0], table.shape[2]), F32),
        ),
        in_specs=[scalars()] + [whole()] * (len(operands) - 1),
        out_specs=(whole(),) * 3,
        scratch_shapes=back_scratch(length, width)
        + [pltpu.VMEM(table.shape, F32), pltpu.VMEM((3, width, length), BF)],
        compiler_params=params(),
        cost_estimate=attention_cost(length, width, model, 5, 8),
    )(*operands)


def cross_backward_kernel(info, *refs):
    saved_near, saved_far, (above, weights_near, weights_far) = refs[:3], refs[3:6], refs[6:9]
    sum_ref, source_ref, grads_near, grads_far, upstream = refs[9:14]
    upright_refs, key_sum, value_sum = refs[14:18], refs[18], refs[19]
    length = above.shape[0]

    @pl.when(info[ROLE] == DECODER)
    def _():
        for saved, weights, grads_ref in (
            (saved_near, weights_near, grads_near),
            (saved_far, weights_far, grads_far),
        ):

            def entering(cols, weights=weights):
                upstream[0, :, cols] = mm(weights[1], above[cols, :], NT).astype(BF)

            by_blocks(length, entering)
            attend_back_loop(
                info,
                saved,
                None,
                upstream,
                grads_ref,
                upright_refs,
                key_sum,
                value_sum,
                None,
                SOURCE_LEN,
            )

        def leaving(cols):
            value = mm(grads_near[0, :, cols], weights_near[0], TN)
            value = value + mm(grads_far[0, :, cols], weights_far[0], TN)
            sum_ref[cols, :] = value.astype(BF)
            source = None
            for grads_ref, weights in ((grads_near, weights_near), (grads_far, weights_far)):
                for place in (1, 2):
                    term = mm(grads_ref[place, :, cols], weights[1 + place], TN)
                    source = term if source is None else source + term
            source_ref[cols, :] = source.astype(BF)

        by_blocks(length, leaving)


def cross_backward(info, saved_near, saved_far, above, weights_near, weights_far):
    length, model = above.shape
    width = weights_near.shape[1]
    out, grads = shape((length, model), BF), shape((3, width, length), BF)
    return pl.pallas_call(
        cross_backward_kernel,
        out_shape=(out, out, grads, grads),
        in_specs=[scalars()] + [whole()] * 9,
        out_specs=(whole(),) * 4,
        scratch_shapes=back_scratch(length, width),
        compiler_params=params(),
        cost_estimate=attention_cost(length, 2 * width, model, 5, 4),
    )(info, *saved_near, *saved_far, above, weights_near, weights_far)


def cross_weights_kernel(info, grads_near, grads_far, out_near, out_far, normed, above, *refs):
    near, far, weight_near, weight_far = refs
    half = near.shape[0]

    @pl.when(info[ROLE] == DECODER)
    def _():
        start = pl.multiple_of(info[CORE] * half, half)
        other = pl.multiple_of((1 - info[CORE]) * half, half)
        for grads, out, target in (
            (grads_near, out_near, weight_near),
            (grads_far, out_far, weight_far),
        ):
            target[0] = mm(grads[0], normed[...], NN).astype(target.dtype)
            target[1] = mm(out[...].astype(BF), above[...], NN).astype(target.dtype)
            for place in (1, 2):
                value = mm(grads[place, :, pl.ds(start, half)], near[...], NN)
                value = value + mm(grads[place, :, pl.ds(other, half)], far[...], NN)
                target[1 + place] = value.astype(target.dtype)


def cross_weights(info, grads_near, grads_far, out_near, out_far, normed, above, near, far):
    length, model = above.shape
    width = out_near.shape[0]
    return pl.pallas_call(
        cross_weights_kernel,
        out_shape=(shape((4, width, model), F32), shape((4, width, model), BF)),
        in_specs=[scalars()] + [whole()] * 8,
        out_specs=(whole(),) * 2,
        compiler_params=params(),
        cost_estimate=cost(16 * length * model * width, length * model * 16),
    )(info, grads_near, grads_far, out_near, out_far, normed, above, near, far)


def row_spec(width):
    return pl.BlockSpec((TILE, width), lambda index: (index, 0))


def fixed_spec(dims):
    return pl.BlockSpec(dims, lambda index: (0,) * len(dims))


def add_norm_kernel(stream, near, far, norm_ref, sum_ref, normed_ref):
    value = stream[...].astype(F32) + (near[...].astype(F32) + far[...].astype(F32))
    sum_ref[...] = value
    normed_ref[...] = norm_of(value, norm_ref).astype(BF)


def add_norm(stream, near, far, norm):
    length, model = stream.shape
    return pl.pallas_call(
        add_norm_kernel,
        grid=(length // TILE,),
        out_shape=(shape((length, model), F32), shape((length, model), BF)),
        in_specs=[row_spec(model)] * 3 + [fixed_spec((2, model))],
        out_specs=(row_spec(model),) * 2,
        compiler_params=params(),
        cost_estimate=cost(length * model * 12, length * model * 14),
    )(stream, near, far, norm)


def row_mask(info, index, at):
    row = index * TILE + lax.broadcasted_iota(jnp.int32, (TILE, 1), 0)
    return row < info[at]


def squares_of(value):
    return jnp.sum(jnp.sum(value * value, 0, keepdims=True), 1, keepdims=True)


def source_kernel(info, stream, near, far, norm_ref, sum_ref, sent_ref, square_ref):
    index = pl.program_id(0)
    value = stream[...] + (near[...].astype(F32) + far[...].astype(F32))
    sum_ref[...] = value
    result = jnp.where(row_mask(info, index, OWN_LEN), norm_of(value, norm_ref), 0.0)
    sent_ref[...] = result.astype(BF)

    @pl.when(index == 0)
    def _():
        square_ref[...] = jnp.zeros_like(square_ref)

    square_ref[...] += squares_of(result)


def source_out(info, stream, near, far, norm):
    length, model = stream.shape
    return pl.pallas_call(
        source_kernel,
        grid=(length // TILE,),
        out_shape=(shape((length, model), F32), shape((length, model), BF), shape((8, 128), F32)),
        in_specs=[scalars()] + [row_spec(model)] * 3 + [fixed_spec((2, model))],
        out_specs=(row_spec(model), row_spec(model), fixed_spec((8, 128))),
        compiler_params=params(),
        cost_estimate=cost(length * model * 14, length * model * 14),
    )(info, stream, near, far, norm)


def finish_kernel(info, stream, near, far, sent, square, out_ref, square_ref):
    index = pl.program_id(0)

    @pl.when(info[ROLE] == DECODER)
    def _():
        value = stream[...] + (near[...].astype(F32) + far[...].astype(F32))
        value = jnp.where(row_mask(info, index, OWN_LEN), value, 0.0)
        out_ref[...] = value.astype(BF)

        @pl.when(index == 0)
        def _():
            square_ref[...] = jnp.zeros_like(square_ref)

        square_ref[...] += squares_of(value)

    @pl.when(info[ROLE] == ENCODER)
    def _():
        out_ref[...] = sent[...]
        square_ref[...] = square[...]


def finish(info, stream, near, far, sent, square):
    length, model = stream.shape
    return pl.pallas_call(
        finish_kernel,
        grid=(length // TILE,),
        out_shape=(shape((length, model), BF), shape((8, 128), F32)),
        in_specs=[scalars()] + [row_spec(model)] * 4 + [fixed_spec((8, 128))],
        out_specs=(row_spec(model), fixed_spec((8, 128))),
        compiler_params=params(),
        cost_estimate=cost(length * model * 6, length * model * 12),
    )(info, stream, near, far, sent, square)


def norm_back(upstream, values, norm_ref):
    centred = values - jnp.mean(values, -1, keepdims=True)
    factor = lax.rsqrt(jnp.mean(centred * centred, -1, keepdims=True) + EPSILON)
    unit = centred * factor
    scaled = upstream * norm_ref[0:1, :]
    inner = scaled - jnp.mean(scaled, -1, keepdims=True)
    inner = inner - unit * jnp.mean(scaled * unit, -1, keepdims=True)
    gain = jnp.sum(upstream * unit, 0, keepdims=True)
    shift = jnp.sum(upstream, 0, keepdims=True)
    return factor * inner, gain, shift


def norm_back_kernel(residual, near, far, values, norm_ref, grad_ref, low_ref, norm_grad_ref):
    upstream = near[...].astype(F32) + far[...].astype(F32)
    grad, gain, shift = norm_back(upstream, values[...].astype(F32), norm_ref)
    grad = residual[...].astype(F32) + grad
    grad_ref[...] = grad
    low_ref[...] = grad.astype(BF)

    @pl.when(pl.program_id(0) == 0)
    def _():
        norm_grad_ref[...] = jnp.zeros_like(norm_grad_ref)

    norm_grad_ref[0:1, :] += gain
    norm_grad_ref[1:2, :] += shift


def norm_backward(residual, near, far, values, norm):
    length, model = values.shape
    return pl.pallas_call(
        norm_back_kernel,
        grid=(length // TILE,),
        out_shape=(shape((length, model), F32), shape((length, model), BF), shape((2, model), F32)),
        in_specs=[row_spec(model)] * 4 + [fixed_spec((2, model))],
        out_specs=(row_spec(model), row_spec(model), fixed_spec((2, model))),
        compiler_params=params(),
        cost_estimate=cost(length * model * 20, length * model * 18),
    )(residual, near, far, values, norm)


def source_back_kernel(
    info, cot, near, far, values, norm_ref, grad_ref, low_ref, norm_grad_ref
):
    index = pl.program_id(0)
    blocks = near.shape[0] // TILE
    rows = pl.ds(pl.multiple_of(lax.rem(index, blocks) * TILE, TILE), TILE)
    mine = (index >= blocks).astype(jnp.int32) == info[CORE]
    returned = jnp.where(mine, near[rows, :].astype(F32), far[rows, :].astype(F32))
    upstream = cot[...].astype(F32) + returned
    upstream = jnp.where(row_mask(info, index, OWN_LEN), upstream, 0.0)
    grad, gain, shift = norm_back(upstream, values[...], norm_ref)
    grad_ref[...] = grad
    low_ref[...] = grad.astype(BF)

    @pl.when(index == 0)
    def _():
        norm_grad_ref[...] = jnp.zeros_like(norm_grad_ref)

    norm_grad_ref[0:1, :] += gain
    norm_grad_ref[1:2, :] += shift


def source_back(info, cot, near, far, values, norm):
    length, model = values.shape
    return pl.pallas_call(
        source_back_kernel,
        grid=(length // TILE,),
        out_shape=(shape((length, model), F32), shape((length, model), BF), shape((2, model), F32)),
        in_specs=[scalars(), row_spec(model), fixed_spec(near.shape), fixed_spec(far.shape)]
        + [row_spec(model), fixed_spec((2, model))],
        out_specs=(row_spec(model), row_spec(model), fixed_spec((2, model))),
        compiler_params=params(),
        cost_estimate=cost(length * model * 20, length * model * 18),
    )(info, cot, near, far, values, norm)


def gelu_parts(hidden):
    half = 0.5 * (1.0 + lax.erf(hidden * math.sqrt(0.5)))
    slope = half + hidden * jnp.exp(-0.5 * hidden * hidden) * (1.0 / math.sqrt(2.0 * math.pi))
    return hidden * half, slope


def feed_forward_kernel(has_sum, info, normed, pack, *refs):
    previous = refs[0] if has_sum else None
    sum_ref, active_ref, slope_ref = refs[1 if has_sum else 0 :]

    @pl.when(info[ROLE] == ENCODER)
    def _():
        active, slope = gelu_parts(mm(normed[...], pack[0], NN))
        active = active.astype(BF)
        active_ref[...] = active
        slope_ref[...] = slope
        value = mm(active, pack[1], NN)
        if has_sum:
            value = value + previous[...]
        sum_ref[...] = value.astype(sum_ref.dtype)


def feed_forward(info, normed, pack, previous):
    length, model = normed.shape
    hidden = pack.shape[2]
    has_sum = previous is not None
    operands = [info, normed, pack] + ([previous] if has_sum else [])
    return pl.pallas_call(
        functools.partial(feed_forward_kernel, has_sum),
        grid=(length // TILE,),
        out_shape=(
            shape((length, model), BF if has_sum else F32),
            shape((length, hidden), BF),
            shape((length, hidden), F32),
        ),
        in_specs=[scalars(), row_spec(model), fixed_spec(pack.shape)]
        + ([row_spec(model)] if has_sum else []),
        out_specs=(row_spec(model), row_spec(hidden), row_spec(hidden)),
        compiler_params=params(),
        cost_estimate=cost(4 * length * model * hidden, length * model * 12),
    )(*operands)


def feed_both_kernel(info, normed, cot, pack_near, pack_far, *refs):
    sum_ref, back_ref = refs[:2]

    @pl.when(info[ROLE] == DECODER)
    def _():
        value, back = None, None
        for pack, active_ref, grad_ref in ((pack_near, *refs[2:4]), (pack_far, *refs[4:6])):
            active, slope = gelu_parts(mm(normed[...], pack[0], NN))
            active = active.astype(BF)
            active_ref[...] = active
            term = mm(active, pack[1], NN)
            value = term if value is None else value + term
            grad = (mm(cot[...], pack[1], NT) * slope).astype(BF)
            grad_ref[...] = grad
            term = mm(grad, pack[0], NT)
            back = term if back is None else back + term
        sum_ref[...] = value.astype(BF)
        back_ref[...] = back.astype(BF)


def feed_both(info, normed, cot, pack_near, pack_far):
    length, model = normed.shape
    hidden = pack_near.shape[2]
    out, unit = shape((length, model), BF), shape((length, hidden), BF)
    return pl.pallas_call(
        feed_both_kernel,
        grid=(length // TILE,),
        out_shape=(out, out, unit, unit, unit, unit),
        in_specs=[
            scalars(),
            row_spec(model),
            row_spec(model),
            fixed_spec(pack_near.shape),
            fixed_spec(pack_far.shape),
        ],
        out_specs=(row_spec(model),) * 2 + (row_spec(hidden),) * 4,
        compiler_params=params(),
        cost_estimate=cost(16 * length * model * hidden, length * model * 20),
    )(info, normed, cot, pack_near, pack_far)


def feed_back_kernel(above, slope_near, slope_far, pack_near, pack_far, back_ref, *grad_refs):
    back = None
    for pack, slope, grad_ref in (
        (pack_near, slope_near, grad_refs[0]),
        (pack_far, slope_far, grad_refs[1]),
    ):
        grad = (mm(above[...], pack[1], NT) * slope[...]).astype(BF)
        grad_ref[...] = grad
        term = mm(grad, pack[0], NT)
        back = term if back is None else back + term
    back_ref[...] = back.astype(BF)


def feed_back(above, slope_near, slope_far, pack_near, pack_far):
    length, model = above.shape
    hidden = pack_near.shape[2]
    unit = shape((length, hidden), BF)
    return pl.pallas_call(
        feed_back_kernel,
        grid=(length // TILE,),
        out_shape=(shape((length, model), BF), unit, unit),
        in_specs=[
            row_spec(model),
            row_spec(hidden),
            row_spec(hidden),
            fixed_spec(pack_near.shape),
            fixed_spec(pack_far.shape),
        ],
        out_specs=(row_spec(model), row_spec(hidden), row_spec(hidden)),
        compiler_params=params(),
        cost_estimate=cost(8 * length * model * hidden, length * model * 16),
    )(above, slope_near, slope_far, pack_near, pack_far)


def product_kernel(left_near, left_far, right_near, right_far, near_ref, far_ref):
    near_ref[...] = mm(left_near[...], right_near[...], TN)
    far_ref[...] = mm(left_far[...], right_far[...], TN).astype(BF)


def feed_weights(left_near, left_far, right_near, right_far):
    length, rows = left_near.shape
    columns = right_near.shape[1]
    left = pl.BlockSpec((length, TILE), lambda index: (0, index))
    right = pl.BlockSpec((length, columns), lambda index: (0, 0))
    out = row_spec(columns)
    return pl.pallas_call(
        product_kernel,
        grid=(rows // TILE,),
        out_shape=(shape((rows, columns), F32), shape((rows, columns), BF)),
        in_specs=[left, left, right, right],
        out_specs=(out, out),
        compiler_params=params(),
        cost_estimate=cost(4 * length * rows * columns, length * rows * 12),
    )(left_near, left_far, right_near, right_far)


def across(value):
    return lax.ppermute(value, "tensor", [(0, 2), (1, 3), (2, 0), (3, 1)])


def across_in(value, role):
    links = [(0, 2), (1, 3), (2, 0), (3, 1)]
    return lax.ppermute(
        value, ("section", "tensor"), [(role * 4 + a, role * 4 + b) for a, b in links]
    )


def beside(value):
    return lax.ppermute(value, "tensor", [(0, 1), (1, 0), (2, 3), (3, 2)])


def to_decoder(value):
    return lax.ppermute(value, "section", [(ENCODER, DECODER)])


def to_encoder(value):
    return lax.ppermute(value, "section", [(DECODER, ENCODER)])


def line_total(value):
    if lax.axis_size("dp") != 4:
        return lax.psum(value, "dp")
    place = lax.axis_index("dp")
    inner = (place == 1) | (place == 2)
    value = value + lax.ppermute(value, "dp", [(0, 1), (3, 2)])
    value = value + lax.ppermute(value, "dp", [(1, 2), (2, 1)])
    return jnp.where(inner, value, lax.ppermute(value, "dp", [(1, 0), (2, 3)]))


def exchange_total(value):
    if lax.axis_size("dp") != value.shape[0]:
        return lax.psum(value, "dp")
    parts = lax.all_to_all(value, "dp", 0, 0, tiled=True)
    total = jnp.sum(parts.astype(F32), 0, keepdims=True).astype(BF)
    return lax.all_to_all(jnp.broadcast_to(total, value.shape), "dp", 0, 0, tiled=True)


def far_added(own, other):
    return (own + across(other).astype(F32)).astype(BF)


def after(value, done):
    return lax.optimization_barrier((value, done))[0]


def body(
    frames,
    lengths,
    bucket_of,
    rel_table,
    norms,
    attn_in,
    attn_out,
    cross_pair,
    ffn_in,
    ffn_out,
    cotangent,
):
    section = lax.axis_index("section")
    tensor = lax.axis_index("tensor")
    pair, core = tensor // 2, tensor % 2
    decoder = section == DECODER
    quarter, model = frames.shape[3], frames.shape[4]
    length = 4 * quarter
    half = length // 2
    width = attn_in.shape[3]
    heads = width // HEAD_DIM
    buckets = rel_table.shape[1]

    own_length = lengths[section, pair, 0]
    source_length = lengths[ENCODER, pair, 0]
    starts = [(tensor ^ step) * quarter for step in range(4)]
    info = jnp.stack([section, own_length, source_length, core] + starts).astype(jnp.int32)

    def pick(array, index):
        return lax.dynamic_index_in_dim(array[0, :, 0], index, 0, keepdims=False)

    self_near = jnp.concatenate([jnp.swapaxes(attn_in[0], 1, 2), attn_out[0][None]])
    feed_near = jnp.stack([ffn_in[0], ffn_out[0]])
    pair_own = jnp.swapaxes(cross_pair[0], 1, 2)
    frame_mine = pick(frames, pair)
    frame_far = across(pick(frames, 1 - pair))
    rel_far = across(rel_table[0])
    self_far = across(after(self_near, frame_far))
    pair_source = to_decoder(pair_own)
    feed_far_e = across_in(after(feed_near, self_far), ENCODER)
    cross_near = jnp.concatenate([pair_own, after(pair_source, self_far)])
    cross_far = across_in(cross_near, DECODER)
    cot_far = across(after(pick(cotangent, 1 - pair), cross_far))
    feed_far_d = across_in(after(feed_near, cot_far), DECODER)

    def quarters(mine, far):
        both = beside(jnp.stack([mine, far]))
        return mine, both[0], far, both[1]

    buckets_here = jnp.pad(bucket_of[0][::-1], (0, 1), constant_values=-1)
    one_hot = (lax.broadcasted_iota(jnp.int32, (buckets, 2 * length), 0) == buckets_here[None]).astype(F32)
    distances = lax.dot_general(
        jnp.concatenate([rel_table[0], rel_far], 1),
        one_hot,
        TN,
        precision=HIGHEST,
        preferred_element_type=F32,
    )
    table_near = skew(distances[:heads])
    table_far = skew(distances[heads:])

    rows, normed_one = enter(info, quarters(frame_mine, frame_far), norms[0, 0])
    part, *saved_near = self_forward(info, normed_one, self_near, table_near, None)
    part, *saved_far = self_forward(
        info, normed_one, after(self_far, pair_source), table_far, part
    )
    stream_one, normed_two = add_norm(rows, part, beside(part), norms[0, 1])

    part, active_e_near, slope_near = feed_forward(
        info, after(normed_two, cross_far), feed_near, None
    )
    part, active_e_far, slope_far = feed_forward(info, normed_two, feed_far_e, part)
    cot = masked_rows(info, quarters(pick(cotangent, pair), cot_far))
    stream_e, sent, squares = source_out(
        info, after(stream_one, cot), part, beside(part), norms[0, 2]
    )
    sent_near = to_decoder(lax.dynamic_slice_in_dim(sent, core * half, half, 0))
    sent_far = beside(sent_near)
    normed_cross = after(normed_two, feed_far_d)

    part, joint_near, joint_far = cross_forward(
        info, normed_cross, sent_near, sent_far, cross_near, cross_far
    )
    stream_d, normed_three = add_norm(stream_one, part, beside(part), norms[0, 2])
    part_d, back, active_d_near, hidden_d_near, active_d_far, hidden_d_far = feed_both(
        info, normed_three, cot, feed_near, feed_far_d
    )
    grad_d, above_d, norm_d = norm_backward(cot, back, beside(back), stream_d, norms[0, 2])
    back_d, returned, d_joint_near, d_joint_far = cross_backward(
        info, joint_near, joint_far, above_d, cross_near, cross_far
    )
    returned_mine = lax.dynamic_slice_in_dim(returned, core * half, half, 0)
    returned_theirs = lax.dynamic_slice_in_dim(returned, (1 - core) * half, half, 0)
    returned = returned_mine.astype(F32) + beside(returned_theirs).astype(F32)
    returned = returned.astype(BF)
    returned_near = to_encoder(returned)
    returned_far = beside(returned_near)

    pair_near, pair_far = cross_weights(
        info,
        d_joint_near,
        d_joint_far,
        joint_near[1],
        joint_far[1],
        normed_two,
        after(above_d, returned),
        sent_near,
        sent_far,
    )
    d_pair = (pair_near + across_in(pair_far, DECODER).astype(F32)).astype(BF)
    d_source = to_encoder(d_pair[2:])

    grad_two, above_e, norm_grad_three = lax.cond(
        decoder,
        lambda: (grad_d, above_d, norm_d),
        lambda: source_back(info, cot, returned_near, returned_far, stream_e, norms[0, 2]),
    )
    down_near, down_far = lax.cond(
        decoder,
        lambda: feed_weights(active_d_near, active_d_far, cot, cot),
        lambda: feed_weights(active_e_near, active_e_far, above_e, above_e),
    )
    d_down = far_added(down_near, down_far)
    d_ffn_out = line_total(d_down).astype(F32)
    back, hidden_near, hidden_far = lax.cond(
        decoder,
        lambda: (back_d, hidden_d_near, hidden_d_far),
        lambda: feed_back(above_e, slope_near, slope_far, feed_near, feed_far_e),
    )
    grad_one, above_one, norm_grad_two = norm_backward(
        grad_two, back, beside(back), stream_one, norms[0, 1]
    )
    up_near, up_far = lax.cond(
        decoder,
        lambda: feed_weights(normed_three, normed_three, hidden_near, hidden_far),
        lambda: feed_weights(normed_two, normed_two, hidden_near, hidden_far),
    )
    d_up = far_added(up_near, up_far)
    d_ffn_in = line_total(d_up).astype(F32)

    back, attn_far, spread_far = self_backward(
        info, saved_far, above_one, normed_one, self_far, table_far, None, BF
    )
    back, attn_near, spread_near = self_backward(
        info, saved_near, after(above_one, d_down), normed_one, self_near, table_near, back, F32
    )
    grad_rows, _, norm_grad_one = norm_backward(grad_one, back, beside(back), rows, norms[0, 0])
    d_attn = exchange_total(far_added(attn_near, attn_far)).astype(F32)
    d_pair = jnp.where(decoder, d_pair[:2], d_source)
    d_pair = line_total(d_pair).astype(F32)

    part_d = after(part_d, returned)
    result, squares = finish(info, stream_d, part_d, beside(part_d), sent, squares)

    def placed(value):
        mine = lax.dynamic_slice_in_dim(value, tensor * quarter, quarter, 0)
        theirs = lax.dynamic_slice_in_dim(value, (tensor ^ 2) * quarter, quarter, 0)
        other = across(theirs.astype(BF)).astype(value.dtype)
        stacked = jnp.where(pair == 0, jnp.stack([mine, other]), jnp.stack([other, mine]))
        return stacked[None, :, None]

    spreads = jnp.concatenate([spread_near, spread_far])
    d_table = lax.dot_general(
        one_hot, spreads, NT, precision=HIGHEST, preferred_element_type=F32
    )
    def table_rows(value):
        rows_used = -(-buckets * heads // model)
        padded = jnp.pad(value.reshape(-1), (0, rows_used * model - buckets * heads))
        return padded.reshape(rows_used, model)

    shared = jnp.concatenate(
        [
            norm_grad_one,
            norm_grad_two,
            norm_grad_three,
            jnp.broadcast_to(squares[:1, :1], (1, model)),
            jnp.broadcast_to(own_length.astype(F32), (1, model)),
        ]
    )
    small = jnp.concatenate([shared, table_rows(d_table[:, :heads])])
    small = small + across(jnp.concatenate([shared, table_rows(d_table[:, heads:])]))
    small = line_total(small)
    d_table = small[8:].reshape(-1)[: buckets * heads].reshape(buckets, heads)
    stats = jnp.sqrt(small[6, :1] / (small[7, :1] * model))
    return (
        placed(result),
        placed(grad_rows),
        d_table[None],
        small[:6].reshape(1, 3, 2, model),
        jnp.swapaxes(d_attn[:3], 1, 2)[None],
        d_attn[3][None],
        jnp.swapaxes(d_pair, 1, 2)[None],
        d_ffn_in[None],
        d_ffn_out[None],
        stats,
    )


def solution(mesh):
    in_specs = (
        P("section", None, "dp", "tensor", None),
        P(None, None, "dp"),
        P("section", None),
        P("section", None, "tensor"),
        P("section", None, None, None),
        P("section", None, None, "tensor"),
        P("section", "tensor", None),
        P("section", None, None, "tensor"),
        P("section", None, "tensor"),
        P("section", "tensor", None),
        P("section", None, "dp", "tensor", None),
    )
    out_specs = (
        P("section", None, "dp", "tensor", None),
        P("section", None, "dp", "tensor", None),
        P("section", None, "tensor"),
        P("section", None, None, None),
        P("section", None, None, "tensor"),
        P("section", "tensor", None),
        P("section", None, None, "tensor"),
        P("section", None, "tensor"),
        P("section", "tensor", None),
        P("section"),
    )
    return jax.shard_map(body, mesh=mesh, in_specs=in_specs, out_specs=out_specs, check_vma=False)
```

```python
import functools
import math

import jax
import jax.numpy as jnp
from jax import lax
from jax.experimental import pallas as pl
from jax.experimental.pallas import tpu as pltpu
from jax.sharding import PartitionSpec as P

HEAD_DIM = 64
SCALE = HEAD_DIM ** (-0.5)
EPSILON = 1e-05
MASKED = -1000000000.0
HIGHEST = lax.Precision.HIGHEST
BF = jnp.bfloat16
F32 = jnp.float32
NN = (((1,), (0,)), ((), ()))
NT = (((1,), (1,)), ((), ()))
TN = (((0,), (0,)), ((), ()))
TILE = 256
BAND = 128
ENCODER, DECODER = 0, 1
ROLE, OWN_LEN, SOURCE_LEN, CORE, START = 0, 1, 2, 3, 4
HIDES_LITTLE = 0.02
HIDES_MUCH = 2.0


def mm(left, right, dims):
    return lax.dot_general(left, right, dims, preferred_element_type=F32)


def whole():
    return pl.BlockSpec(memory_space=pltpu.VMEM)


def scalars():
    return pl.BlockSpec(memory_space=pltpu.SMEM)


def shape(dims, dtype):
    return jax.ShapeDtypeStruct(dims, dtype)


def cost(flops, nbytes, weight=HIDES_LITTLE):
    return pl.CostEstimate(
        flops=int(flops * weight), bytes_accessed=int(nbytes * weight), transcendentals=0
    )


def params(megabytes=28):
    return pltpu.CompilerParams(vmem_limit_bytes=megabytes * 1024 * 1024)


def norm_of(values, norm_ref):
    centred = values - jnp.mean(values, -1, keepdims=True)
    factor = lax.rsqrt(jnp.mean(centred * centred, -1, keepdims=True) + EPSILON)
    return centred * factor * norm_ref[0:1, :] + norm_ref[1:2, :]


def enter_kernel(info, mine, core_mine, far, core_far, norm_ref, rows_ref, normed_ref):
    quarter = mine.shape[0]
    for step, piece in enumerate((mine, core_mine, far, core_far)):
        start = pl.multiple_of(info[START + step], quarter)
        values = piece[...]
        rows_ref[pl.ds(start, quarter), :] = values
        normed_ref[pl.ds(start, quarter), :] = norm_of(values.astype(F32), norm_ref).astype(BF)


def enter(info, pieces, norm):
    quarter, width = pieces[0].shape
    out = shape((4 * quarter, width), BF)
    return pl.pallas_call(
        enter_kernel,
        out_shape=(out, out),
        in_specs=[scalars()] + [whole()] * 5,
        out_specs=(whole(), whole()),
        compiler_params=params(),
        cost_estimate=cost(16 * quarter * width * 4, quarter * width * 24),
    )(info, *pieces, norm)


def masked_kernel(info, mine, core_mine, far, core_far, rows_ref):
    quarter = mine.shape[0]
    for step, piece in enumerate((mine, core_mine, far, core_far)):
        start = pl.multiple_of(info[START + step], quarter)
        row = start + lax.broadcasted_iota(jnp.int32, (quarter, 1), 0)
        values = jnp.where(row < info[OWN_LEN], piece[...].astype(F32), 0.0)
        rows_ref[pl.ds(start, quarter), :] = values.astype(BF)


def masked_rows(info, pieces):
    quarter, width = pieces[0].shape
    return pl.pallas_call(
        masked_kernel,
        out_shape=shape((4 * quarter, width), BF),
        in_specs=[scalars()] + [whole()] * 4,
        out_specs=whole(),
        compiler_params=params(),
        cost_estimate=cost(quarter * width * 8, quarter * width * 16),
    )(info, *pieces)


def skew_kernel(distance_ref, table_ref):
    width = table_ref.shape[2]
    for head in range(distance_ref.shape[0]):
        row = jnp.broadcast_to(distance_ref[head : head + 1, :], (BAND, width))
        table_ref[head] = pltpu.roll(row, width - (BAND - 1), 1, stride=1, stride_axis=0)


def skew(distances):
    heads, width = distances.shape
    return pl.pallas_call(
        skew_kernel,
        out_shape=shape((heads, BAND, width), F32),
        in_specs=[whole()],
        out_specs=whole(),
        compiler_params=params(),
        cost_estimate=cost(heads * BAND * width, heads * BAND * width * 4),
    )(distances)


def unskewed(band):
    rows, width = band.shape
    while rows > 8:
        rows //= 2
        band = pltpu.roll(band[:rows], rows, 1) + band[rows:]
    amount = (rows - 1) - lax.broadcasted_iota(jnp.int32, (rows, width), 0)
    for bit in range(3):
        band = jnp.where(((amount >> bit) & 1) == 1, pltpu.roll(band, 1 << bit, 1), band)
    return jnp.sum(band, 0, keepdims=True)


def by_blocks(count, body):
    def step(index, carry):
        body(pl.ds(pl.multiple_of(index * TILE, TILE), TILE))
        return carry

    lax.fori_loop(0, count // TILE, step, 0)


def head_span(head):
    return slice(head * HEAD_DIM, (head + 1) * HEAD_DIM)


def allowed_keys(info, length, causal, length_at):
    key = lax.broadcasted_iota(jnp.int32, (length, length), 0)
    last = info[length_at] - 1
    if not causal:
        return key <= last
    query = lax.broadcasted_iota(jnp.int32, (1, length), 1)
    free = jnp.where(info[ROLE] == DECODER, 0, 1 << 20)
    return key <= jnp.minimum(query + free, last)


def scores_of(queries, keys, allowed, table_ref, head):
    scores = mm(keys, queries, TN)
    if table_ref is not None:
        length = scores.shape[0]
        starts = range(length - BAND, -BAND, -BAND)
        bands = [table_ref[head, :, start : start + length] for start in starts]
        scores = scores + jnp.concatenate(bands, 0)
    return jnp.where(allowed, scores, MASKED)


def attend(info, qkv_ref, table_ref, out_ref, lse_ref, length_at):
    width, length = out_ref.shape
    allowed = allowed_keys(info, length, table_ref is not None, length_at)
    for head in range(width // HEAD_DIM):
        span = head_span(head)
        queries = qkv_ref[0, span, :] * jnp.asarray(SCALE, BF)
        scores = scores_of(queries, qkv_ref[1, span, :], allowed, table_ref, head)
        peak = jnp.max(scores, 0, keepdims=True)
        lifted = jnp.exp(scores - peak)
        total = jnp.sum(lifted, 0, keepdims=True)
        mixed = mm(qkv_ref[2, span, :], lifted.astype(BF), NN)
        out_ref[span, :] = mixed / total
        lse_ref[head : head + 1, :] = peak + jnp.log(total)


def self_forward_kernel(has_sum, info, normed, weights, table, *refs):
    previous = refs[0] if has_sum else None
    sum_ref, qkv_ref, out_ref, lse_ref = refs[1 if has_sum else 0 :]
    length = out_ref.shape[1]

    def inputs(cols):
        block = normed[cols, :]
        for place in range(3):
            qkv_ref[place, :, cols] = mm(weights[place], block, NT).astype(BF)

    by_blocks(length, inputs)
    attend(info, qkv_ref, table, out_ref, lse_ref, OWN_LEN)

    def outputs(cols):
        value = mm(out_ref[:, cols].astype(BF), weights[3], TN)
        if has_sum:
            value = value + previous[cols, :]
        sum_ref[cols, :] = value.astype(sum_ref.dtype)

    by_blocks(length, outputs)


def attention_cost(length, width, model, matmuls, projections, weight=HIDES_LITTLE):
    heads = width // HEAD_DIM
    return cost(
        heads * length * length * HEAD_DIM * 2 * matmuls * 4 + projections * 2 * length * model * width,
        length * model * 8,
        weight,
    )


def saved_shapes(length, width):
    return (shape((3, width, length), BF), shape((width, length), F32), shape((8, length), F32))


def self_forward(info, normed, weights, table, previous):
    length, model = normed.shape
    width = weights.shape[1]
    has_sum = previous is not None
    operands = [info, normed, weights, table] + ([previous] if has_sum else [])
    return pl.pallas_call(
        functools.partial(self_forward_kernel, has_sum),
        out_shape=(shape((length, model), BF if has_sum else F32),) + saved_shapes(length, width),
        in_specs=[scalars()] + [whole()] * (len(operands) - 1),
        out_specs=(whole(),) * 4,
        compiler_params=params(),
        cost_estimate=attention_cost(length, width, model, 2, 4, HIDES_MUCH),
    )(*operands)


def rows_of(ref, place, width):
    return ref[place * width : (place + 1) * width, :]


def cross_forward_kernel(info, normed, near, far, weights_near, weights_far, *refs):
    sum_ref = refs[0]
    length, width = normed.shape[0], weights_near.shape[0] // 4
    half = near.shape[0]
    sides = ((weights_near, refs[1:4]), (weights_far, refs[4:7]))

    @pl.when(info[ROLE] == DECODER)
    def _():
        for weights, (qkv_ref, out_ref, lse_ref) in sides:

            def queries(cols, weights=weights, qkv_ref=qkv_ref):
                qkv_ref[0, :, cols] = mm(rows_of(weights, 0, width), normed[cols, :], NT).astype(BF)

            by_blocks(length, queries)
            for piece, side in ((near, info[CORE]), (far, 1 - info[CORE])):
                base = side * half

                def sources(index, carry, piece=piece, base=base, weights=weights, qkv_ref=qkv_ref):
                    local = pl.multiple_of(index * TILE, TILE)
                    block = piece[pl.ds(local, TILE), :]
                    cols = pl.ds(pl.multiple_of(base + local, TILE), TILE)
                    for place in (1, 2):
                        qkv_ref[place, :, cols] = mm(rows_of(weights, 1 + place, width), block, NT).astype(BF)
                    return carry

                lax.fori_loop(0, half // TILE, sources, 0)
            attend(info, qkv_ref, None, out_ref, lse_ref, SOURCE_LEN)

        def outputs(cols):
            value = mm(refs[2][:, cols].astype(BF), rows_of(weights_near, 1, width), TN)
            value = value + mm(refs[5][:, cols].astype(BF), rows_of(weights_far, 1, width), TN)
            sum_ref[cols, :] = value.astype(sum_ref.dtype)

        by_blocks(length, outputs)


def cross_forward(info, normed, near, far, weights_near, weights_far):
    length, model = normed.shape
    width = weights_near.shape[0] // 4
    saved = saved_shapes(length, width)
    results = pl.pallas_call(
        cross_forward_kernel,
        out_shape=(shape((length, model), BF),) + saved + saved,
        in_specs=[scalars()] + [whole()] * 5,
        out_specs=(whole(),) * 7,
        compiler_params=params(),
        cost_estimate=attention_cost(length, 2 * width, model, 2, 4),
    )(info, normed, near, far, weights_near, weights_far)
    return results[0], results[1:4], results[4:7]


def attend_back(info, saved, table_ref, upstream, grads_ref, band, length_at):
    qkv_ref, out_ref, lse_ref = saved
    width, length = out_ref.shape
    allowed = allowed_keys(info, length, table_ref is not None, length_at)
    if table_ref is not None:
        band[...] = jnp.zeros_like(band)
    for head in range(width // HEAD_DIM):
        span = head_span(head)
        queries = qkv_ref[0, span, :] * jnp.asarray(SCALE, BF)
        keys, above = qkv_ref[1, span, :], upstream[span, :]
        scores = scores_of(queries, keys, allowed, table_ref, head)
        probs = jnp.exp(scores - lse_ref[head : head + 1, :])
        inner = jnp.sum(above.astype(F32) * out_ref[span, :], 0, keepdims=True)
        d_scores = probs * (mm(qkv_ref[2, span, :], above, TN) - inner)
        low = d_scores.astype(BF)
        grads_ref[0, span, :] = (mm(keys, low, NN) * SCALE).astype(BF)
        grads_ref[1, span, :] = mm(queries, low, NT).astype(BF)
        grads_ref[2, span, :] = mm(above, probs.astype(BF), NT).astype(BF)
        if table_ref is not None:
            for part in range(length // BAND):
                start = length - BAND - part * BAND
                rows = slice(part * BAND, (part + 1) * BAND)
                band[head, :, start : start + length] += d_scores[rows, :]


def self_backward_kernel(has_sum, info, qkv, out, lse, above, normed, weights, table, *refs):
    previous = refs[0] if has_sum else None
    refs = refs[1 if has_sum else 0 :]
    sum_ref, weight_ref, spread_ref, upstream = refs[:4]
    band, grads_ref = refs[4:6]
    length = above.shape[0]

    def entering(cols):
        upstream[:, cols] = mm(weights[3], above[cols, :], NT).astype(BF)

    by_blocks(length, entering)
    attend_back(info, (qkv, out, lse), table, upstream, grads_ref, band, OWN_LEN)

    def leaving(cols):
        value = mm(grads_ref[0, :, cols], weights[0], TN)
        for place in (1, 2):
            value = value + mm(grads_ref[place, :, cols], weights[place], TN)
        if has_sum:
            value = value + previous[cols, :]
        sum_ref[cols, :] = value.astype(sum_ref.dtype)

    by_blocks(length, leaving)
    for place in range(3):
        weight_ref[place] = mm(grads_ref[place], normed[...], NN).astype(weight_ref.dtype)
    weight_ref[3] = mm(out[...].astype(BF), above[...], NN).astype(weight_ref.dtype)
    for head in range(table.shape[0]):
        spread_ref[head : head + 1, :] = unskewed(band[head])


def self_backward(info, saved, above, normed, weights, table, previous, weight_type):
    length, model = above.shape
    width = weights.shape[1]
    has_sum = previous is not None
    operands = [info, *saved, above, normed, weights, table] + ([previous] if has_sum else [])
    return pl.pallas_call(
        functools.partial(self_backward_kernel, has_sum),
        out_shape=(
            shape((length, model), BF if has_sum else F32),
            shape((4, width, model), weight_type),
            shape((table.shape[0], table.shape[2]), F32),
        ),
        in_specs=[scalars()] + [whole()] * (len(operands) - 1),
        out_specs=(whole(),) * 3,
        scratch_shapes=[
            pltpu.VMEM((width, length), BF),
            pltpu.VMEM(table.shape, F32),
            pltpu.VMEM((3, width, length), BF),
        ],
        compiler_params=params(),
        cost_estimate=attention_cost(length, width, model, 5, 8, HIDES_MUCH),
    )(*operands)


def cross_backward_kernel(info, *refs):
    saved_near, saved_far, (above, weights_near, weights_far) = refs[:3], refs[3:6], refs[6:9]
    sum_ref, source_ref, grads_near, grads_far, upstream = refs[9:14]
    length, width = above.shape[0], weights_near.shape[0] // 4

    @pl.when(info[ROLE] == DECODER)
    def _():
        for saved, weights, grads_ref in (
            (saved_near, weights_near, grads_near),
            (saved_far, weights_far, grads_far),
        ):

            def entering(cols, weights=weights):
                upstream[:, cols] = mm(rows_of(weights, 1, width), above[cols, :], NT).astype(BF)

            by_blocks(length, entering)
            attend_back(info, saved, None, upstream, grads_ref, None, SOURCE_LEN)

        def leaving(cols):
            value = mm(grads_near[0, :, cols], rows_of(weights_near, 0, width), TN)
            value = value + mm(grads_far[0, :, cols], rows_of(weights_far, 0, width), TN)
            sum_ref[cols, :] = value.astype(BF)
            source = None
            for grads_ref, weights in ((grads_near, weights_near), (grads_far, weights_far)):
                for place in (1, 2):
                    term = mm(grads_ref[place, :, cols], rows_of(weights, 1 + place, width), TN)
                    source = term if source is None else source + term
            source_ref[cols, :] = source.astype(BF)

        by_blocks(length, leaving)


def cross_backward(info, saved_near, saved_far, above, weights_near, weights_far):
    length, model = above.shape
    width = weights_near.shape[0] // 4
    out, grads = shape((length, model), BF), shape((3, width, length), BF)
    return pl.pallas_call(
        cross_backward_kernel,
        out_shape=(out, out, grads, grads),
        in_specs=[scalars()] + [whole()] * 9,
        out_specs=(whole(),) * 4,
        scratch_shapes=[pltpu.VMEM((width, length), BF)],
        compiler_params=params(),
        cost_estimate=attention_cost(length, 2 * width, model, 5, 4),
    )(info, *saved_near, *saved_far, above, weights_near, weights_far)


def cross_weights_kernel(info, grads_near, grads_far, out_near, out_far, normed, above, *refs):
    near, far, weight_near, weight_far = refs
    half = near.shape[0]

    @pl.when(info[ROLE] == DECODER)
    def _():
        start = pl.multiple_of(info[CORE] * half, half)
        other = pl.multiple_of((1 - info[CORE]) * half, half)
        for grads, out, target in (
            (grads_near, out_near, weight_near),
            (grads_far, out_far, weight_far),
        ):
            target[0] = mm(grads[0], normed[...], NN).astype(target.dtype)
            target[1] = mm(out[...].astype(BF), above[...], NN).astype(target.dtype)
            for place in (1, 2):
                value = mm(grads[place, :, pl.ds(start, half)], near[...], NN)
                value = value + mm(grads[place, :, pl.ds(other, half)], far[...], NN)
                target[1 + place] = value.astype(target.dtype)


def cross_weights(info, grads_near, grads_far, out_near, out_far, normed, above, near, far):
    length, model = above.shape
    width = out_near.shape[0]
    return pl.pallas_call(
        cross_weights_kernel,
        out_shape=(shape((4, width, model), F32), shape((4, width, model), BF)),
        in_specs=[scalars()] + [whole()] * 8,
        out_specs=(whole(),) * 2,
        compiler_params=params(),
        cost_estimate=cost(16 * length * model * width, length * model * 16),
    )(info, grads_near, grads_far, out_near, out_far, normed, above, near, far)


def row_spec(width):
    return pl.BlockSpec((TILE, width), lambda index: (index, 0))


def pack_spec(place, width):
    return pl.BlockSpec((width, width), lambda index: (place, 0))


def fixed_spec(dims):
    return pl.BlockSpec(dims, lambda index: (0,) * len(dims))


def add_norm_kernel(stream, near, far, norm_ref, sum_ref, normed_ref):
    value = stream[...].astype(F32) + (near[...].astype(F32) + far[...].astype(F32))
    sum_ref[...] = value
    normed_ref[...] = norm_of(value, norm_ref).astype(BF)


def add_norm(stream, near, far, norm):
    length, model = stream.shape
    return pl.pallas_call(
        add_norm_kernel,
        grid=(length // TILE,),
        out_shape=(shape((length, model), F32), shape((length, model), BF)),
        in_specs=[row_spec(model)] * 3 + [fixed_spec((2, model))],
        out_specs=(row_spec(model),) * 2,
        compiler_params=params(),
        cost_estimate=cost(length * model * 12, length * model * 14),
    )(stream, near, far, norm)


def row_mask(info, index, at):
    row = index * TILE + lax.broadcasted_iota(jnp.int32, (TILE, 1), 0)
    return row < info[at]


def squares_of(value):
    return jnp.sum(jnp.sum(value * value, 0, keepdims=True), 1, keepdims=True)


def source_kernel(info, stream, near, far, norm_ref, sum_ref, sent_ref, square_ref):
    index = pl.program_id(0)
    value = stream[...] + (near[...].astype(F32) + far[...].astype(F32))
    sum_ref[...] = value
    result = jnp.where(row_mask(info, index, OWN_LEN), norm_of(value, norm_ref), 0.0)
    sent_ref[...] = result.astype(BF)

    @pl.when(index == 0)
    def _():
        square_ref[...] = jnp.zeros_like(square_ref)

    square_ref[...] += squares_of(result)


def source_out(info, stream, near, far, norm):
    length, model = stream.shape
    return pl.pallas_call(
        source_kernel,
        grid=(length // TILE,),
        out_shape=(shape((length, model), F32), shape((length, model), BF), shape((8, 128), F32)),
        in_specs=[scalars()] + [row_spec(model)] * 3 + [fixed_spec((2, model))],
        out_specs=(row_spec(model), row_spec(model), fixed_spec((8, 128))),
        compiler_params=params(),
        cost_estimate=cost(length * model * 14, length * model * 14),
    )(info, stream, near, far, norm)


def finish_kernel(info, stream, near, far, sent, square, out_ref, square_ref):
    index = pl.program_id(0)

    @pl.when(info[ROLE] == DECODER)
    def _():
        value = stream[...] + (near[...].astype(F32) + far[...].astype(F32))
        value = jnp.where(row_mask(info, index, OWN_LEN), value, 0.0)
        out_ref[...] = value.astype(BF)

        @pl.when(index == 0)
        def _():
            square_ref[...] = jnp.zeros_like(square_ref)

        square_ref[...] += squares_of(value)

    @pl.when(info[ROLE] == ENCODER)
    def _():
        out_ref[...] = sent[...]
        square_ref[...] = square[...]


def finish(info, stream, near, far, sent, square):
    length, model = stream.shape
    return pl.pallas_call(
        finish_kernel,
        grid=(length // TILE,),
        out_shape=(shape((length, model), BF), shape((8, 128), F32)),
        in_specs=[scalars()] + [row_spec(model)] * 4 + [fixed_spec((8, 128))],
        out_specs=(row_spec(model), fixed_spec((8, 128))),
        compiler_params=params(),
        cost_estimate=cost(length * model * 6, length * model * 12),
    )(info, stream, near, far, sent, square)


def norm_back(upstream, values, norm_ref):
    centred = values - jnp.mean(values, -1, keepdims=True)
    factor = lax.rsqrt(jnp.mean(centred * centred, -1, keepdims=True) + EPSILON)
    unit = centred * factor
    scaled = upstream * norm_ref[0:1, :]
    inner = scaled - jnp.mean(scaled, -1, keepdims=True)
    inner = inner - unit * jnp.mean(scaled * unit, -1, keepdims=True)
    gain = jnp.sum(upstream * unit, 0, keepdims=True)
    shift = jnp.sum(upstream, 0, keepdims=True)
    return factor * inner, gain, shift


def norm_back_kernel(residual, near, far, values, norm_ref, grad_ref, low_ref, norm_grad_ref):
    upstream = near[...].astype(F32) + far[...].astype(F32)
    grad, gain, shift = norm_back(upstream, values[...].astype(F32), norm_ref)
    grad = residual[...].astype(F32) + grad
    grad_ref[...] = grad
    low_ref[...] = grad.astype(BF)

    @pl.when(pl.program_id(0) == 0)
    def _():
        norm_grad_ref[...] = jnp.zeros_like(norm_grad_ref)

    norm_grad_ref[0:1, :] += gain
    norm_grad_ref[1:2, :] += shift


def norm_backward(residual, near, far, values, norm):
    length, model = values.shape
    return pl.pallas_call(
        norm_back_kernel,
        grid=(length // TILE,),
        out_shape=(shape((length, model), F32), shape((length, model), BF), shape((2, model), F32)),
        in_specs=[row_spec(model)] * 4 + [fixed_spec((2, model))],
        out_specs=(row_spec(model), row_spec(model), fixed_spec((2, model))),
        compiler_params=params(),
        cost_estimate=cost(length * model * 20, length * model * 18),
    )(residual, near, far, values, norm)


def gelu_parts(hidden):
    half = 0.5 * (1.0 + lax.erf(hidden * math.sqrt(0.5)))
    slope = half + hidden * jnp.exp(-0.5 * hidden * hidden) * (1.0 / math.sqrt(2.0 * math.pi))
    return hidden * half, slope


def feed_forward_kernel(has_sum, info, normed, pack, *refs):
    previous = refs[0] if has_sum else None
    sum_ref, active_ref, slope_ref = refs[1 if has_sum else 0 :]

    @pl.when(info[ROLE] == ENCODER)
    def _():
        active, slope = gelu_parts(mm(normed[...], pack[0], NN))
        active = active.astype(BF)
        active_ref[...] = active
        slope_ref[...] = slope.astype(BF)
        value = mm(active, pack[1], NN)
        if has_sum:
            value = value + previous[...]
        sum_ref[...] = value.astype(sum_ref.dtype)


def feed_forward(info, normed, pack, previous):
    length, model = normed.shape
    hidden = pack.shape[2]
    has_sum = previous is not None
    operands = [info, normed, pack] + ([previous] if has_sum else [])
    return pl.pallas_call(
        functools.partial(feed_forward_kernel, has_sum),
        grid=(length // TILE,),
        out_shape=(
            shape((length, model), BF if has_sum else F32),
            shape((length, hidden), BF),
            shape((length, hidden), BF),
        ),
        in_specs=[scalars(), row_spec(model), fixed_spec(pack.shape)]
        + ([row_spec(model)] if has_sum else []),
        out_specs=(row_spec(model), row_spec(hidden), row_spec(hidden)),
        compiler_params=params(),
        cost_estimate=cost(4 * length * model * hidden, length * model * 12),
    )(*operands)


def feed_above_kernel(info, cot, down_near, down_far, near_ref, far_ref):
    @pl.when(info[ROLE] == DECODER)
    def _():
        near_ref[...] = mm(cot[...], down_near[...], NT)
        far_ref[...] = mm(cot[...], down_far[...], NT)


def feed_above(info, cot, down_near, down_far):
    length, model = cot.shape
    hidden = down_near.shape[0]
    unit = shape((length, hidden), F32)
    return pl.pallas_call(
        feed_above_kernel,
        grid=(length // TILE,),
        out_shape=(unit, unit),
        in_specs=[
            scalars(),
            row_spec(model),
            fixed_spec(down_near.shape),
            pack_spec(1, model),
        ],
        out_specs=(row_spec(hidden),) * 2,
        compiler_params=params(),
        cost_estimate=cost(4 * length * model * hidden, length * model * 10),
    )(info, cot, down_near, down_far)


def feed_both_kernel(info, normed, above_near, above_far, up_near, up_far, back_ref, *refs):
    @pl.when(info[ROLE] == DECODER)
    def _():
        back = None
        for up, above, active_ref, grad_ref in (
            (up_near, above_near, *refs[0:2]),
            (up_far, above_far, *refs[2:4]),
        ):
            active, slope = gelu_parts(mm(normed[...], up[...], NN))
            active_ref[...] = active.astype(BF)
            grad = (above[...] * slope).astype(BF)
            grad_ref[...] = grad
            term = mm(grad, up[...], NT)
            back = term if back is None else back + term
        back_ref[...] = back.astype(BF)


def feed_both(info, normed, above, up_near, up_far):
    length, model = normed.shape
    hidden = up_near.shape[1]
    out, unit = shape((length, model), BF), shape((length, hidden), BF)
    return pl.pallas_call(
        feed_both_kernel,
        grid=(length // TILE,),
        out_shape=(out, unit, unit, unit, unit),
        in_specs=[
            scalars(),
            row_spec(model),
            row_spec(hidden),
            row_spec(hidden),
            fixed_spec(up_near.shape),
            fixed_spec(up_far.shape),
        ],
        out_specs=(row_spec(model),) + (row_spec(hidden),) * 4,
        compiler_params=params(),
        cost_estimate=cost(8 * length * model * hidden, length * model * 20),
    )(info, normed, *above, up_near, up_far)


def feed_value_kernel(info, active_near, active_far, down_near, down_far, sum_ref):
    @pl.when(info[ROLE] == DECODER)
    def _():
        value = mm(active_near[...], down_near[...], NN) + mm(active_far[...], down_far[...], NN)
        sum_ref[...] = value.astype(BF)


def feed_value(info, active_near, active_far, down_near, down_far):
    length, hidden = active_near.shape
    model = down_near.shape[1]
    return pl.pallas_call(
        feed_value_kernel,
        grid=(length // TILE,),
        out_shape=shape((length, model), BF),
        in_specs=[
            scalars(),
            row_spec(hidden),
            row_spec(hidden),
            fixed_spec(down_near.shape),
            pack_spec(1, model),
        ],
        out_specs=row_spec(model),
        compiler_params=params(),
        cost_estimate=cost(4 * length * model * hidden, length * model * 6),
    )(info, active_near, active_far, down_near, down_far)


def source_back_kernel(info, cot, near, far, values, norm_ref, *refs):
    slope_near, slope_far, pack_near, pack_far, grad_ref, low_ref, norm_grad_ref = refs[:7]
    back_ref, hidden_near, hidden_far = refs[7:]
    index = pl.program_id(0)
    blocks = near.shape[0] // TILE
    rows = pl.ds(pl.multiple_of(lax.rem(index, blocks) * TILE, TILE), TILE)
    mine = (index >= blocks).astype(jnp.int32) == info[CORE]
    returned = jnp.where(mine, near[rows, :].astype(F32), far[rows, :].astype(F32))
    upstream = cot[...].astype(F32) + returned
    upstream = jnp.where(row_mask(info, index, OWN_LEN), upstream, 0.0)
    grad, gain, shift = norm_back(upstream, values[...], norm_ref)
    low = grad.astype(BF)
    grad_ref[...] = grad
    low_ref[...] = low

    @pl.when(index == 0)
    def _():
        norm_grad_ref[...] = jnp.zeros_like(norm_grad_ref)

    norm_grad_ref[0:1, :] += gain
    norm_grad_ref[1:2, :] += shift
    back = None
    for pack, slope, hidden_ref in (
        (pack_near, slope_near, hidden_near),
        (pack_far, slope_far, hidden_far),
    ):
        hidden = (mm(low, pack[1], NT) * slope[...].astype(F32)).astype(BF)
        hidden_ref[...] = hidden
        term = mm(hidden, pack[0], NT)
        back = term if back is None else back + term
    back_ref[...] = back.astype(BF)


def source_back(info, cot, near, far, values, norm, slope_near, slope_far, pack_near, pack_far):
    length, model = values.shape
    hidden = pack_near.shape[2]
    unit = shape((length, hidden), BF)
    return pl.pallas_call(
        source_back_kernel,
        grid=(length // TILE,),
        out_shape=(
            shape((length, model), F32),
            shape((length, model), BF),
            shape((2, model), F32),
            shape((length, model), BF),
            unit,
            unit,
        ),
        in_specs=[
            scalars(),
            row_spec(model),
            fixed_spec(near.shape),
            fixed_spec(far.shape),
            row_spec(model),
            fixed_spec((2, model)),
            row_spec(hidden),
            row_spec(hidden),
            fixed_spec(pack_near.shape),
            fixed_spec(pack_far.shape),
        ],
        out_specs=(
            row_spec(model),
            row_spec(model),
            fixed_spec((2, model)),
            row_spec(model),
            row_spec(hidden),
            row_spec(hidden),
        ),
        compiler_params=params(),
        cost_estimate=cost(8 * length * model * hidden, length * model * 30),
    )(info, cot, near, far, values, norm, slope_near, slope_far, pack_near, pack_far)


def product_kernel(left_near, left_far, right_near, right_far, near_ref, far_ref):
    near_ref[...] = mm(left_near[...], right_near[...], TN)
    far_ref[...] = mm(left_far[...], right_far[...], TN).astype(BF)


def feed_weights(left_near, left_far, right_near, right_far):
    length, rows = left_near.shape
    columns = right_near.shape[1]
    left = pl.BlockSpec((length, TILE), lambda index: (0, index))
    right = pl.BlockSpec((length, columns), lambda index: (0, 0))
    out = row_spec(columns)
    return pl.pallas_call(
        product_kernel,
        grid=(rows // TILE,),
        out_shape=(shape((rows, columns), F32), shape((rows, columns), BF)),
        in_specs=[left, left, right, right],
        out_specs=(out, out),
        compiler_params=params(),
        cost_estimate=cost(4 * length * rows * columns, length * rows * 12),
    )(left_near, left_far, right_near, right_far)


def across(value):
    return lax.ppermute(value, "tensor", [(0, 2), (1, 3), (2, 0), (3, 1)])


def across_in(value, role):
    links = [(0, 2), (1, 3), (2, 0), (3, 1)]
    return lax.ppermute(
        value, ("section", "tensor"), [(role * 4 + a, role * 4 + b) for a, b in links]
    )


def beside(value):
    return lax.ppermute(value, "tensor", [(0, 1), (1, 0), (2, 3), (3, 2)])


def to_decoder(value):
    return lax.ppermute(value, "section", [(ENCODER, DECODER)])


def to_encoder(value):
    return lax.ppermute(value, "section", [(DECODER, ENCODER)])


class Line:
    def __init__(self, value):
        self.four = lax.axis_size("dp") == 4
        self.value = value
        self.done = 0

    def inward(self, behind=None):
        if self.four:
            arrived = lax.ppermute(self.value, "dp", [(0, 1), (3, 2)])
            self.value = self.value + (arrived if behind is None else after(arrived, behind))
        self.done = 1

    def swap(self):
        if self.four:
            self.value = self.value + lax.ppermute(self.value, "dp", [(1, 2), (2, 1)])
        self.done = 2

    def total(self):
        if not self.four:
            return lax.psum(self.value, "dp").astype(F32)
        if self.done < 1:
            self.inward()
        if self.done < 2:
            self.swap()
        place = lax.axis_index("dp")
        inner = (place == 1) | (place == 2)
        outward = lax.ppermute(self.value, "dp", [(1, 0), (2, 3)])
        return jnp.where(inner, self.value, outward).astype(F32)


def near_added(own, other):
    return (own + other.astype(F32)).astype(BF)


def after(value, done):
    return lax.optimization_barrier((value, done))[0]


def body(
    frames,
    lengths,
    bucket_of,
    rel_table,
    norms,
    attn_in,
    attn_out,
    cross_pair,
    ffn_in,
    ffn_out,
    cotangent,
):
    section = lax.axis_index("section")
    tensor = lax.axis_index("tensor")
    pair, core = tensor // 2, tensor % 2
    decoder = section == DECODER
    quarter, model = frames.shape[3], frames.shape[4]
    length = 4 * quarter
    half = length // 2
    width = attn_in.shape[3]
    heads = width // HEAD_DIM
    buckets = rel_table.shape[1]

    own_length = lengths[section, pair, 0]
    source_length = lengths[ENCODER, pair, 0]
    starts = [(tensor ^ step) * quarter for step in range(4)]
    info = jnp.stack([section, own_length, source_length, core] + starts).astype(jnp.int32)

    def pick(array, index):
        return lax.dynamic_index_in_dim(array[0, :, 0], index, 0, keepdims=False)

    self_near = jnp.concatenate([jnp.swapaxes(attn_in[0], 1, 2), attn_out[0][None]])
    feed_near = jnp.stack([ffn_in[0], ffn_out[0]])
    pair_own = jnp.swapaxes(cross_pair[0], 1, 2)
    frame_mine = pick(frames, pair)
    frame_far = across(pick(frames, 1 - pair))
    rel_far = across(rel_table[0])
    self_far = across(after(self_near, rel_far))
    pair_source = to_decoder(pair_own)
    feed_far_e = across_in(after(feed_near, frame_far), ENCODER)
    cross_near = jnp.concatenate([pair_own, pair_source]).reshape(4 * width, model)
    pack_near = jnp.concatenate([cross_near, ffn_out[0]])
    pack_far = across_in(after(pack_near, frame_far), DECODER)
    up_far_d = across_in(after(ffn_in[0], pack_far), DECODER)
    cot_mine, cot_other = pick(cotangent, pair), pick(cotangent, 1 - pair)

    def quarters(mine, far):
        both = beside(jnp.stack([mine, far]))
        return mine, both[0], far, both[1]

    buckets_here = jnp.pad(bucket_of[0][::-1], (0, 1), constant_values=-1)
    one_hot = (lax.broadcasted_iota(jnp.int32, (buckets, 2 * length), 0) == buckets_here[None]).astype(F32)
    distances = lax.dot_general(
        jnp.concatenate([rel_table[0], rel_far], 1),
        one_hot,
        TN,
        precision=HIGHEST,
        preferred_element_type=F32,
    )
    table_near = skew(distances[:heads])
    table_far = skew(distances[heads:])

    rows, normed_one = enter(info, quarters(frame_mine, frame_far), norms[0, 0])
    part, *saved_near = self_forward(info, normed_one, self_near, table_near, None)
    part, *saved_far = self_forward(
        info, normed_one, after(self_far, pack_near), table_far, part
    )
    stream_one, normed_two = add_norm(
        rows, part, beside(part), norms[0, 1]
    )

    part, active_e_near, slope_near = feed_forward(
        info, normed_two, feed_near, None
    )
    part, active_e_far, slope_far = feed_forward(
        info, normed_two, after(feed_far_e, pack_far), part
    )
    stream_e, sent, squares = source_out(
        info, stream_one, part, beside(part), norms[0, 2]
    )
    sent_near = to_decoder(lax.dynamic_slice_in_dim(sent, core * half, half, 0))
    sent_far = beside(sent_near)
    cot = masked_rows(info, quarters(cot_mine, across(after(cot_other, sent))))
    hidden_pre = feed_above(info, cot, ffn_out[0], pack_far)
    normed_cross = after(normed_two, (hidden_pre, up_far_d))

    part, joint_near, joint_far = cross_forward(
        info, normed_cross, sent_near, sent_far, cross_near, pack_far
    )
    stream_d, normed_three = add_norm(stream_one, part, beside(part), norms[0, 2])
    back, active_d_near, hidden_d_near, active_d_far, hidden_d_far = feed_both(
        info, normed_three, hidden_pre, ffn_in[0], up_far_d
    )
    grad_d, above_d, norm_d = norm_backward(cot, back, beside(back), stream_d, norms[0, 2])
    back_d, returned, d_joint_near, d_joint_far = cross_backward(
        info, joint_near, joint_far, above_d, cross_near, pack_far
    )
    returned_mine = lax.dynamic_slice_in_dim(returned, core * half, half, 0)
    returned_theirs = lax.dynamic_slice_in_dim(returned, (1 - core) * half, half, 0)
    returned = returned_mine.astype(F32) + beside(returned_theirs).astype(F32)
    returned = returned.astype(BF)
    returned_near = to_encoder(returned)
    returned_far = beside(returned_near)

    grad_two, above_feed, norm_grad_three, back, hidden_near, hidden_far = lax.cond(
        decoder,
        lambda: (grad_d, cot, norm_d, back_d, hidden_d_near, hidden_d_far),
        lambda: source_back(
            info,
            cot,
            returned_near,
            returned_far,
            stream_e,
            norms[0, 2],
            slope_near,
            slope_far,
            feed_near,
            feed_far_e,
        ),
    )
    down_near, down_far = lax.cond(
        decoder,
        lambda: feed_weights(active_d_near, active_d_far, above_feed, above_feed),
        lambda: feed_weights(active_e_near, active_e_far, above_feed, above_feed),
    )
    down_other = across(down_far)
    grad_one, above_one, norm_grad_two = norm_backward(
        grad_two, back, beside(back), stream_one, norms[0, 1]
    )
    up_near, up_far = lax.cond(
        decoder,
        lambda: feed_weights(normed_three, normed_three, hidden_near, hidden_far),
        lambda: feed_weights(normed_two, normed_two, hidden_near, hidden_far),
    )
    up_other = across(up_far)

    back, attn_far, spread_far = self_backward(
        info, saved_far, after(above_one, up_far), normed_one, self_far, table_far, None, BF
    )
    pair_near, pair_far = cross_weights(
        info,
        d_joint_near,
        d_joint_far,
        joint_near[1],
        joint_far[1],
        normed_two,
        after(above_d, attn_far),
        sent_near,
        sent_far,
    )
    attn_other = across(attn_far)
    d_down = Line(near_added(down_near, after(down_other, attn_far)))
    above_near = after(above_one, d_down.value)
    back, attn_near, spread_near = self_backward(
        info, saved_near, above_near, normed_one, self_near, table_near, back, F32
    )

    d_down.inward(attn_near)
    d_up = Line(near_added(up_near, after(up_other, attn_near)))
    d_up.inward()
    d_down.swap()
    d_attn = Line(near_added(attn_near, after(attn_other, d_down.value)))
    d_attn.inward()
    d_up.value = after(d_up.value, d_down.value)
    d_up.swap()
    grad_rows, _, norm_grad_one = norm_backward(grad_one, back, beside(back), rows, norms[0, 0])
    d_ffn_out = d_down.total()
    d_attn.swap()
    d_pair = (pair_near + across_in(pair_far, DECODER).astype(F32)).astype(BF)
    d_source = to_encoder(d_pair[2:])
    d_pair = Line(after(jnp.where(decoder, d_pair[:2], d_source), d_up.value))
    d_ffn_in = d_up.total()
    reached = d_attn.value
    d_attn = d_attn.total()
    d_pair = d_pair.total()

    part_d = feed_value(
        info, after(active_d_near, hidden_near), active_d_far, ffn_out[0], pack_far
    )
    result, squares = finish(info, stream_d, part_d, beside(part_d), sent, squares)

    def placed(value):
        mine = lax.dynamic_slice_in_dim(value, tensor * quarter, quarter, 0)
        theirs = lax.dynamic_slice_in_dim(value, (tensor ^ 2) * quarter, quarter, 0)
        other = across(theirs.astype(BF)).astype(value.dtype)
        stacked = jnp.where(pair == 0, jnp.stack([mine, other]), jnp.stack([other, mine]))
        return stacked[None, :, None]

    spreads = jnp.concatenate([spread_near, spread_far])
    d_table = lax.dot_general(
        one_hot, spreads, NT, precision=HIGHEST, preferred_element_type=F32
    )
    def table_rows(value):
        rows_used = -(-buckets * heads // model)
        padded = jnp.pad(value.reshape(-1), (0, rows_used * model - buckets * heads))
        return padded.reshape(rows_used, model)

    shared = jnp.concatenate(
        [
            norm_grad_one,
            norm_grad_two,
            norm_grad_three,
            jnp.broadcast_to(squares[:1, :1], (1, model)),
            jnp.broadcast_to(own_length.astype(F32), (1, model)),
        ]
    )
    small = jnp.concatenate([shared, table_rows(d_table[:, :heads])])
    small = small + across(jnp.concatenate([shared, table_rows(d_table[:, heads:])]))
    small = Line(after(small, reached)).total()
    d_table = small[8:].reshape(-1)[: buckets * heads].reshape(buckets, heads)
    stats = jnp.sqrt(small[6, :1] / (small[7, :1] * model))
    return (
        placed(result),
        placed(grad_rows),
        d_table[None],
        small[:6].reshape(1, 3, 2, model),
        jnp.swapaxes(d_attn[:3], 1, 2)[None],
        d_attn[3][None],
        jnp.swapaxes(d_pair, 1, 2)[None],
        d_ffn_in[None],
        d_ffn_out[None],
        stats,
    )


def solution(mesh):
    in_specs = (
        P("section", None, "dp", "tensor", None),
        P(None, None, "dp"),
        P("section", None),
        P("section", None, "tensor"),
        P("section", None, None, None),
        P("section", None, None, "tensor"),
        P("section", "tensor", None),
        P("section", None, None, "tensor"),
        P("section", None, "tensor"),
        P("section", "tensor", None),
        P("section", None, "dp", "tensor", None),
    )
    out_specs = (
        P("section", None, "dp", "tensor", None),
        P("section", None, "dp", "tensor", None),
        P("section", None, "tensor"),
        P("section", None, None, None),
        P("section", None, None, "tensor"),
        P("section", "tensor", None),
        P("section", None, None, "tensor"),
        P("section", None, "tensor"),
        P("section", "tensor", None),
        P("section"),
    )
    return jax.shard_map(body, mesh=mesh, in_specs=in_specs, out_specs=out_specs, check_vma=False)
```

```python
import functools
import math

import jax
import jax.numpy as jnp
from jax import lax
from jax.experimental import pallas as pl
from jax.experimental.pallas import tpu as pltpu
from jax.sharding import PartitionSpec as P

HEAD_DIM = 64
SCALE = HEAD_DIM ** (-0.5)
EPSILON = 1e-05
MASKED = -1000000000.0
HIGHEST = lax.Precision.HIGHEST
BF = jnp.bfloat16
F32 = jnp.float32
NN = (((1,), (0,)), ((), ()))
NT = (((1,), (1,)), ((), ()))
TN = (((0,), (0,)), ((), ()))
TILE = 256
BAND = 128
ENCODER, DECODER = 0, 1
ROLE, OWN_LEN, SOURCE_LEN, CORE, START = 0, 1, 2, 3, 4
HIDES_LITTLE = 0.02
HIDES_MUCH = 2.0


def mm(left, right, dims):
    return lax.dot_general(left, right, dims, preferred_element_type=F32)


def whole():
    return pl.BlockSpec(memory_space=pltpu.VMEM)


def scalars():
    return pl.BlockSpec(memory_space=pltpu.SMEM)


def shape(dims, dtype):
    return jax.ShapeDtypeStruct(dims, dtype)


def cost(flops, nbytes, weight=HIDES_LITTLE):
    return pl.CostEstimate(
        flops=int(flops * weight), bytes_accessed=int(nbytes * weight), transcendentals=0
    )


def params(megabytes=28):
    return pltpu.CompilerParams(vmem_limit_bytes=megabytes * 1024 * 1024)


def norm_of(values, norm_ref):
    centred = values - jnp.mean(values, -1, keepdims=True)
    factor = lax.rsqrt(jnp.mean(centred * centred, -1, keepdims=True) + EPSILON)
    return centred * factor * norm_ref[0:1, :] + norm_ref[1:2, :]


def enter_kernel(info, mine, core_mine, far, core_far, norm_ref, rows_ref, normed_ref):
    quarter = mine.shape[0]
    for step, piece in enumerate((mine, core_mine, far, core_far)):
        start = pl.multiple_of(info[START + step], quarter)
        values = piece[...]
        rows_ref[pl.ds(start, quarter), :] = values
        normed_ref[pl.ds(start, quarter), :] = norm_of(values.astype(F32), norm_ref).astype(BF)


def enter(info, pieces, norm):
    quarter, width = pieces[0].shape
    out = shape((4 * quarter, width), BF)
    return pl.pallas_call(
        enter_kernel,
        out_shape=(out, out),
        in_specs=[scalars()] + [whole()] * 5,
        out_specs=(whole(), whole()),
        compiler_params=params(),
        cost_estimate=cost(16 * quarter * width * 4, quarter * width * 24),
    )(info, *pieces, norm)


def masked_kernel(info, mine, core_mine, far, core_far, rows_ref):
    quarter = mine.shape[0]
    for step, piece in enumerate((mine, core_mine, far, core_far)):
        start = pl.multiple_of(info[START + step], quarter)
        row = start + lax.broadcasted_iota(jnp.int32, (quarter, 1), 0)
        values = jnp.where(row < info[OWN_LEN], piece[...].astype(F32), 0.0)
        rows_ref[pl.ds(start, quarter), :] = values.astype(BF)


def masked_rows(info, pieces):
    quarter, width = pieces[0].shape
    return pl.pallas_call(
        masked_kernel,
        out_shape=shape((4 * quarter, width), BF),
        in_specs=[scalars()] + [whole()] * 4,
        out_specs=whole(),
        compiler_params=params(),
        cost_estimate=cost(quarter * width * 8, quarter * width * 16),
    )(info, *pieces)


def skew_kernel(distance_ref, table_ref):
    width = table_ref.shape[2]
    for head in range(distance_ref.shape[0]):
        row = jnp.broadcast_to(distance_ref[head : head + 1, :], (BAND, width))
        table_ref[head] = pltpu.roll(row, width - (BAND - 1), 1, stride=1, stride_axis=0)


def skew(distances):
    heads, width = distances.shape
    return pl.pallas_call(
        skew_kernel,
        out_shape=shape((heads, BAND, width), F32),
        in_specs=[whole()],
        out_specs=whole(),
        compiler_params=params(),
        cost_estimate=cost(heads * BAND * width, heads * BAND * width * 4),
    )(distances)


def unskewed(band):
    rows, width = band.shape
    while rows > 8:
        rows //= 2
        band = pltpu.roll(band[:rows], rows, 1) + band[rows:]
    amount = (rows - 1) - lax.broadcasted_iota(jnp.int32, (rows, width), 0)
    for bit in range(3):
        band = jnp.where(((amount >> bit) & 1) == 1, pltpu.roll(band, 1 << bit, 1), band)
    return jnp.sum(band, 0, keepdims=True)


def by_blocks(count, body):
    def step(index, carry):
        body(pl.ds(pl.multiple_of(index * TILE, TILE), TILE))
        return carry

    lax.fori_loop(0, count // TILE, step, 0)


def head_span(head):
    return slice(head * HEAD_DIM, (head + 1) * HEAD_DIM)


def allowed_keys(info, length, causal, length_at):
    key = lax.broadcasted_iota(jnp.int32, (length, length), 0)
    last = info[length_at] - 1
    if not causal:
        return key <= last
    query = lax.broadcasted_iota(jnp.int32, (1, length), 1)
    free = jnp.where(info[ROLE] == DECODER, 0, 1 << 20)
    return key <= jnp.minimum(query + free, last)


def scores_of(queries, keys, allowed, table_ref, head):
    scores = mm(keys, queries, TN)
    if table_ref is not None:
        length = scores.shape[0]
        starts = range(length - BAND, -BAND, -BAND)
        bands = [table_ref[head, :, start : start + length] for start in starts]
        scores = scores + jnp.concatenate(bands, 0)
    return jnp.where(allowed, scores, MASKED)


def attend(info, qkv_ref, table_ref, out_ref, lse_ref, length_at):
    width, length = out_ref.shape
    allowed = allowed_keys(info, length, table_ref is not None, length_at)
    for head in range(width // HEAD_DIM):
        span = head_span(head)
        queries = qkv_ref[0, span, :] * jnp.asarray(SCALE, BF)
        scores = scores_of(queries, qkv_ref[1, span, :], allowed, table_ref, head)
        peak = jnp.max(scores, 0, keepdims=True)
        lifted = jnp.exp(scores - peak)
        total = jnp.sum(lifted, 0, keepdims=True)
        mixed = mm(qkv_ref[2, span, :], lifted.astype(BF), NN)
        out_ref[span, :] = mixed / total
        lse_ref[head : head + 1, :] = peak + jnp.log(total)


def self_forward_kernel(has_sum, info, normed, weights, table, *refs):
    previous = refs[0] if has_sum else None
    sum_ref, qkv_ref, out_ref, lse_ref = refs[1 if has_sum else 0 :]
    length = out_ref.shape[1]

    def inputs(cols):
        block = normed[cols, :]
        for place in range(3):
            qkv_ref[place, :, cols] = mm(weights[place], block, NT).astype(BF)

    by_blocks(length, inputs)
    attend(info, qkv_ref, table, out_ref, lse_ref, OWN_LEN)

    def outputs(cols):
        value = mm(out_ref[:, cols].astype(BF), weights[3], TN)
        if has_sum:
            value = value + previous[cols, :]
        sum_ref[cols, :] = value.astype(sum_ref.dtype)

    by_blocks(length, outputs)


def attention_cost(length, width, model, matmuls, projections, weight=HIDES_LITTLE):
    heads = width // HEAD_DIM
    return cost(
        heads * length * length * HEAD_DIM * 2 * matmuls * 4 + projections * 2 * length * model * width,
        length * model * 8,
        weight,
    )


def saved_shapes(length, width):
    return (shape((3, width, length), BF), shape((width, length), F32), shape((8, length), F32))


def self_forward(info, normed, weights, table, previous):
    length, model = normed.shape
    width = weights.shape[1]
    has_sum = previous is not None
    operands = [info, normed, weights, table] + ([previous] if has_sum else [])
    return pl.pallas_call(
        functools.partial(self_forward_kernel, has_sum),
        out_shape=(shape((length, model), BF if has_sum else F32),) + saved_shapes(length, width),
        in_specs=[scalars()] + [whole()] * (len(operands) - 1),
        out_specs=(whole(),) * 4,
        compiler_params=params(),
        cost_estimate=attention_cost(length, width, model, 2, 4, HIDES_MUCH),
    )(*operands)


def rows_of(ref, place, width):
    return ref[place * width : (place + 1) * width, :]


def cross_forward_kernel(info, normed, near, far, weights_near, weights_far, *refs):
    sum_ref = refs[0]
    length, width = normed.shape[0], weights_near.shape[0] // 4
    half = near.shape[0]
    sides = ((weights_near, refs[1:4]), (weights_far, refs[4:7]))

    @pl.when(info[ROLE] == DECODER)
    def _():
        for weights, (qkv_ref, out_ref, lse_ref) in sides:

            def queries(cols, weights=weights, qkv_ref=qkv_ref):
                qkv_ref[0, :, cols] = mm(rows_of(weights, 0, width), normed[cols, :], NT).astype(BF)

            by_blocks(length, queries)
            for piece, side in ((near, info[CORE]), (far, 1 - info[CORE])):
                base = side * half

                def sources(index, carry, piece=piece, base=base, weights=weights, qkv_ref=qkv_ref):
                    local = pl.multiple_of(index * TILE, TILE)
                    block = piece[pl.ds(local, TILE), :]
                    cols = pl.ds(pl.multiple_of(base + local, TILE), TILE)
                    for place in (1, 2):
                        qkv_ref[place, :, cols] = mm(rows_of(weights, 1 + place, width), block, NT).astype(BF)
                    return carry

                lax.fori_loop(0, half // TILE, sources, 0)
            attend(info, qkv_ref, None, out_ref, lse_ref, SOURCE_LEN)

        def outputs(cols):
            value = mm(refs[2][:, cols].astype(BF), rows_of(weights_near, 1, width), TN)
            value = value + mm(refs[5][:, cols].astype(BF), rows_of(weights_far, 1, width), TN)
            sum_ref[cols, :] = value.astype(sum_ref.dtype)

        by_blocks(length, outputs)


def cross_forward(info, normed, near, far, weights_near, weights_far):
    length, model = normed.shape
    width = weights_near.shape[0] // 4
    saved = saved_shapes(length, width)
    results = pl.pallas_call(
        cross_forward_kernel,
        out_shape=(shape((length, model), BF),) + saved + saved,
        in_specs=[scalars()] + [whole()] * 5,
        out_specs=(whole(),) * 7,
        compiler_params=params(),
        cost_estimate=attention_cost(length, 2 * width, model, 2, 4),
    )(info, normed, near, far, weights_near, weights_far)
    return results[0], results[1:4], results[4:7]


def attend_back(info, saved, table_ref, upstream, grads_ref, band, length_at):
    qkv_ref, out_ref, lse_ref = saved
    width, length = out_ref.shape
    allowed = allowed_keys(info, length, table_ref is not None, length_at)
    if table_ref is not None:
        band[...] = jnp.zeros_like(band)
    for head in range(width // HEAD_DIM):
        span = head_span(head)
        queries = qkv_ref[0, span, :] * jnp.asarray(SCALE, BF)
        keys, above = qkv_ref[1, span, :], upstream[span, :]
        scores = scores_of(queries, keys, allowed, table_ref, head)
        probs = jnp.exp(scores - lse_ref[head : head + 1, :])
        inner = jnp.sum(above.astype(F32) * out_ref[span, :], 0, keepdims=True)
        d_scores = probs * (mm(qkv_ref[2, span, :], above, TN) - inner)
        low = d_scores.astype(BF)
        grads_ref[0, span, :] = (mm(keys, low, NN) * SCALE).astype(BF)
        grads_ref[1, span, :] = mm(queries, low, NT).astype(BF)
        grads_ref[2, span, :] = mm(above, probs.astype(BF), NT).astype(BF)
        if table_ref is not None:
            for part in range(length // BAND):
                start = length - BAND - part * BAND
                rows = slice(part * BAND, (part + 1) * BAND)
                band[head, :, start : start + length] += d_scores[rows, :]


def self_backward_kernel(has_sum, info, qkv, out, lse, above, normed, weights, table, *refs):
    previous = refs[0] if has_sum else None
    refs = refs[1 if has_sum else 0 :]
    sum_ref, weight_ref, spread_ref, upstream = refs[:4]
    band, grads_ref = refs[4:6]
    length = above.shape[0]

    def entering(cols):
        upstream[:, cols] = mm(weights[3], above[cols, :], NT).astype(BF)

    by_blocks(length, entering)
    attend_back(info, (qkv, out, lse), table, upstream, grads_ref, band, OWN_LEN)

    def leaving(cols):
        value = mm(grads_ref[0, :, cols], weights[0], TN)
        for place in (1, 2):
            value = value + mm(grads_ref[place, :, cols], weights[place], TN)
        if has_sum:
            value = value + previous[cols, :]
        sum_ref[cols, :] = value.astype(sum_ref.dtype)

    by_blocks(length, leaving)
    for place in range(3):
        weight_ref[place] = mm(grads_ref[place], normed[...], NN).astype(weight_ref.dtype)
    weight_ref[3] = mm(out[...].astype(BF), above[...], NN).astype(weight_ref.dtype)
    for head in range(table.shape[0]):
        spread_ref[head : head + 1, :] = unskewed(band[head])


def self_backward(info, saved, above, normed, weights, table, previous, weight_type, hides):
    length, model = above.shape
    width = weights.shape[1]
    has_sum = previous is not None
    operands = [info, *saved, above, normed, weights, table] + ([previous] if has_sum else [])
    return pl.pallas_call(
        functools.partial(self_backward_kernel, has_sum),
        out_shape=(
            shape((length, model), BF if has_sum else F32),
            shape((4, width, model), weight_type),
            shape((table.shape[0], table.shape[2]), F32),
        ),
        in_specs=[scalars()] + [whole()] * (len(operands) - 1),
        out_specs=(whole(),) * 3,
        scratch_shapes=[
            pltpu.VMEM((width, length), BF),
            pltpu.VMEM(table.shape, F32),
            pltpu.VMEM((3, width, length), BF),
        ],
        compiler_params=params(),
        cost_estimate=attention_cost(length, width, model, 5, 8, hides),
    )(*operands)


def cross_backward_kernel(info, *refs):
    saved_near, saved_far, (above, weights_near, weights_far) = refs[:3], refs[3:6], refs[6:9]
    sum_ref, source_ref, grads_near, grads_far, upstream = refs[9:14]
    length, width = above.shape[0], weights_near.shape[0] // 4

    @pl.when(info[ROLE] == DECODER)
    def _():
        for saved, weights, grads_ref in (
            (saved_near, weights_near, grads_near),
            (saved_far, weights_far, grads_far),
        ):

            def entering(cols, weights=weights):
                upstream[:, cols] = mm(rows_of(weights, 1, width), above[cols, :], NT).astype(BF)

            by_blocks(length, entering)
            attend_back(info, saved, None, upstream, grads_ref, None, SOURCE_LEN)

        def leaving(cols):
            value = mm(grads_near[0, :, cols], rows_of(weights_near, 0, width), TN)
            value = value + mm(grads_far[0, :, cols], rows_of(weights_far, 0, width), TN)
            sum_ref[cols, :] = value.astype(BF)
            source = None
            for grads_ref, weights in ((grads_near, weights_near), (grads_far, weights_far)):
                for place in (1, 2):
                    term = mm(grads_ref[place, :, cols], rows_of(weights, 1 + place, width), TN)
                    source = term if source is None else source + term
            source_ref[cols, :] = source.astype(BF)

        by_blocks(length, leaving)


def cross_backward(info, saved_near, saved_far, above, weights_near, weights_far):
    length, model = above.shape
    width = weights_near.shape[0] // 4
    out, grads = shape((length, model), BF), shape((3, width, length), BF)
    return pl.pallas_call(
        cross_backward_kernel,
        out_shape=(out, out, grads, grads),
        in_specs=[scalars()] + [whole()] * 9,
        out_specs=(whole(),) * 4,
        scratch_shapes=[pltpu.VMEM((width, length), BF)],
        compiler_params=params(),
        cost_estimate=attention_cost(length, 2 * width, model, 5, 4),
    )(info, *saved_near, *saved_far, above, weights_near, weights_far)


def cross_weights_kernel(info, grads_near, grads_far, out_near, out_far, normed, above, *refs):
    near, far, weight_near, weight_far = refs
    half = near.shape[0]

    @pl.when(info[ROLE] == DECODER)
    def _():
        start = pl.multiple_of(info[CORE] * half, half)
        other = pl.multiple_of((1 - info[CORE]) * half, half)
        for grads, out, target in (
            (grads_near, out_near, weight_near),
            (grads_far, out_far, weight_far),
        ):
            target[0] = mm(grads[0], normed[...], NN).astype(target.dtype)
            target[1] = mm(out[...].astype(BF), above[...], NN).astype(target.dtype)
            for place in (1, 2):
                value = mm(grads[place, :, pl.ds(start, half)], near[...], NN)
                value = value + mm(grads[place, :, pl.ds(other, half)], far[...], NN)
                target[1 + place] = value.astype(target.dtype)


def cross_weights(info, grads_near, grads_far, out_near, out_far, normed, above, near, far):
    length, model = above.shape
    width = out_near.shape[0]
    return pl.pallas_call(
        cross_weights_kernel,
        out_shape=(shape((4, width, model), F32), shape((4, width, model), BF)),
        in_specs=[scalars()] + [whole()] * 8,
        out_specs=(whole(),) * 2,
        compiler_params=params(),
        cost_estimate=cost(16 * length * model * width, length * model * 16),
    )(info, grads_near, grads_far, out_near, out_far, normed, above, near, far)


def row_spec(width):
    return pl.BlockSpec((TILE, width), lambda index: (index, 0))


def pack_spec(place, width):
    return pl.BlockSpec((width, width), lambda index: (place, 0))


def fixed_spec(dims):
    return pl.BlockSpec(dims, lambda index: (0,) * len(dims))


def add_norm_kernel(stream, near, far, norm_ref, sum_ref, normed_ref):
    value = stream[...].astype(F32) + (near[...].astype(F32) + far[...].astype(F32))
    sum_ref[...] = value
    normed_ref[...] = norm_of(value, norm_ref).astype(BF)


def add_norm(stream, near, far, norm):
    length, model = stream.shape
    return pl.pallas_call(
        add_norm_kernel,
        grid=(length // TILE,),
        out_shape=(shape((length, model), F32), shape((length, model), BF)),
        in_specs=[row_spec(model)] * 3 + [fixed_spec((2, model))],
        out_specs=(row_spec(model),) * 2,
        compiler_params=params(),
        cost_estimate=cost(length * model * 12, length * model * 14),
    )(stream, near, far, norm)


def row_mask(info, index, at):
    row = index * TILE + lax.broadcasted_iota(jnp.int32, (TILE, 1), 0)
    return row < info[at]


def squares_of(value):
    return jnp.sum(jnp.sum(value * value, 0, keepdims=True), 1, keepdims=True)


def source_kernel(info, stream, near, far, norm_ref, sum_ref, sent_ref, square_ref):
    index = pl.program_id(0)
    value = stream[...] + (near[...].astype(F32) + far[...].astype(F32))
    sum_ref[...] = value
    result = jnp.where(row_mask(info, index, OWN_LEN), norm_of(value, norm_ref), 0.0)
    sent_ref[...] = result.astype(BF)

    @pl.when(index == 0)
    def _():
        square_ref[...] = jnp.zeros_like(square_ref)

    square_ref[...] += squares_of(result)


def source_out(info, stream, near, far, norm):
    length, model = stream.shape
    return pl.pallas_call(
        source_kernel,
        grid=(length // TILE,),
        out_shape=(shape((length, model), F32), shape((length, model), BF), shape((8, 128), F32)),
        in_specs=[scalars()] + [row_spec(model)] * 3 + [fixed_spec((2, model))],
        out_specs=(row_spec(model), row_spec(model), fixed_spec((8, 128))),
        compiler_params=params(),
        cost_estimate=cost(length * model * 14, length * model * 14),
    )(info, stream, near, far, norm)


def finish_kernel(info, stream, near, far, sent, square, out_ref, square_ref):
    index = pl.program_id(0)

    @pl.when(info[ROLE] == DECODER)
    def _():
        value = stream[...] + (near[...].astype(F32) + far[...].astype(F32))
        value = jnp.where(row_mask(info, index, OWN_LEN), value, 0.0)
        out_ref[...] = value.astype(BF)

        @pl.when(index == 0)
        def _():
            square_ref[...] = jnp.zeros_like(square_ref)

        square_ref[...] += squares_of(value)

    @pl.when(info[ROLE] == ENCODER)
    def _():
        out_ref[...] = sent[...]
        square_ref[...] = square[...]


def finish(info, stream, near, far, sent, square):
    length, model = stream.shape
    return pl.pallas_call(
        finish_kernel,
        grid=(length // TILE,),
        out_shape=(shape((length, model), BF), shape((8, 128), F32)),
        in_specs=[scalars()] + [row_spec(model)] * 4 + [fixed_spec((8, 128))],
        out_specs=(row_spec(model), fixed_spec((8, 128))),
        compiler_params=params(),
        cost_estimate=cost(length * model * 6, length * model * 12),
    )(info, stream, near, far, sent, square)


def norm_back(upstream, values, norm_ref):
    centred = values - jnp.mean(values, -1, keepdims=True)
    factor = lax.rsqrt(jnp.mean(centred * centred, -1, keepdims=True) + EPSILON)
    unit = centred * factor
    scaled = upstream * norm_ref[0:1, :]
    inner = scaled - jnp.mean(scaled, -1, keepdims=True)
    inner = inner - unit * jnp.mean(scaled * unit, -1, keepdims=True)
    gain = jnp.sum(upstream * unit, 0, keepdims=True)
    shift = jnp.sum(upstream, 0, keepdims=True)
    return factor * inner, gain, shift


def norm_back_kernel(residual, near, far, values, norm_ref, grad_ref, low_ref, norm_grad_ref):
    upstream = near[...].astype(F32) + far[...].astype(F32)
    grad, gain, shift = norm_back(upstream, values[...].astype(F32), norm_ref)
    grad = residual[...].astype(F32) + grad
    grad_ref[...] = grad
    low_ref[...] = grad.astype(BF)

    @pl.when(pl.program_id(0) == 0)
    def _():
        norm_grad_ref[...] = jnp.zeros_like(norm_grad_ref)

    norm_grad_ref[0:1, :] += gain
    norm_grad_ref[1:2, :] += shift


def norm_backward(residual, near, far, values, norm):
    length, model = values.shape
    return pl.pallas_call(
        norm_back_kernel,
        grid=(length // TILE,),
        out_shape=(shape((length, model), F32), shape((length, model), BF), shape((2, model), F32)),
        in_specs=[row_spec(model)] * 4 + [fixed_spec((2, model))],
        out_specs=(row_spec(model), row_spec(model), fixed_spec((2, model))),
        compiler_params=params(),
        cost_estimate=cost(length * model * 20, length * model * 18),
    )(residual, near, far, values, norm)


def gelu_parts(hidden):
    half = 0.5 * (1.0 + lax.erf(hidden * math.sqrt(0.5)))
    slope = half + hidden * jnp.exp(-0.5 * hidden * hidden) * (1.0 / math.sqrt(2.0 * math.pi))
    return hidden * half, slope


def feed_forward_kernel(has_sum, info, normed, pack, *refs):
    previous = refs[0] if has_sum else None
    sum_ref, active_ref, slope_ref = refs[1 if has_sum else 0 :]

    @pl.when(info[ROLE] == ENCODER)
    def _():
        active, slope = gelu_parts(mm(normed[...], pack[0], NN))
        active = active.astype(BF)
        active_ref[...] = active
        slope_ref[...] = slope.astype(BF)
        value = mm(active, pack[1], NN)
        if has_sum:
            value = value + previous[...]
        sum_ref[...] = value.astype(sum_ref.dtype)


def feed_forward(info, normed, pack, previous):
    length, model = normed.shape
    hidden = pack.shape[2]
    has_sum = previous is not None
    operands = [info, normed, pack] + ([previous] if has_sum else [])
    return pl.pallas_call(
        functools.partial(feed_forward_kernel, has_sum),
        grid=(length // TILE,),
        out_shape=(
            shape((length, model), BF if has_sum else F32),
            shape((length, hidden), BF),
            shape((length, hidden), BF),
        ),
        in_specs=[scalars(), row_spec(model), fixed_spec(pack.shape)]
        + ([row_spec(model)] if has_sum else []),
        out_specs=(row_spec(model), row_spec(hidden), row_spec(hidden)),
        compiler_params=params(),
        cost_estimate=cost(4 * length * model * hidden, length * model * 12),
    )(*operands)


def feed_above_kernel(info, cot, down_near, down_far, near_ref, far_ref):
    @pl.when(info[ROLE] == DECODER)
    def _():
        near_ref[...] = mm(cot[...], down_near[...], NT)
        far_ref[...] = mm(cot[...], down_far[...], NT)


def feed_above(info, cot, down_near, down_far):
    length, model = cot.shape
    hidden = down_near.shape[0]
    unit = shape((length, hidden), F32)
    return pl.pallas_call(
        feed_above_kernel,
        grid=(length // TILE,),
        out_shape=(unit, unit),
        in_specs=[
            scalars(),
            row_spec(model),
            fixed_spec(down_near.shape),
            pack_spec(1, model),
        ],
        out_specs=(row_spec(hidden),) * 2,
        compiler_params=params(),
        cost_estimate=cost(4 * length * model * hidden, length * model * 10),
    )(info, cot, down_near, down_far)


def feed_both_kernel(info, normed, above_near, above_far, up_near, up_far, back_ref, *refs):
    @pl.when(info[ROLE] == DECODER)
    def _():
        back = None
        for up, above, active_ref, grad_ref in (
            (up_near, above_near, *refs[0:2]),
            (up_far, above_far, *refs[2:4]),
        ):
            active, slope = gelu_parts(mm(normed[...], up[...], NN))
            active_ref[...] = active.astype(BF)
            grad = (above[...] * slope).astype(BF)
            grad_ref[...] = grad
            term = mm(grad, up[...], NT)
            back = term if back is None else back + term
        back_ref[...] = back.astype(BF)


def feed_both(info, normed, above, up_near, up_far):
    length, model = normed.shape
    hidden = up_near.shape[1]
    out, unit = shape((length, model), BF), shape((length, hidden), BF)
    return pl.pallas_call(
        feed_both_kernel,
        grid=(length // TILE,),
        out_shape=(out, unit, unit, unit, unit),
        in_specs=[
            scalars(),
            row_spec(model),
            row_spec(hidden),
            row_spec(hidden),
            fixed_spec(up_near.shape),
            fixed_spec(up_far.shape),
        ],
        out_specs=(row_spec(model),) + (row_spec(hidden),) * 4,
        compiler_params=params(),
        cost_estimate=cost(8 * length * model * hidden, length * model * 20),
    )(info, normed, *above, up_near, up_far)


def feed_value_kernel(info, active_near, active_far, down_near, down_far, sum_ref):
    @pl.when(info[ROLE] == DECODER)
    def _():
        value = mm(active_near[...], down_near[...], NN) + mm(active_far[...], down_far[...], NN)
        sum_ref[...] = value.astype(BF)


def feed_value(info, active_near, active_far, down_near, down_far):
    length, hidden = active_near.shape
    model = down_near.shape[1]
    return pl.pallas_call(
        feed_value_kernel,
        grid=(length // TILE,),
        out_shape=shape((length, model), BF),
        in_specs=[
            scalars(),
            row_spec(hidden),
            row_spec(hidden),
            fixed_spec(down_near.shape),
            pack_spec(1, model),
        ],
        out_specs=row_spec(model),
        compiler_params=params(),
        cost_estimate=cost(4 * length * model * hidden, length * model * 6),
    )(info, active_near, active_far, down_near, down_far)


def source_back_kernel(info, cot, near, far, values, norm_ref, *refs):
    slope_near, slope_far, pack_near, pack_far, grad_ref, low_ref, norm_grad_ref = refs[:7]
    back_ref, hidden_near, hidden_far = refs[7:]
    index = pl.program_id(0)
    blocks = near.shape[0] // TILE
    rows = pl.ds(pl.multiple_of(lax.rem(index, blocks) * TILE, TILE), TILE)
    mine = (index >= blocks).astype(jnp.int32) == info[CORE]
    returned = jnp.where(mine, near[rows, :].astype(F32), far[rows, :].astype(F32))
    upstream = cot[...].astype(F32) + returned
    upstream = jnp.where(row_mask(info, index, OWN_LEN), upstream, 0.0)
    grad, gain, shift = norm_back(upstream, values[...], norm_ref)
    low = grad.astype(BF)
    grad_ref[...] = grad
    low_ref[...] = low

    @pl.when(index == 0)
    def _():
        norm_grad_ref[...] = jnp.zeros_like(norm_grad_ref)

    norm_grad_ref[0:1, :] += gain
    norm_grad_ref[1:2, :] += shift
    back = None
    for pack, slope, hidden_ref in (
        (pack_near, slope_near, hidden_near),
        (pack_far, slope_far, hidden_far),
    ):
        hidden = (mm(low, pack[1], NT) * slope[...].astype(F32)).astype(BF)
        hidden_ref[...] = hidden
        term = mm(hidden, pack[0], NT)
        back = term if back is None else back + term
    back_ref[...] = back.astype(BF)


def source_back(info, cot, near, far, values, norm, slope_near, slope_far, pack_near, pack_far):
    length, model = values.shape
    hidden = pack_near.shape[2]
    unit = shape((length, hidden), BF)
    return pl.pallas_call(
        source_back_kernel,
        grid=(length // TILE,),
        out_shape=(
            shape((length, model), F32),
            shape((length, model), BF),
            shape((2, model), F32),
            shape((length, model), BF),
            unit,
            unit,
        ),
        in_specs=[
            scalars(),
            row_spec(model),
            fixed_spec(near.shape),
            fixed_spec(far.shape),
            row_spec(model),
            fixed_spec((2, model)),
            row_spec(hidden),
            row_spec(hidden),
            fixed_spec(pack_near.shape),
            fixed_spec(pack_far.shape),
        ],
        out_specs=(
            row_spec(model),
            row_spec(model),
            fixed_spec((2, model)),
            row_spec(model),
            row_spec(hidden),
            row_spec(hidden),
        ),
        compiler_params=params(),
        cost_estimate=cost(8 * length * model * hidden, length * model * 30),
    )(info, cot, near, far, values, norm, slope_near, slope_far, pack_near, pack_far)


def product_kernel(left_near, left_far, right_near, right_far, near_ref, far_ref):
    near_ref[...] = mm(left_near[...], right_near[...], TN)
    far_ref[...] = mm(left_far[...], right_far[...], TN).astype(BF)


def feed_weights(left_near, left_far, right_near, right_far):
    length, rows = left_near.shape
    columns = right_near.shape[1]
    left = pl.BlockSpec((length, TILE), lambda index: (0, index))
    right = pl.BlockSpec((length, columns), lambda index: (0, 0))
    out = row_spec(columns)
    return pl.pallas_call(
        product_kernel,
        grid=(rows // TILE,),
        out_shape=(shape((rows, columns), F32), shape((rows, columns), BF)),
        in_specs=[left, left, right, right],
        out_specs=(out, out),
        compiler_params=params(),
        cost_estimate=cost(4 * length * rows * columns, length * rows * 12),
    )(left_near, left_far, right_near, right_far)


def across(value):
    return lax.ppermute(value, "tensor", [(0, 2), (1, 3), (2, 0), (3, 1)])


def across_in(value, role):
    links = [(0, 2), (1, 3), (2, 0), (3, 1)]
    return lax.ppermute(
        value, ("section", "tensor"), [(role * 4 + a, role * 4 + b) for a, b in links]
    )


def beside(value):
    return lax.ppermute(value, "tensor", [(0, 1), (1, 0), (2, 3), (3, 2)])


def to_decoder(value):
    return lax.ppermute(value, "section", [(ENCODER, DECODER)])


def to_encoder(value):
    return lax.ppermute(value, "section", [(DECODER, ENCODER)])


class Line:
    def __init__(self, value):
        self.four = lax.axis_size("dp") == 4
        self.value = value
        self.done = 0

    def inward(self, behind=None):
        if self.four:
            arrived = lax.ppermute(self.value, "dp", [(0, 1), (3, 2)])
            self.value = self.value + (arrived if behind is None else after(arrived, behind))
        self.done = 1

    def swap(self):
        if self.four:
            self.value = self.value + lax.ppermute(self.value, "dp", [(1, 2), (2, 1)])
        self.done = 2

    def total(self):
        if not self.four:
            return lax.psum(self.value, "dp").astype(F32)
        if self.done < 1:
            self.inward()
        if self.done < 2:
            self.swap()
        place = lax.axis_index("dp")
        inner = (place == 1) | (place == 2)
        outward = lax.ppermute(self.value, "dp", [(1, 0), (2, 3)])
        return jnp.where(inner, self.value, outward).astype(F32)


def near_added(own, other):
    return (own + other.astype(F32)).astype(BF)


def after(value, done):
    return lax.optimization_barrier((value, done))[0]


def body(
    frames,
    lengths,
    bucket_of,
    rel_table,
    norms,
    attn_in,
    attn_out,
    cross_pair,
    ffn_in,
    ffn_out,
    cotangent,
):
    section = lax.axis_index("section")
    tensor = lax.axis_index("tensor")
    pair, core = tensor // 2, tensor % 2
    decoder = section == DECODER
    quarter, model = frames.shape[3], frames.shape[4]
    length = 4 * quarter
    half = length // 2
    width = attn_in.shape[3]
    heads = width // HEAD_DIM
    buckets = rel_table.shape[1]

    own_length = lengths[section, pair, 0]
    source_length = lengths[ENCODER, pair, 0]
    starts = [(tensor ^ step) * quarter for step in range(4)]
    info = jnp.stack([section, own_length, source_length, core] + starts).astype(jnp.int32)

    def pick(array, index):
        return lax.dynamic_index_in_dim(array[0, :, 0], index, 0, keepdims=False)

    self_near = jnp.concatenate([jnp.swapaxes(attn_in[0], 1, 2), attn_out[0][None]])
    feed_near = jnp.stack([ffn_in[0], ffn_out[0]])
    pair_own = jnp.swapaxes(cross_pair[0], 1, 2)
    frame_mine = pick(frames, pair)
    frame_far = across(pick(frames, 1 - pair))
    rel_far = across(rel_table[0])
    self_far = across(after(self_near, rel_far))
    pair_source = to_decoder(pair_own)
    feed_far_e = across_in(after(feed_near, frame_far), ENCODER)
    cross_near = jnp.concatenate([pair_own, pair_source]).reshape(4 * width, model)
    pack_near = jnp.concatenate([cross_near, ffn_out[0]])
    pack_far = across_in(after(pack_near, frame_far), DECODER)
    up_far_d = across_in(after(ffn_in[0], pack_far), DECODER)
    cot_mine, cot_other = pick(cotangent, pair), pick(cotangent, 1 - pair)

    def quarters(mine, far):
        both = beside(jnp.stack([mine, far]))
        return mine, both[0], far, both[1]

    buckets_here = jnp.pad(bucket_of[0][::-1], (0, 1), constant_values=-1)
    one_hot = (lax.broadcasted_iota(jnp.int32, (buckets, 2 * length), 0) == buckets_here[None]).astype(F32)
    distances = lax.dot_general(
        jnp.concatenate([rel_table[0], rel_far], 1),
        one_hot,
        TN,
        precision=HIGHEST,
        preferred_element_type=F32,
    )
    table_near = skew(distances[:heads])
    table_far = skew(distances[heads:])

    rows, normed_one = enter(info, quarters(frame_mine, frame_far), norms[0, 0])
    part, *saved_near = self_forward(info, normed_one, self_near, table_near, None)
    part, *saved_far = self_forward(
        info, normed_one, after(self_far, pack_near), table_far, part
    )
    stream_one, normed_two = add_norm(
        rows, part, beside(part), norms[0, 1]
    )

    part, active_e_near, slope_near = feed_forward(
        info, normed_two, feed_near, None
    )
    part, active_e_far, slope_far = feed_forward(
        info, normed_two, after(feed_far_e, pack_far), part
    )
    stream_e, sent, squares = source_out(
        info, stream_one, part, beside(part), norms[0, 2]
    )
    sent_near = to_decoder(lax.dynamic_slice_in_dim(sent, core * half, half, 0))
    sent_far = beside(sent_near)
    cot = masked_rows(info, quarters(cot_mine, across(after(cot_other, sent))))
    hidden_pre = feed_above(info, cot, ffn_out[0], pack_far)
    normed_cross = after(normed_two, (hidden_pre, up_far_d))

    part, joint_near, joint_far = cross_forward(
        info, normed_cross, sent_near, sent_far, cross_near, pack_far
    )
    stream_d, normed_three = add_norm(stream_one, part, beside(part), norms[0, 2])
    back, active_d_near, hidden_d_near, active_d_far, hidden_d_far = feed_both(
        info, normed_three, hidden_pre, ffn_in[0], up_far_d
    )
    grad_d, above_d, norm_d = norm_backward(cot, back, beside(back), stream_d, norms[0, 2])
    back_d, returned, d_joint_near, d_joint_far = cross_backward(
        info, joint_near, joint_far, above_d, cross_near, pack_far
    )
    returned_mine = lax.dynamic_slice_in_dim(returned, core * half, half, 0)
    returned_theirs = lax.dynamic_slice_in_dim(returned, (1 - core) * half, half, 0)
    returned = returned_mine.astype(F32) + beside(returned_theirs).astype(F32)
    returned = returned.astype(BF)
    returned_near = to_encoder(returned)
    returned_far = beside(returned_near)

    grad_two, above_feed, norm_grad_three, back, hidden_near, hidden_far = lax.cond(
        decoder,
        lambda: (grad_d, cot, norm_d, back_d, hidden_d_near, hidden_d_far),
        lambda: source_back(
            info,
            cot,
            returned_near,
            returned_far,
            stream_e,
            norms[0, 2],
            slope_near,
            slope_far,
            feed_near,
            feed_far_e,
        ),
    )
    down_near, down_far = lax.cond(
        decoder,
        lambda: feed_weights(active_d_near, active_d_far, above_feed, above_feed),
        lambda: feed_weights(active_e_near, active_e_far, above_feed, above_feed),
    )
    down_other = across(down_far)
    grad_one, above_one, norm_grad_two = norm_backward(
        grad_two, back, beside(back), stream_one, norms[0, 1]
    )
    up_near, up_far = lax.cond(
        decoder,
        lambda: feed_weights(normed_three, normed_three, hidden_near, hidden_far),
        lambda: feed_weights(normed_two, normed_two, hidden_near, hidden_far),
    )
    up_other = across(up_far)

    back, attn_far, spread_far = self_backward(
        info,
        saved_far,
        after(above_one, up_far),
        normed_one,
        self_far,
        table_far,
        None,
        BF,
        HIDES_MUCH,
    )
    pair_near, pair_far = cross_weights(
        info,
        d_joint_near,
        d_joint_far,
        joint_near[1],
        joint_far[1],
        normed_two,
        after(above_d, attn_far),
        sent_near,
        sent_far,
    )
    attn_other = across(attn_far)
    d_down = Line(near_added(down_near, after(down_other, attn_far)))
    above_near = after(above_one, d_down.value)
    back, attn_near, spread_near = self_backward(
        info, saved_near, above_near, normed_one, self_near, table_near, back, F32, HIDES_LITTLE
    )

    d_down.inward(attn_near)
    d_up = Line(near_added(up_near, after(up_other, attn_near)))
    d_up.inward()
    d_down.swap()
    d_attn = Line(near_added(attn_near, after(attn_other, d_down.value)))
    d_attn.inward()
    d_up.value = after(d_up.value, d_down.value)
    d_up.swap()
    grad_rows, _, norm_grad_one = norm_backward(grad_one, back, beside(back), rows, norms[0, 0])
    d_ffn_out = d_down.total()
    d_attn.value = after(d_attn.value, d_ffn_out)
    d_attn.swap()
    d_pair = (pair_near + across_in(pair_far, DECODER).astype(F32)).astype(BF)
    d_source = to_encoder(d_pair[2:])
    d_pair = Line(after(jnp.where(decoder, d_pair[:2], d_source), d_up.value))
    d_ffn_in = d_up.total()
    reached = d_attn.value
    d_attn = d_attn.total()
    d_pair = d_pair.total()

    part_d = feed_value(
        info, after(active_d_near, hidden_near), active_d_far, ffn_out[0], pack_far
    )
    result, squares = finish(info, stream_d, part_d, beside(part_d), sent, squares)

    def placed(value):
        mine = lax.dynamic_slice_in_dim(value, tensor * quarter, quarter, 0)
        theirs = lax.dynamic_slice_in_dim(value, (tensor ^ 2) * quarter, quarter, 0)
        other = across(theirs.astype(BF)).astype(value.dtype)
        stacked = jnp.where(pair == 0, jnp.stack([mine, other]), jnp.stack([other, mine]))
        return stacked[None, :, None]

    spreads = jnp.concatenate([spread_near, spread_far])
    d_table = lax.dot_general(
        one_hot, spreads, NT, precision=HIGHEST, preferred_element_type=F32
    )
    def table_rows(value):
        rows_used = -(-buckets * heads // model)
        padded = jnp.pad(value.reshape(-1), (0, rows_used * model - buckets * heads))
        return padded.reshape(rows_used, model)

    shared = jnp.concatenate(
        [
            norm_grad_one,
            norm_grad_two,
            norm_grad_three,
            jnp.broadcast_to(squares[:1, :1], (1, model)),
            jnp.broadcast_to(own_length.astype(F32), (1, model)),
        ]
    )
    small = jnp.concatenate([shared, table_rows(d_table[:, :heads])])
    small = small + across(jnp.concatenate([shared, table_rows(d_table[:, heads:])]))
    small = Line(after(small, reached)).total()
    d_table = small[8:].reshape(-1)[: buckets * heads].reshape(buckets, heads)
    stats = jnp.sqrt(small[6, :1] / (small[7, :1] * model))
    return (
        placed(result),
        placed(grad_rows),
        d_table[None],
        small[:6].reshape(1, 3, 2, model),
        jnp.swapaxes(d_attn[:3], 1, 2)[None],
        d_attn[3][None],
        jnp.swapaxes(d_pair, 1, 2)[None],
        d_ffn_in[None],
        d_ffn_out[None],
        stats,
    )


def solution(mesh):
    in_specs = (
        P("section", None, "dp", "tensor", None),
        P(None, None, "dp"),
        P("section", None),
        P("section", None, "tensor"),
        P("section", None, None, None),
        P("section", None, None, "tensor"),
        P("section", "tensor", None),
        P("section", None, None, "tensor"),
        P("section", None, "tensor"),
        P("section", "tensor", None),
        P("section", None, "dp", "tensor", None),
    )
    out_specs = (
        P("section", None, "dp", "tensor", None),
        P("section", None, "dp", "tensor", None),
        P("section", None, "tensor"),
        P("section", None, None, None),
        P("section", None, None, "tensor"),
        P("section", "tensor", None),
        P("section", None, None, "tensor"),
        P("section", None, "tensor"),
        P("section", "tensor", None),
        P("section"),
    )
    return jax.shard_map(body, mesh=mesh, in_specs=in_specs, out_specs=out_specs, check_vma=False)
```

```python
import functools
import math

import jax
import jax.numpy as jnp
from jax import lax
from jax.experimental import pallas as pl
from jax.experimental.pallas import tpu as pltpu
from jax.sharding import PartitionSpec as P

HEAD_DIM = 64
SCALE = HEAD_DIM ** (-0.5)
EPSILON = 1e-05
MASKED = -1000000000.0
HIGHEST = lax.Precision.HIGHEST
BF = jnp.bfloat16
F32 = jnp.float32
NN = (((1,), (0,)), ((), ()))
NT = (((1,), (1,)), ((), ()))
TN = (((0,), (0,)), ((), ()))
TILE = 256
BAND = 128
ENCODER, DECODER = 0, 1
ROLE, OWN_LEN, SOURCE_LEN, CORE, START = 0, 1, 2, 3, 4
HIDES_LITTLE = 0.02
HIDES_MUCH = 2.0


def mm(left, right, dims):
    return lax.dot_general(left, right, dims, preferred_element_type=F32)


def whole():
    return pl.BlockSpec(memory_space=pltpu.VMEM)


def scalars():
    return pl.BlockSpec(memory_space=pltpu.SMEM)


def shape(dims, dtype):
    return jax.ShapeDtypeStruct(dims, dtype)


def cost(flops, nbytes, weight=HIDES_LITTLE):
    return pl.CostEstimate(
        flops=int(flops * weight), bytes_accessed=int(nbytes * weight), transcendentals=0
    )


def params(megabytes=28):
    return pltpu.CompilerParams(vmem_limit_bytes=megabytes * 1024 * 1024)


def norm_of(values, norm_ref):
    centred = values - jnp.mean(values, -1, keepdims=True)
    factor = lax.rsqrt(jnp.mean(centred * centred, -1, keepdims=True) + EPSILON)
    return centred * factor * norm_ref[0:1, :] + norm_ref[1:2, :]


def enter_kernel(info, mine, core_mine, far, core_far, norm_ref, rows_ref, normed_ref):
    quarter = mine.shape[0]
    for step, piece in enumerate((mine, core_mine, far, core_far)):
        start = pl.multiple_of(info[START + step], quarter)
        values = piece[...]
        rows_ref[pl.ds(start, quarter), :] = values
        normed_ref[pl.ds(start, quarter), :] = norm_of(values.astype(F32), norm_ref).astype(BF)


def enter(info, pieces, norm):
    quarter, width = pieces[0].shape
    out = shape((4 * quarter, width), BF)
    return pl.pallas_call(
        enter_kernel,
        out_shape=(out, out),
        in_specs=[scalars()] + [whole()] * 5,
        out_specs=(whole(), whole()),
        compiler_params=params(),
        cost_estimate=cost(16 * quarter * width * 4, quarter * width * 24),
    )(info, *pieces, norm)


def masked_kernel(info, mine, core_mine, far, core_far, rows_ref):
    quarter = mine.shape[0]
    for step, piece in enumerate((mine, core_mine, far, core_far)):
        start = pl.multiple_of(info[START + step], quarter)
        row = start + lax.broadcasted_iota(jnp.int32, (quarter, 1), 0)
        values = jnp.where(row < info[OWN_LEN], piece[...].astype(F32), 0.0)
        rows_ref[pl.ds(start, quarter), :] = values.astype(BF)


def masked_rows(info, pieces):
    quarter, width = pieces[0].shape
    return pl.pallas_call(
        masked_kernel,
        out_shape=shape((4 * quarter, width), BF),
        in_specs=[scalars()] + [whole()] * 4,
        out_specs=whole(),
        compiler_params=params(),
        cost_estimate=cost(quarter * width * 8, quarter * width * 16),
    )(info, *pieces)


def skew_kernel(distance_ref, table_ref):
    width = table_ref.shape[2]
    for head in range(distance_ref.shape[0]):
        row = jnp.broadcast_to(distance_ref[head : head + 1, :], (BAND, width))
        table_ref[head] = pltpu.roll(row, width - (BAND - 1), 1, stride=1, stride_axis=0)


def skew(distances):
    heads, width = distances.shape
    return pl.pallas_call(
        skew_kernel,
        out_shape=shape((heads, BAND, width), F32),
        in_specs=[whole()],
        out_specs=whole(),
        compiler_params=params(),
        cost_estimate=cost(heads * BAND * width, heads * BAND * width * 4),
    )(distances)


def unskewed(band):
    rows, width = band.shape
    while rows > 8:
        rows //= 2
        band = pltpu.roll(band[:rows], rows, 1) + band[rows:]
    amount = (rows - 1) - lax.broadcasted_iota(jnp.int32, (rows, width), 0)
    for bit in range(3):
        band = jnp.where(((amount >> bit) & 1) == 1, pltpu.roll(band, 1 << bit, 1), band)
    return jnp.sum(band, 0, keepdims=True)


def by_blocks(count, body):
    def step(index, carry):
        body(pl.ds(pl.multiple_of(index * TILE, TILE), TILE))
        return carry

    lax.fori_loop(0, count // TILE, step, 0)


def head_span(head):
    return slice(head * HEAD_DIM, (head + 1) * HEAD_DIM)


def allowed_keys(info, length, causal, length_at):
    key = lax.broadcasted_iota(jnp.int32, (length, length), 0)
    last = info[length_at] - 1
    if not causal:
        return key <= last
    query = lax.broadcasted_iota(jnp.int32, (1, length), 1)
    free = jnp.where(info[ROLE] == DECODER, 0, 1 << 20)
    return key <= jnp.minimum(query + free, last)


def scores_of(queries, keys, allowed, table_ref, head):
    scores = mm(keys, queries, TN)
    if table_ref is not None:
        length = scores.shape[0]
        starts = range(length - BAND, -BAND, -BAND)
        bands = [table_ref[head, :, start : start + length] for start in starts]
        scores = scores + jnp.concatenate(bands, 0)
    return jnp.where(allowed, scores, MASKED)


def attend(info, qkv_ref, table_ref, out_ref, lse_ref, length_at):
    width, length = out_ref.shape
    allowed = allowed_keys(info, length, table_ref is not None, length_at)
    for head in range(width // HEAD_DIM):
        span = head_span(head)
        queries = qkv_ref[0, span, :] * jnp.asarray(SCALE, BF)
        scores = scores_of(queries, qkv_ref[1, span, :], allowed, table_ref, head)
        peak = jnp.max(scores, 0, keepdims=True)
        lifted = jnp.exp(scores - peak)
        total = jnp.sum(lifted, 0, keepdims=True)
        mixed = mm(qkv_ref[2, span, :], lifted.astype(BF), NN)
        out_ref[span, :] = mixed / total
        lse_ref[head : head + 1, :] = peak + jnp.log(total)


def self_forward_kernel(has_sum, info, normed, weights, table, *refs):
    previous = refs[0] if has_sum else None
    sum_ref, qkv_ref, out_ref, lse_ref = refs[1 if has_sum else 0 :]
    length = out_ref.shape[1]

    def inputs(cols):
        block = normed[cols, :]
        for place in range(3):
            qkv_ref[place, :, cols] = mm(weights[place], block, NT).astype(BF)

    by_blocks(length, inputs)
    attend(info, qkv_ref, table, out_ref, lse_ref, OWN_LEN)

    def outputs(cols):
        value = mm(out_ref[:, cols].astype(BF), weights[3], TN)
        if has_sum:
            value = value + previous[cols, :]
        sum_ref[cols, :] = value.astype(sum_ref.dtype)

    by_blocks(length, outputs)


def attention_cost(length, width, model, matmuls, projections, weight=HIDES_LITTLE):
    heads = width // HEAD_DIM
    return cost(
        heads * length * length * HEAD_DIM * 2 * matmuls * 4 + projections * 2 * length * model * width,
        length * model * 8,
        weight,
    )


def saved_shapes(length, width):
    return (shape((3, width, length), BF), shape((width, length), F32), shape((8, length), F32))


def self_forward(info, normed, weights, table, previous):
    length, model = normed.shape
    width = weights.shape[1]
    has_sum = previous is not None
    operands = [info, normed, weights, table] + ([previous] if has_sum else [])
    return pl.pallas_call(
        functools.partial(self_forward_kernel, has_sum),
        out_shape=(shape((length, model), BF if has_sum else F32),) + saved_shapes(length, width),
        in_specs=[scalars()] + [whole()] * (len(operands) - 1),
        out_specs=(whole(),) * 4,
        compiler_params=params(),
        cost_estimate=attention_cost(length, width, model, 2, 4, HIDES_MUCH),
    )(*operands)


def rows_of(ref, place, width):
    return ref[place * width : (place + 1) * width, :]


def cross_forward_kernel(info, normed, near, far, weights_near, weights_far, *refs):
    sum_ref = refs[0]
    length, width = normed.shape[0], weights_near.shape[0] // 4
    half = near.shape[0]
    sides = ((weights_near, refs[1:4]), (weights_far, refs[4:7]))

    @pl.when(info[ROLE] == DECODER)
    def _():
        for weights, (qkv_ref, out_ref, lse_ref) in sides:

            def queries(cols, weights=weights, qkv_ref=qkv_ref):
                qkv_ref[0, :, cols] = mm(rows_of(weights, 0, width), normed[cols, :], NT).astype(BF)

            by_blocks(length, queries)
            for piece, side in ((near, info[CORE]), (far, 1 - info[CORE])):
                base = side * half

                def sources(index, carry, piece=piece, base=base, weights=weights, qkv_ref=qkv_ref):
                    local = pl.multiple_of(index * TILE, TILE)
                    block = piece[pl.ds(local, TILE), :]
                    cols = pl.ds(pl.multiple_of(base + local, TILE), TILE)
                    for place in (1, 2):
                        qkv_ref[place, :, cols] = mm(rows_of(weights, 1 + place, width), block, NT).astype(BF)
                    return carry

                lax.fori_loop(0, half // TILE, sources, 0)
            attend(info, qkv_ref, None, out_ref, lse_ref, SOURCE_LEN)

        def outputs(cols):
            value = mm(refs[2][:, cols].astype(BF), rows_of(weights_near, 1, width), TN)
            value = value + mm(refs[5][:, cols].astype(BF), rows_of(weights_far, 1, width), TN)
            sum_ref[cols, :] = value.astype(sum_ref.dtype)

        by_blocks(length, outputs)


def cross_forward(info, normed, near, far, weights_near, weights_far):
    length, model = normed.shape
    width = weights_near.shape[0] // 4
    saved = saved_shapes(length, width)
    results = pl.pallas_call(
        cross_forward_kernel,
        out_shape=(shape((length, model), BF),) + saved + saved,
        in_specs=[scalars()] + [whole()] * 5,
        out_specs=(whole(),) * 7,
        compiler_params=params(),
        cost_estimate=attention_cost(length, 2 * width, model, 2, 4),
    )(info, normed, near, far, weights_near, weights_far)
    return results[0], results[1:4], results[4:7]


def attend_back(info, saved, table_ref, upstream, grads_ref, band, length_at):
    qkv_ref, out_ref, lse_ref = saved
    width, length = out_ref.shape
    allowed = allowed_keys(info, length, table_ref is not None, length_at)
    if table_ref is not None:
        band[...] = jnp.zeros_like(band)
    for head in range(width // HEAD_DIM):
        span = head_span(head)
        queries = qkv_ref[0, span, :] * jnp.asarray(SCALE, BF)
        keys, above = qkv_ref[1, span, :], upstream[span, :]
        scores = scores_of(queries, keys, allowed, table_ref, head)
        probs = jnp.exp(scores - lse_ref[head : head + 1, :])
        inner = jnp.sum(above.astype(F32) * out_ref[span, :], 0, keepdims=True)
        d_scores = probs * (mm(qkv_ref[2, span, :], above, TN) - inner)
        low = d_scores.astype(BF)
        grads_ref[0, span, :] = (mm(keys, low, NN) * SCALE).astype(BF)
        grads_ref[1, span, :] = mm(queries, low, NT).astype(BF)
        grads_ref[2, span, :] = mm(above, probs.astype(BF), NT).astype(BF)
        if table_ref is not None:
            for part in range(length // BAND):
                start = length - BAND - part * BAND
                rows = slice(part * BAND, (part + 1) * BAND)
                band[head, :, start : start + length] += d_scores[rows, :]


def self_backward_kernel(has_sum, info, qkv, out, lse, above, normed, weights, table, *refs):
    previous = refs[0] if has_sum else None
    refs = refs[1 if has_sum else 0 :]
    sum_ref, weight_ref, spread_ref, upstream = refs[:4]
    band, grads_ref = refs[4:6]
    length = above.shape[0]

    def entering(cols):
        upstream[:, cols] = mm(weights[3], above[cols, :], NT).astype(BF)

    by_blocks(length, entering)
    attend_back(info, (qkv, out, lse), table, upstream, grads_ref, band, OWN_LEN)

    def leaving(cols):
        value = mm(grads_ref[0, :, cols], weights[0], TN)
        for place in (1, 2):
            value = value + mm(grads_ref[place, :, cols], weights[place], TN)
        if has_sum:
            value = value + previous[cols, :]
        sum_ref[cols, :] = value.astype(sum_ref.dtype)

    by_blocks(length, leaving)
    for place in range(3):
        weight_ref[place] = mm(grads_ref[place], normed[...], NN).astype(weight_ref.dtype)
    weight_ref[3] = mm(out[...].astype(BF), above[...], NN).astype(weight_ref.dtype)
    for head in range(table.shape[0]):
        spread_ref[head : head + 1, :] = unskewed(band[head])


def self_backward(info, saved, above, normed, weights, table, previous, weight_type, hides):
    length, model = above.shape
    width = weights.shape[1]
    has_sum = previous is not None
    operands = [info, *saved, above, normed, weights, table] + ([previous] if has_sum else [])
    return pl.pallas_call(
        functools.partial(self_backward_kernel, has_sum),
        out_shape=(
            shape((length, model), BF if has_sum else F32),
            shape((4, width, model), weight_type),
            shape((table.shape[0], table.shape[2]), F32),
        ),
        in_specs=[scalars()] + [whole()] * (len(operands) - 1),
        out_specs=(whole(),) * 3,
        scratch_shapes=[
            pltpu.VMEM((width, length), BF),
            pltpu.VMEM(table.shape, F32),
            pltpu.VMEM((3, width, length), BF),
        ],
        compiler_params=params(),
        cost_estimate=attention_cost(length, width, model, 5, 8, hides),
    )(*operands)


def cross_backward_kernel(info, *refs):
    saved_near, saved_far, (above, weights_near, weights_far) = refs[:3], refs[3:6], refs[6:9]
    sum_ref, source_ref, grads_near, grads_far, upstream = refs[9:14]
    length, width = above.shape[0], weights_near.shape[0] // 4

    @pl.when(info[ROLE] == DECODER)
    def _():
        for saved, weights, grads_ref in (
            (saved_near, weights_near, grads_near),
            (saved_far, weights_far, grads_far),
        ):

            def entering(cols, weights=weights):
                upstream[:, cols] = mm(rows_of(weights, 1, width), above[cols, :], NT).astype(BF)

            by_blocks(length, entering)
            attend_back(info, saved, None, upstream, grads_ref, None, SOURCE_LEN)

        def leaving(cols):
            value = mm(grads_near[0, :, cols], rows_of(weights_near, 0, width), TN)
            value = value + mm(grads_far[0, :, cols], rows_of(weights_far, 0, width), TN)
            sum_ref[cols, :] = value.astype(BF)
            source = None
            for grads_ref, weights in ((grads_near, weights_near), (grads_far, weights_far)):
                for place in (1, 2):
                    term = mm(grads_ref[place, :, cols], rows_of(weights, 1 + place, width), TN)
                    source = term if source is None else source + term
            source_ref[cols, :] = source.astype(BF)

        by_blocks(length, leaving)


def cross_backward(info, saved_near, saved_far, above, weights_near, weights_far):
    length, model = above.shape
    width = weights_near.shape[0] // 4
    out, grads = shape((length, model), BF), shape((3, width, length), BF)
    return pl.pallas_call(
        cross_backward_kernel,
        out_shape=(out, out, grads, grads),
        in_specs=[scalars()] + [whole()] * 9,
        out_specs=(whole(),) * 4,
        scratch_shapes=[pltpu.VMEM((width, length), BF)],
        compiler_params=params(),
        cost_estimate=attention_cost(length, 2 * width, model, 5, 4),
    )(info, *saved_near, *saved_far, above, weights_near, weights_far)


def cross_weights_kernel(info, grads_near, grads_far, out_near, out_far, normed, above, *refs):
    near, far, weight_near, weight_far = refs
    half = near.shape[0]

    @pl.when(info[ROLE] == DECODER)
    def _():
        start = pl.multiple_of(info[CORE] * half, half)
        other = pl.multiple_of((1 - info[CORE]) * half, half)
        for grads, out, target in (
            (grads_near, out_near, weight_near),
            (grads_far, out_far, weight_far),
        ):
            target[0] = mm(grads[0], normed[...], NN).astype(target.dtype)
            target[1] = mm(out[...].astype(BF), above[...], NN).astype(target.dtype)
            for place in (1, 2):
                value = mm(grads[place, :, pl.ds(start, half)], near[...], NN)
                value = value + mm(grads[place, :, pl.ds(other, half)], far[...], NN)
                target[1 + place] = value.astype(target.dtype)


def cross_weights(info, grads_near, grads_far, out_near, out_far, normed, above, near, far):
    length, model = above.shape
    width = out_near.shape[0]
    return pl.pallas_call(
        cross_weights_kernel,
        out_shape=(shape((4, width, model), F32), shape((4, width, model), BF)),
        in_specs=[scalars()] + [whole()] * 8,
        out_specs=(whole(),) * 2,
        compiler_params=params(),
        cost_estimate=cost(16 * length * model * width, length * model * 16),
    )(info, grads_near, grads_far, out_near, out_far, normed, above, near, far)


def row_spec(width):
    return pl.BlockSpec((TILE, width), lambda index: (index, 0))


def pack_spec(place, width):
    return pl.BlockSpec((width, width), lambda index: (place, 0))


def fixed_spec(dims):
    return pl.BlockSpec(dims, lambda index: (0,) * len(dims))


def add_norm_kernel(stream, near, far, norm_ref, sum_ref, normed_ref):
    value = stream[...].astype(F32) + (near[...].astype(F32) + far[...].astype(F32))
    sum_ref[...] = value
    normed_ref[...] = norm_of(value, norm_ref).astype(BF)


def add_norm(stream, near, far, norm):
    length, model = stream.shape
    return pl.pallas_call(
        add_norm_kernel,
        grid=(length // TILE,),
        out_shape=(shape((length, model), F32), shape((length, model), BF)),
        in_specs=[row_spec(model)] * 3 + [fixed_spec((2, model))],
        out_specs=(row_spec(model),) * 2,
        compiler_params=params(),
        cost_estimate=cost(length * model * 12, length * model * 14),
    )(stream, near, far, norm)


def row_mask(info, index, at):
    row = index * TILE + lax.broadcasted_iota(jnp.int32, (TILE, 1), 0)
    return row < info[at]


def squares_of(value):
    return jnp.sum(jnp.sum(value * value, 0, keepdims=True), 1, keepdims=True)


def source_kernel(info, stream, near, far, norm_ref, sum_ref, sent_ref, square_ref):
    index = pl.program_id(0)
    value = stream[...] + (near[...].astype(F32) + far[...].astype(F32))
    sum_ref[...] = value
    result = jnp.where(row_mask(info, index, OWN_LEN), norm_of(value, norm_ref), 0.0)
    sent_ref[...] = result.astype(BF)

    @pl.when(index == 0)
    def _():
        square_ref[...] = jnp.zeros_like(square_ref)

    square_ref[...] += squares_of(result)


def source_out(info, stream, near, far, norm):
    length, model = stream.shape
    return pl.pallas_call(
        source_kernel,
        grid=(length // TILE,),
        out_shape=(shape((length, model), F32), shape((length, model), BF), shape((8, 128), F32)),
        in_specs=[scalars()] + [row_spec(model)] * 3 + [fixed_spec((2, model))],
        out_specs=(row_spec(model), row_spec(model), fixed_spec((8, 128))),
        compiler_params=params(),
        cost_estimate=cost(length * model * 14, length * model * 14),
    )(info, stream, near, far, norm)


def finish_kernel(info, stream, near, far, sent, square, out_ref, square_ref):
    index = pl.program_id(0)

    @pl.when(info[ROLE] == DECODER)
    def _():
        value = stream[...] + (near[...].astype(F32) + far[...].astype(F32))
        value = jnp.where(row_mask(info, index, OWN_LEN), value, 0.0)
        out_ref[...] = value.astype(BF)

        @pl.when(index == 0)
        def _():
            square_ref[...] = jnp.zeros_like(square_ref)

        square_ref[...] += squares_of(value)

    @pl.when(info[ROLE] == ENCODER)
    def _():
        out_ref[...] = sent[...]
        square_ref[...] = square[...]


def finish(info, stream, near, far, sent, square):
    length, model = stream.shape
    return pl.pallas_call(
        finish_kernel,
        grid=(length // TILE,),
        out_shape=(shape((length, model), BF), shape((8, 128), F32)),
        in_specs=[scalars()] + [row_spec(model)] * 4 + [fixed_spec((8, 128))],
        out_specs=(row_spec(model), fixed_spec((8, 128))),
        compiler_params=params(),
        cost_estimate=cost(length * model * 6, length * model * 12),
    )(info, stream, near, far, sent, square)


def norm_back(upstream, values, norm_ref):
    centred = values - jnp.mean(values, -1, keepdims=True)
    factor = lax.rsqrt(jnp.mean(centred * centred, -1, keepdims=True) + EPSILON)
    unit = centred * factor
    scaled = upstream * norm_ref[0:1, :]
    inner = scaled - jnp.mean(scaled, -1, keepdims=True)
    inner = inner - unit * jnp.mean(scaled * unit, -1, keepdims=True)
    gain = jnp.sum(upstream * unit, 0, keepdims=True)
    shift = jnp.sum(upstream, 0, keepdims=True)
    return factor * inner, gain, shift


def norm_back_kernel(residual, near, far, values, norm_ref, grad_ref, low_ref, norm_grad_ref):
    upstream = near[...].astype(F32) + far[...].astype(F32)
    grad, gain, shift = norm_back(upstream, values[...].astype(F32), norm_ref)
    grad = residual[...].astype(F32) + grad
    grad_ref[...] = grad
    low_ref[...] = grad.astype(BF)

    @pl.when(pl.program_id(0) == 0)
    def _():
        norm_grad_ref[...] = jnp.zeros_like(norm_grad_ref)

    norm_grad_ref[0:1, :] += gain
    norm_grad_ref[1:2, :] += shift


def norm_backward(residual, near, far, values, norm):
    length, model = values.shape
    return pl.pallas_call(
        norm_back_kernel,
        grid=(length // TILE,),
        out_shape=(shape((length, model), F32), shape((length, model), BF), shape((2, model), F32)),
        in_specs=[row_spec(model)] * 4 + [fixed_spec((2, model))],
        out_specs=(row_spec(model), row_spec(model), fixed_spec((2, model))),
        compiler_params=params(),
        cost_estimate=cost(length * model * 20, length * model * 18),
    )(residual, near, far, values, norm)


def gelu_parts(hidden):
    half = 0.5 * (1.0 + lax.erf(hidden * math.sqrt(0.5)))
    slope = half + hidden * jnp.exp(-0.5 * hidden * hidden) * (1.0 / math.sqrt(2.0 * math.pi))
    return hidden * half, slope


def feed_forward_kernel(has_sum, info, normed, pack, *refs):
    previous = refs[0] if has_sum else None
    sum_ref, active_ref, slope_ref = refs[1 if has_sum else 0 :]

    @pl.when(info[ROLE] == ENCODER)
    def _():
        active, slope = gelu_parts(mm(normed[...], pack[0], NN))
        active = active.astype(BF)
        active_ref[...] = active
        slope_ref[...] = slope.astype(BF)
        value = mm(active, pack[1], NN)
        if has_sum:
            value = value + previous[...]
        sum_ref[...] = value.astype(sum_ref.dtype)


def feed_forward(info, normed, pack, previous):
    length, model = normed.shape
    hidden = pack.shape[2]
    has_sum = previous is not None
    operands = [info, normed, pack] + ([previous] if has_sum else [])
    return pl.pallas_call(
        functools.partial(feed_forward_kernel, has_sum),
        grid=(length // TILE,),
        out_shape=(
            shape((length, model), BF if has_sum else F32),
            shape((length, hidden), BF),
            shape((length, hidden), BF),
        ),
        in_specs=[scalars(), row_spec(model), fixed_spec(pack.shape)]
        + ([row_spec(model)] if has_sum else []),
        out_specs=(row_spec(model), row_spec(hidden), row_spec(hidden)),
        compiler_params=params(),
        cost_estimate=cost(4 * length * model * hidden, length * model * 12),
    )(*operands)


def feed_above_kernel(info, cot, down_near, down_far, near_ref, far_ref):
    @pl.when(info[ROLE] == DECODER)
    def _():
        near_ref[...] = mm(cot[...], down_near[...], NT)
        far_ref[...] = mm(cot[...], down_far[...], NT)


def feed_above(info, cot, down_near, down_far):
    length, model = cot.shape
    hidden = down_near.shape[0]
    unit = shape((length, hidden), F32)
    return pl.pallas_call(
        feed_above_kernel,
        grid=(length // TILE,),
        out_shape=(unit, unit),
        in_specs=[
            scalars(),
            row_spec(model),
            fixed_spec(down_near.shape),
            pack_spec(1, model),
        ],
        out_specs=(row_spec(hidden),) * 2,
        compiler_params=params(),
        cost_estimate=cost(4 * length * model * hidden, length * model * 10),
    )(info, cot, down_near, down_far)


def feed_both_kernel(info, normed, above_near, above_far, up_near, up_far, back_ref, *refs):
    @pl.when(info[ROLE] == DECODER)
    def _():
        back = None
        for up, above, active_ref, grad_ref in (
            (up_near, above_near, *refs[0:2]),
            (up_far, above_far, *refs[2:4]),
        ):
            active, slope = gelu_parts(mm(normed[...], up[...], NN))
            active_ref[...] = active.astype(BF)
            grad = (above[...] * slope).astype(BF)
            grad_ref[...] = grad
            term = mm(grad, up[...], NT)
            back = term if back is None else back + term
        back_ref[...] = back.astype(BF)


def feed_both(info, normed, above, up_near, up_far):
    length, model = normed.shape
    hidden = up_near.shape[1]
    out, unit = shape((length, model), BF), shape((length, hidden), BF)
    return pl.pallas_call(
        feed_both_kernel,
        grid=(length // TILE,),
        out_shape=(out, unit, unit, unit, unit),
        in_specs=[
            scalars(),
            row_spec(model),
            row_spec(hidden),
            row_spec(hidden),
            fixed_spec(up_near.shape),
            fixed_spec(up_far.shape),
        ],
        out_specs=(row_spec(model),) + (row_spec(hidden),) * 4,
        compiler_params=params(),
        cost_estimate=cost(8 * length * model * hidden, length * model * 20),
    )(info, normed, *above, up_near, up_far)


def feed_value_kernel(info, active_near, active_far, down_near, down_far, sum_ref):
    @pl.when(info[ROLE] == DECODER)
    def _():
        value = mm(active_near[...], down_near[...], NN) + mm(active_far[...], down_far[...], NN)
        sum_ref[...] = value.astype(BF)


def feed_value(info, active_near, active_far, down_near, down_far):
    length, hidden = active_near.shape
    model = down_near.shape[1]
    return pl.pallas_call(
        feed_value_kernel,
        grid=(length // TILE,),
        out_shape=shape((length, model), BF),
        in_specs=[
            scalars(),
            row_spec(hidden),
            row_spec(hidden),
            fixed_spec(down_near.shape),
            pack_spec(1, model),
        ],
        out_specs=row_spec(model),
        compiler_params=params(),
        cost_estimate=cost(4 * length * model * hidden, length * model * 6),
    )(info, active_near, active_far, down_near, down_far)


def source_back_kernel(info, cot, near, far, values, norm_ref, *refs):
    slope_near, slope_far, pack_near, pack_far, grad_ref, low_ref, norm_grad_ref = refs[:7]
    back_ref, hidden_near, hidden_far = refs[7:]
    index = pl.program_id(0)
    blocks = near.shape[0] // TILE
    rows = pl.ds(pl.multiple_of(lax.rem(index, blocks) * TILE, TILE), TILE)
    mine = (index >= blocks).astype(jnp.int32) == info[CORE]
    returned = jnp.where(mine, near[rows, :].astype(F32), far[rows, :].astype(F32))
    upstream = cot[...].astype(F32) + returned
    upstream = jnp.where(row_mask(info, index, OWN_LEN), upstream, 0.0)
    grad, gain, shift = norm_back(upstream, values[...], norm_ref)
    low = grad.astype(BF)
    grad_ref[...] = grad
    low_ref[...] = low

    @pl.when(index == 0)
    def _():
        norm_grad_ref[...] = jnp.zeros_like(norm_grad_ref)

    norm_grad_ref[0:1, :] += gain
    norm_grad_ref[1:2, :] += shift
    back = None
    for pack, slope, hidden_ref in (
        (pack_near, slope_near, hidden_near),
        (pack_far, slope_far, hidden_far),
    ):
        hidden = (mm(low, pack[1], NT) * slope[...].astype(F32)).astype(BF)
        hidden_ref[...] = hidden
        term = mm(hidden, pack[0], NT)
        back = term if back is None else back + term
    back_ref[...] = back.astype(BF)


def source_back(info, cot, near, far, values, norm, slope_near, slope_far, pack_near, pack_far):
    length, model = values.shape
    hidden = pack_near.shape[2]
    unit = shape((length, hidden), BF)
    return pl.pallas_call(
        source_back_kernel,
        grid=(length // TILE,),
        out_shape=(
            shape((length, model), F32),
            shape((length, model), BF),
            shape((2, model), F32),
            shape((length, model), BF),
            unit,
            unit,
        ),
        in_specs=[
            scalars(),
            row_spec(model),
            fixed_spec(near.shape),
            fixed_spec(far.shape),
            row_spec(model),
            fixed_spec((2, model)),
            row_spec(hidden),
            row_spec(hidden),
            fixed_spec(pack_near.shape),
            fixed_spec(pack_far.shape),
        ],
        out_specs=(
            row_spec(model),
            row_spec(model),
            fixed_spec((2, model)),
            row_spec(model),
            row_spec(hidden),
            row_spec(hidden),
        ),
        compiler_params=params(),
        cost_estimate=cost(8 * length * model * hidden, length * model * 30),
    )(info, cot, near, far, values, norm, slope_near, slope_far, pack_near, pack_far)


def product_kernel(left_near, left_far, right_near, right_far, near_ref, far_ref):
    near_ref[...] = mm(left_near[...], right_near[...], TN)
    far_ref[...] = mm(left_far[...], right_far[...], TN).astype(BF)


def feed_weights(left_near, left_far, right_near, right_far):
    length, rows = left_near.shape
    columns = right_near.shape[1]
    left = pl.BlockSpec((length, TILE), lambda index: (0, index))
    right = pl.BlockSpec((length, columns), lambda index: (0, 0))
    out = row_spec(columns)
    return pl.pallas_call(
        product_kernel,
        grid=(rows // TILE,),
        out_shape=(shape((rows, columns), F32), shape((rows, columns), BF)),
        in_specs=[left, left, right, right],
        out_specs=(out, out),
        compiler_params=params(),
        cost_estimate=cost(4 * length * rows * columns, length * rows * 12),
    )(left_near, left_far, right_near, right_far)


def across(value):
    return lax.ppermute(value, "tensor", [(0, 2), (1, 3), (2, 0), (3, 1)])


def across_in(value, role):
    links = [(0, 2), (1, 3), (2, 0), (3, 1)]
    return lax.ppermute(
        value, ("section", "tensor"), [(role * 4 + a, role * 4 + b) for a, b in links]
    )


def beside(value):
    return lax.ppermute(value, "tensor", [(0, 1), (1, 0), (2, 3), (3, 2)])


def to_decoder(value):
    return lax.ppermute(value, "section", [(ENCODER, DECODER)])


def to_encoder(value):
    return lax.ppermute(value, "section", [(DECODER, ENCODER)])


class Line:
    def __init__(self, value):
        self.four = lax.axis_size("dp") == 4
        self.value = value
        self.done = 0

    def inward(self, behind=None):
        if self.four:
            arrived = lax.ppermute(self.value, "dp", [(0, 1), (3, 2)])
            self.value = self.value + (arrived if behind is None else after(arrived, behind))
        self.done = 1

    def swap(self):
        if self.four:
            self.value = self.value + lax.ppermute(self.value, "dp", [(1, 2), (2, 1)])
        self.done = 2

    def total(self):
        if not self.four:
            return lax.psum(self.value, "dp").astype(F32)
        if self.done < 1:
            self.inward()
        if self.done < 2:
            self.swap()
        place = lax.axis_index("dp")
        inner = (place == 1) | (place == 2)
        outward = lax.ppermute(self.value, "dp", [(1, 0), (2, 3)])
        return jnp.where(inner, self.value, outward).astype(F32)


def near_added(own, other):
    return (own + other.astype(F32)).astype(BF)


def after(value, done):
    return lax.optimization_barrier((value, done))[0]


def body(
    frames,
    lengths,
    bucket_of,
    rel_table,
    norms,
    attn_in,
    attn_out,
    cross_pair,
    ffn_in,
    ffn_out,
    cotangent,
):
    section = lax.axis_index("section")
    tensor = lax.axis_index("tensor")
    pair, core = tensor // 2, tensor % 2
    decoder = section == DECODER
    quarter, model = frames.shape[3], frames.shape[4]
    length = 4 * quarter
    half = length // 2
    width = attn_in.shape[3]
    heads = width // HEAD_DIM
    buckets = rel_table.shape[1]

    own_length = lengths[section, pair, 0]
    source_length = lengths[ENCODER, pair, 0]
    starts = [(tensor ^ step) * quarter for step in range(4)]
    info = jnp.stack([section, own_length, source_length, core] + starts).astype(jnp.int32)

    def pick(array, index):
        return lax.dynamic_index_in_dim(array[0, :, 0], index, 0, keepdims=False)

    self_near = jnp.concatenate([jnp.swapaxes(attn_in[0], 1, 2), attn_out[0][None]])
    feed_near = jnp.stack([ffn_in[0], ffn_out[0]])
    pair_own = jnp.swapaxes(cross_pair[0], 1, 2)
    frame_mine = pick(frames, pair)
    frame_far = across(pick(frames, 1 - pair))
    rel_far = across(rel_table[0])
    self_far = across(after(self_near, rel_far))
    pair_source = to_decoder(pair_own)
    feed_far_e = across_in(after(feed_near, frame_far), ENCODER)
    cross_near = jnp.concatenate([pair_own, pair_source]).reshape(4 * width, model)
    pack_near = jnp.concatenate([cross_near, ffn_out[0]])
    pack_far = across_in(after(pack_near, frame_far), DECODER)
    up_far_d = across_in(after(ffn_in[0], pack_far), DECODER)
    cot_mine, cot_other = pick(cotangent, pair), pick(cotangent, 1 - pair)

    def quarters(mine, far):
        both = beside(jnp.stack([mine, far]))
        return mine, both[0], far, both[1]

    buckets_here = jnp.pad(bucket_of[0][::-1], (0, 1), constant_values=-1)
    one_hot = (lax.broadcasted_iota(jnp.int32, (buckets, 2 * length), 0) == buckets_here[None]).astype(F32)
    distances = lax.dot_general(
        jnp.concatenate([rel_table[0], rel_far], 1),
        one_hot,
        TN,
        precision=HIGHEST,
        preferred_element_type=F32,
    )
    table_near = skew(distances[:heads])
    table_far = skew(distances[heads:])

    rows, normed_one = enter(info, quarters(frame_mine, frame_far), norms[0, 0])
    part, *saved_near = self_forward(info, normed_one, self_near, table_near, None)
    part, *saved_far = self_forward(
        info, normed_one, after(self_far, pack_near), table_far, part
    )
    stream_one, normed_two = add_norm(
        rows, part, beside(part), norms[0, 1]
    )

    part, active_e_near, slope_near = feed_forward(
        info, normed_two, feed_near, None
    )
    part, active_e_far, slope_far = feed_forward(
        info, normed_two, after(feed_far_e, pack_far), part
    )
    stream_e, sent, squares = source_out(
        info, stream_one, part, beside(part), norms[0, 2]
    )
    sent_near = to_decoder(lax.dynamic_slice_in_dim(sent, core * half, half, 0))
    sent_far = beside(sent_near)
    cot = masked_rows(info, quarters(cot_mine, across(after(cot_other, sent))))
    hidden_pre = feed_above(info, cot, ffn_out[0], pack_far)
    normed_cross = after(normed_two, (hidden_pre, up_far_d))

    part, joint_near, joint_far = cross_forward(
        info, normed_cross, sent_near, sent_far, cross_near, pack_far
    )
    stream_d, normed_three = add_norm(stream_one, part, beside(part), norms[0, 2])
    back, active_d_near, hidden_d_near, active_d_far, hidden_d_far = feed_both(
        info, normed_three, hidden_pre, ffn_in[0], up_far_d
    )
    grad_d, above_d, norm_d = norm_backward(cot, back, beside(back), stream_d, norms[0, 2])
    back_d, returned, d_joint_near, d_joint_far = cross_backward(
        info, joint_near, joint_far, above_d, cross_near, pack_far
    )
    returned_mine = lax.dynamic_slice_in_dim(returned, core * half, half, 0)
    returned_theirs = lax.dynamic_slice_in_dim(returned, (1 - core) * half, half, 0)
    returned = returned_mine.astype(F32) + beside(returned_theirs).astype(F32)
    returned = returned.astype(BF)
    returned_near = to_encoder(returned)
    returned_far = beside(returned_near)

    grad_two, above_feed, norm_grad_three, back, hidden_near, hidden_far = lax.cond(
        decoder,
        lambda: (grad_d, cot, norm_d, back_d, hidden_d_near, hidden_d_far),
        lambda: source_back(
            info,
            cot,
            returned_near,
            returned_far,
            stream_e,
            norms[0, 2],
            slope_near,
            slope_far,
            feed_near,
            feed_far_e,
        ),
    )
    down_near, down_far = lax.cond(
        decoder,
        lambda: feed_weights(active_d_near, active_d_far, above_feed, above_feed),
        lambda: feed_weights(active_e_near, active_e_far, above_feed, above_feed),
    )
    down_other = across(down_far)
    grad_one, above_one, norm_grad_two = norm_backward(
        grad_two, back, beside(back), stream_one, norms[0, 1]
    )
    up_near, up_far = lax.cond(
        decoder,
        lambda: feed_weights(normed_three, normed_three, hidden_near, hidden_far),
        lambda: feed_weights(normed_two, normed_two, hidden_near, hidden_far),
    )
    up_other = across(up_far)

    back, attn_far, spread_far = self_backward(
        info,
        saved_far,
        after(above_one, up_far),
        normed_one,
        self_far,
        table_far,
        None,
        BF,
        HIDES_MUCH,
    )
    pair_near, pair_far = cross_weights(
        info,
        d_joint_near,
        d_joint_far,
        joint_near[1],
        joint_far[1],
        normed_two,
        after(above_d, attn_far),
        sent_near,
        sent_far,
    )
    attn_other = across(attn_far)
    d_down = Line(near_added(down_near, after(down_other, attn_far)))
    above_near = after(above_one, d_down.value)
    back, attn_near, spread_near = self_backward(
        info, saved_near, above_near, normed_one, self_near, table_near, back, F32, HIDES_LITTLE
    )

    d_down.inward(attn_near)
    d_up = Line(near_added(up_near, after(up_other, attn_near)))
    d_up.inward()
    d_down.swap()
    d_attn = Line(near_added(attn_near, after(attn_other, d_down.value)))
    d_attn.inward()
    d_up.value = after(d_up.value, d_down.value)
    d_up.swap()
    grad_rows, _, norm_grad_one = norm_backward(grad_one, back, beside(back), rows, norms[0, 0])
    d_ffn_out = d_down.total()
    d_attn.value = after(d_attn.value, d_ffn_out)
    d_attn.swap()
    d_pair = (pair_near + across_in(pair_far, DECODER).astype(F32)).astype(BF)
    d_source = to_encoder(d_pair[2:])
    d_ffn_in = d_up.total()
    reached = d_attn.value
    d_pair = Line(after(jnp.where(decoder, d_pair[:2], d_source), reached))
    d_attn = d_attn.total()
    d_pair = d_pair.total()

    part_d = feed_value(
        info, after(active_d_near, hidden_near), active_d_far, ffn_out[0], pack_far
    )
    result, squares = finish(info, stream_d, part_d, beside(part_d), sent, squares)

    def placed(value):
        mine = lax.dynamic_slice_in_dim(value, tensor * quarter, quarter, 0)
        theirs = lax.dynamic_slice_in_dim(value, (tensor ^ 2) * quarter, quarter, 0)
        other = across(theirs.astype(BF)).astype(value.dtype)
        stacked = jnp.where(pair == 0, jnp.stack([mine, other]), jnp.stack([other, mine]))
        return stacked[None, :, None]

    spreads = jnp.concatenate([spread_near, spread_far])
    d_table = lax.dot_general(
        one_hot, spreads, NT, precision=HIGHEST, preferred_element_type=F32
    )
    def table_rows(value):
        rows_used = -(-buckets * heads // model)
        padded = jnp.pad(value.reshape(-1), (0, rows_used * model - buckets * heads))
        return padded.reshape(rows_used, model)

    shared = jnp.concatenate(
        [
            norm_grad_one,
            norm_grad_two,
            norm_grad_three,
            jnp.broadcast_to(squares[:1, :1], (1, model)),
            jnp.broadcast_to(own_length.astype(F32), (1, model)),
        ]
    )
    small = jnp.concatenate([shared, table_rows(d_table[:, :heads])])
    small = small + across(jnp.concatenate([shared, table_rows(d_table[:, heads:])]))
    small = Line(after(small, reached)).total()
    d_table = small[8:].reshape(-1)[: buckets * heads].reshape(buckets, heads)
    stats = jnp.sqrt(small[6, :1] / (small[7, :1] * model))
    return (
        placed(result),
        placed(grad_rows),
        d_table[None],
        small[:6].reshape(1, 3, 2, model),
        jnp.swapaxes(d_attn[:3], 1, 2)[None],
        d_attn[3][None],
        jnp.swapaxes(d_pair, 1, 2)[None],
        d_ffn_in[None],
        d_ffn_out[None],
        stats,
    )


def solution(mesh):
    in_specs = (
        P("section", None, "dp", "tensor", None),
        P(None, None, "dp"),
        P("section", None),
        P("section", None, "tensor"),
        P("section", None, None, None),
        P("section", None, None, "tensor"),
        P("section", "tensor", None),
        P("section", None, None, "tensor"),
        P("section", None, "tensor"),
        P("section", "tensor", None),
        P("section", None, "dp", "tensor", None),
    )
    out_specs = (
        P("section", None, "dp", "tensor", None),
        P("section", None, "dp", "tensor", None),
        P("section", None, "tensor"),
        P("section", None, None, None),
        P("section", None, None, "tensor"),
        P("section", "tensor", None),
        P("section", None, None, "tensor"),
        P("section", None, "tensor"),
        P("section", "tensor", None),
        P("section"),
    )
    return jax.shard_map(body, mesh=mesh, in_specs=in_specs, out_specs=out_specs, check_vma=False)
```
